32 devices in a mesh: dp: 8 (over z, y), tensor: 4 (over x, core).
Axes of the slice: x: 2, y: 2, z: 4, core: 2. Of those that a mesh axis runs over, the one named last changes fastest.
Arguments:
- tokens: bfloat16 [32768, 1024], P(('dp', 'tensor')), may hold values from -6 to 6
- lengths: int32 [16], P('dp'), may hold values from 1 to 2048, as said below
- gain_first: float32 [1024], replicated, may hold values from 0.25 to 1.75
- shift_first: float32 [1024], replicated, may hold values from -3 to 3
- query_weight: bfloat16 [1024, 1024], P(None, 'tensor'), may hold values from -0.1875 to 0.1875
- key_weight: bfloat16 [1024, 1024], P(None, 'tensor'), may hold values from -0.1875 to 0.1875
- value_weight: bfloat16 [1024, 1024], P(None, 'tensor'), may hold values from -0.1875 to 0.1875
- output_weight: bfloat16 [1024, 1024], P('tensor'), may hold values from -3 to 3
- gain_second: float32 [1024], replicated, may hold values from 0.25 to 1.75
- shift_second: float32 [1024], replicated, may hold values from -3 to 3
- gate_weight: bfloat16 [1024, 4096], P(None, 'tensor'), may hold values from -0.1875 to 0.1875
- up_weight: bfloat16 [1024, 4096], P(None, 'tensor'), may hold values from -0.1875 to 0.1875
- down_weight: bfloat16 [4096, 1024], P('tensor'), may hold values from -0.09375 to 0.09375
- cotangent: bfloat16 [32768, 1024], P(('dp', 'tensor')), may hold values from -6 to 6
Outputs:
- output: bfloat16 [32768, 1024], P(('dp', 'tensor'))
- input_grad: bfloat16 [32768, 1024], P(('dp', 'tensor'))
- grad_query: float32 [1024, 1024], P(None, 'tensor')
- grad_key: float32 [1024, 1024], P(None, 'tensor')
- grad_value: float32 [1024, 1024], P(None, 'tensor')
- grad_output: float32 [1024, 1024], P('tensor')
- grad_gate: float32 [1024, 4096], P(None, 'tensor')
- grad_up: float32 [1024, 4096], P(None, 'tensor')
- grad_down: float32 [4096, 1024], P('tensor')
- grad_gain_first: float32 [1024], replicated
- grad_shift_first: float32 [1024], replicated
- grad_gain_second: float32 [1024], replicated
- grad_shift_second: float32 [1024], replicated
The draws below stay inside these ranges and needn't reach their ends.
Inputs may be any that keep to these rules, and one draw needn't show every extreme that they name: `lengths`: real tokens of each window, from position 0; window 0 is full (2048); the last window holds at most 1024.
All inputs are finite; a program needn't handle non-finite values.
Results may differ from the reference program's by a relative error of at most 0.015.
Values may be sent and summed in bfloat16 or wider, within the bound.
No kernel may reach another device: no remote copies, remote signals or barrier semaphores. Data moves between devices by JAX's collectives and lax.ppermute only.
A program may use at most 256 MiB of HBM per device.

```python
import math
import jax
import jax.numpy as jnp
from jax import lax

D = 1024
H = 16
FF = 4096
HD = 64
LEN = 2048
QBLK = 512
WINDOWS = 16
TOKENS = 32768


def draw_lengths(key, part):
    key_one, key_two, key_three = jax.random.split(key, 3)
    factor_one = jax.random.randint(key_one, (WINDOWS,), 1, LEN + 1)
    factor_two = jax.random.randint(key_two, (WINDOWS,), 1, LEN + 1)
    shorter = jnp.minimum(factor_one * factor_two // LEN + 1, LEN)
    whole = jax.random.randint(key_three, (WINDOWS,), 0, 3) > 0
    drawn = jnp.where(whole, LEN, shorter)
    drawn = drawn.at[WINDOWS - 1].set(jnp.minimum(shorter[WINDOWS - 1], LEN // 2))
    return drawn.at[0].set(LEN).astype(jnp.int32)


def steps_of(own_key, extent, shards, smallest, largest):
    level = 1.0
    for dim, blocks in shards:
        steps = jax.random.uniform(jax.random.fold_in(jax.random.fold_in(own_key, 6), dim), (blocks,), jnp.float32, smallest / len(shards), largest / len(shards))
        level = level * jnp.repeat(jnp.exp(steps), extent[dim] // blocks).reshape((-1,) + (1,) * (len(extent) - 1 - dim))
    return level


def scatter_about(own_key, extent, deviation, most, cuts=(), kind=jnp.bfloat16):
    gain = steps_of(own_key, extent, cuts, -0.22, 0.18) if cuts else 1.0
    array = jax.random.normal(own_key, extent, jnp.float32) * deviation * gain
    return jnp.minimum(jnp.maximum(array, -most), most).astype(kind)


def setup_inputs(seed: int = 0) -> dict:
    arg_keys = jax.random.split(jax.random.key(seed), 15)
    return {
        "tokens": scatter_about(arg_keys[0], (TOKENS, D), 1.0, 6.0, ((0, 32),)),
        "lengths": draw_lengths(jax.random.fold_in(arg_keys[14], 71), 0),
        "gain_first": jnp.clip(1.0 + 0.15 * jax.random.normal(arg_keys[2], (D,), jnp.float32), 0.25, 1.75),
        "shift_first": scatter_about(arg_keys[3], (D,), 0.5, 3.0, (), jnp.float32),
        "query_weight": scatter_about(arg_keys[4], (D, D), D ** -0.5, 0.1875, ((1, 4),)),
        "key_weight": scatter_about(arg_keys[5], (D, D), D ** -0.5, 0.1875, ((1, 4),)),
        "value_weight": scatter_about(arg_keys[6], (D, D), D ** -0.5, 0.1875, ((1, 4),)),
        "output_weight": scatter_about(arg_keys[7], (D, D), (max(D // 256, 2)) ** -0.5, 3.0, ((0, 4),)),
        "gain_second": jnp.clip(1.0 + 0.15 * jax.random.normal(arg_keys[8], (D,), jnp.float32), 0.25, 1.75),
        "shift_second": scatter_about(arg_keys[9], (D,), 0.5, 3.0, (), jnp.float32),
        "gate_weight": scatter_about(arg_keys[10], (D, FF), D ** -0.5, 0.1875, ((1, 4),)),
        "up_weight": scatter_about(arg_keys[11], (D, FF), D ** -0.5, 0.1875, ((1, 4),)),
        "down_weight": scatter_about(arg_keys[12], (FF, D), FF ** -0.5, 0.09375, ((0, 4),)),
        "cotangent": scatter_about(arg_keys[13], (TOKENS, D), 1.0, 6.0, ((0, 32),)),
    }


@jax.custom_vjp
def low(v):
    return lax.optimization_barrier(v.astype(jnp.bfloat16)).astype(jnp.float32)

@jax.custom_vjp
def low_back(v):
    return v

def low_keep(v):
    return (low(v), None)

def low_pass(kept, grad):
    return (grad,)

def back_keep(v):
    return (v, None)

def back_low(kept, grad):
    return (low(grad),)
low.defvjp(low_keep, low_pass)
low_back.defvjp(back_keep, back_low)
EPSILON = 1e-05
MASKED = -1e+30

def layer_norm(inputs, norm_gain, norm_shift):
    row_mean = lax.optimization_barrier(jnp.mean(inputs, axis=-1, keepdims=True))
    centred = inputs - row_mean
    row_scale = lax.rsqrt(lax.optimization_barrier(jnp.mean(jnp.square(centred), axis=-1, keepdims=True)) + EPSILON)
    return centred * row_scale * norm_gain + norm_shift

def rope_tables(length, head_width):
    position = jnp.arange(length, dtype=jnp.float32)
    inverse = 10000.0 ** (-2.0 * jnp.arange(head_width // 2, dtype=jnp.float32) / head_width)
    angles = position[:, None] * inverse[None, :]
    return (jnp.cos(angles), jnp.sin(angles))

def rotate(tensor, cosines, sines):
    half_width = tensor.shape[-1] // 2
    front_half = tensor[..., :half_width]
    back_half = tensor[..., half_width:]
    return jnp.concatenate([front_half * cosines - back_half * sines, front_half * sines + back_half * cosines], axis=-1)

def forward(window_x, weights, length):
    gain_first, shift_first, query_weight, key_weight, value_weight, output_weight, gain_second, shift_second, gate_weight, up_weight, down_weight = weights
    highest = lax.Precision.HIGHEST
    factor = 1.0 / math.sqrt(HD)
    cosines, sines = rope_tables(LEN, HD)

    def split_heads(matrix):
        return matrix.reshape(LEN, H, HD).transpose(1, 0, 2)
    normed_one = low(layer_norm(window_x, gain_first, shift_first))
    queries = low(rotate(split_heads(low_back(jnp.dot(normed_one, query_weight, precision=highest))), cosines, sines))
    keys = low(rotate(split_heads(low_back(jnp.dot(normed_one, key_weight, precision=highest))), cosines, sines))
    values = split_heads(low(low_back(jnp.dot(normed_one, value_weight, precision=highest))))
    key_valid = jnp.arange(LEN) < length

    def score_block(query_block):
        scores = low_back(jnp.einsum('hqd,hkd->hqk', query_block, keys, precision=highest) * factor)
        scores = jnp.where(key_valid[None, None, :], scores, MASKED)
        probs = low(jax.nn.softmax(scores, axis=-1))
        return jnp.einsum('hqk,hkd->hqd', probs, values, precision=highest)
    blocked = queries.reshape(H, LEN // QBLK, QBLK, HD).transpose(1, 0, 2, 3)
    mixed = lax.map(jax.checkpoint(score_block), blocked)
    mixed = mixed.transpose(1, 0, 2, 3).reshape(H, LEN, HD).transpose(1, 0, 2).reshape(LEN, H * HD)
    mixed = low(low_back(mixed))
    hidden_one = window_x + low_back(jnp.dot(mixed, output_weight, precision=highest))
    normed_two = low(layer_norm(hidden_one, gain_second, shift_second))
    gate_pre = low_back(jnp.dot(normed_two, gate_weight, precision=highest))
    up_pre = low_back(jnp.dot(normed_two, up_weight, precision=highest))
    inner = low(jax.nn.silu(gate_pre) * up_pre)
    return hidden_one + jnp.dot(inner, down_weight, precision=highest)

def reference(tokens, lengths, gain_first, shift_first, query_weight, key_weight, value_weight, output_weight, gain_second, shift_second, gate_weight, up_weight, down_weight, cotangent):
    params = tuple((argument.astype(jnp.float32) for argument in (gain_first, shift_first, query_weight, key_weight, value_weight, output_weight, gain_second, shift_second, gate_weight, up_weight, down_weight)))
    inputs = tokens.astype(jnp.float32).reshape(WINDOWS, LEN, D)
    targets = cotangent.astype(jnp.float32).reshape(WINDOWS, LEN, D)

    def window_step(totals, pieces):
        window_in, window_target, length = pieces

        def run_layer(window_x, weights):
            return forward(window_x, weights, length)
        result, pullback = jax.vjp(run_layer, window_in, params)
        grad_in, grad_weights = pullback(window_target)
        totals = jax.tree.map(jnp.add, totals, grad_weights)
        return (totals, (result.astype(jnp.bfloat16), grad_in.astype(jnp.bfloat16)))
    starting = tuple((jnp.zeros_like(argument) for argument in params))
    totals, (results, grads) = lax.scan(window_step, starting, (inputs, targets, lengths))
    return (results.reshape(TOKENS, D), grads.reshape(TOKENS, D), totals[2], totals[3], totals[4], totals[5], totals[8], totals[9], totals[10], totals[0], totals[1], totals[6], totals[7])
```

```python
import functools
import math

import jax
import jax.numpy as jnp
from jax import lax
from jax.experimental import pallas as pl
from jax.experimental.pallas import tpu as pltpu
from jax.sharding import PartitionSpec as P

HD = 64
LEN = 2048
EPSILON = 1e-05
MASKED = -1e30
LANES = 128
LOG2E = math.log2(math.e)
BF16 = jnp.bfloat16
F32 = jnp.float32
MIB = 1 << 20
COST_SHARE = 0.1
PIECES = 4


def contract(left, right, left_dim, right_dim):
    return lax.dot_general(
        left, right, (((left_dim,), (right_dim,)), ((), ())), preferred_element_type=F32
    )


def cost(flops, moved, transcendentals=0):
    return pl.CostEstimate(
        flops=int(flops * COST_SHARE),
        bytes_accessed=int(moved * COST_SHARE),
        transcendentals=int(transcendentals * COST_SHARE),
    )


def swap_halves(value):
    columns = value.shape[1]
    lane = lax.broadcasted_iota(jnp.int32, value.shape, 1)
    return jnp.where(
        lane % HD < HD // 2,
        pltpu.roll(value, columns - HD // 2, 1),
        pltpu.roll(value, HD // 2, 1),
    )


def project_kernel(rows_ref, weight_ref, cos_ref, sin_ref, q_ref, k_ref, v_ref):
    columns = q_ref.shape[1]
    product = contract(rows_ref[...], weight_ref[...], 1, 0)
    cosines = jnp.concatenate([cos_ref[...]] * (columns // LANES), axis=1)
    sines = jnp.concatenate([sin_ref[...]] * (columns // LANES), axis=1)
    for part, out_ref in ((0, q_ref), (1, k_ref)):
        value = product[:, part * columns : (part + 1) * columns]
        out_ref[...] = (value * cosines + swap_halves(value) * sines).astype(BF16)
    v_ref[...] = product[:, 2 * columns :].astype(BF16)


def project(rows, weight, cosines, sines, block=512):
    count, width = rows.shape
    columns = weight.shape[1] // 3
    table = pl.BlockSpec((block, LANES), lambda i: (i, 0))
    out = pl.BlockSpec((block, columns), lambda i: (i, 0))
    return pl.pallas_call(
        project_kernel,
        grid=(count // block,),
        in_specs=[
            pl.BlockSpec((block, width), lambda i: (i, 0)),
            pl.BlockSpec(weight.shape, lambda i: (0, 0)),
            table,
            table,
        ],
        out_specs=[out, out, out],
        out_shape=[jax.ShapeDtypeStruct((count, columns), BF16)] * 3,
        cost_estimate=cost(2 * count * width * 3 * columns, 2 * (count * width + width * 3 * columns + count * 3 * columns), 0),
        compiler_params=pltpu.CompilerParams(vmem_limit_bytes=40 * MIB),
        name="project_rope",
    )(rows, weight, cosines, sines)


def masked_keys(place_ref, key_ref, masked_ref):
    count = key_ref.shape[0]
    lane = lax.broadcasted_iota(jnp.int32, (count, LANES), 1)
    row = lax.broadcasted_iota(jnp.int32, (count, LANES), 0) + place_ref[1]
    position = jnp.where(row >= count, row - count, row)
    bias = jnp.where(position >= place_ref[0], MASKED, 0.0).astype(BF16)
    nothing = jnp.zeros_like(bias)
    key = key_ref[...]
    masked_ref[0] = jnp.where(lane < HD, key, jnp.where(lane == HD, bias, nothing))
    masked_ref[1] = jnp.where(lane >= HD, key, jnp.where(lane == 0, bias, nothing))


def masked_queries(query):
    lane = lax.broadcasted_iota(jnp.int32, query.shape, 1)
    scaled = query * jnp.asarray(1.0 / math.sqrt(HD), BF16)
    one = jnp.ones_like(query)
    nothing = jnp.zeros_like(query)
    return (
        scaled,
        jnp.where(lane < HD, scaled, jnp.where(lane == HD, one, nothing)),
        jnp.where(lane >= HD, scaled, jnp.where(lane == 0, one, nothing)),
    )


def attend_kernel(place_ref, q_ref, k_ref, v_ref, out_ref, log_ref, keys, values_t, *, chunk):
    count = k_ref.shape[0]

    @pl.when(pl.program_id(1) == 0)
    def _():
        masked_keys(place_ref, k_ref, keys)
        values_t[...] = v_ref[...].T

    queries = masked_queries(q_ref[...])[1:]
    mixed, logs = [], []
    for head in range(2):
        scores = [
            contract(keys[head, start : start + chunk, :], queries[head], 1, 1)
            for start in range(0, count, chunk)
        ]
        top = functools.reduce(
            jnp.maximum, [jnp.max(block, axis=0, keepdims=True) for block in scores]
        )
        total = 0.0
        summed = 0.0
        for index, block in enumerate(scores):
            weights = jnp.exp2((block - top) * LOG2E)
            total = total + jnp.sum(weights, axis=0, keepdims=True)
            value = values_t[
                head * HD : (head + 1) * HD, index * chunk : (index + 1) * chunk
            ]
            summed = summed + contract(value, weights.astype(BF16), 1, 0)
        mixed.append(summed / total)
        logs.append(top * LOG2E + jnp.log2(total))
    out_ref[...] = jnp.concatenate(mixed, axis=0).T.astype(BF16)
    log_ref[0] = jnp.concatenate(logs + [jnp.zeros((6, q_ref.shape[0]), F32)], axis=0)


def attend(place, queries, keys, values, block=1024, chunk=512):
    count, columns = queries.shape
    pairs = columns // LANES
    whole = pl.BlockSpec((count, LANES), lambda p, i, _: (0, p))
    rows = pl.BlockSpec((block, LANES), lambda p, i, _: (i, p))
    return pl.pallas_call(
        functools.partial(attend_kernel, chunk=chunk),
        grid_spec=pltpu.PrefetchScalarGridSpec(
            num_scalar_prefetch=1,
            grid=(pairs, count // block),
            in_specs=[rows, whole, whole],
            out_specs=[rows, pl.BlockSpec((1, 8, block), lambda p, i, _: (p, 0, i))],
            scratch_shapes=[
                pltpu.VMEM((2, count, LANES), BF16),
                pltpu.VMEM((LANES, count), BF16),
            ],
        ),
        out_shape=[
            jax.ShapeDtypeStruct((count, columns), BF16),
            jax.ShapeDtypeStruct((pairs, 8, count), F32),
        ],
        cost_estimate=cost(16 * count * count * columns, 8 * count * columns, count * count * columns // HD),
        compiler_params=pltpu.CompilerParams(vmem_limit_bytes=56 * MIB),
        name="attention_forward",
    )(place, queries, keys, values)


def attend_back_kernel(
    place_ref,
    q_ref,
    k_ref,
    v_ref,
    out_ref,
    up_ref,
    log_ref,
    cos_row_ref,
    sin_row_ref,
    cos_ref,
    sin_ref,
    *rest,
    chunk,
):
    grad_ref, keys, grad_keys_t, grad_values_t = rest[-4:]
    count = k_ref.shape[0]
    step = pl.program_id(1)

    @pl.when(step == 0)
    def _():
        masked_keys(place_ref, k_ref, keys)
        grad_keys_t[...] = jnp.zeros_like(grad_keys_t)
        grad_values_t[...] = jnp.zeros_like(grad_values_t)

    scaled, *queries = masked_queries(q_ref[...])
    upstream = up_ref[...]
    lane = lax.broadcasted_iota(jnp.int32, upstream.shape, 1)
    nothing = jnp.zeros_like(upstream)
    products = upstream.astype(F32) * out_ref[...].astype(F32)
    scaled_t = scaled.T
    upstream_t = upstream.T
    logs = log_ref[0].T
    grad_queries = []
    for head in range(2):
        mine = (lane < HD) == (head == 0)
        own_upstream = jnp.where(mine, upstream, nothing)
        row_dot = jnp.sum(jnp.where(mine, products, 0.0), axis=1, keepdims=True)
        log_total = logs[:, head : head + 1]
        heads = slice(head * HD, (head + 1) * HD)
        grad_query = 0.0
        for start in range(0, count, chunk):
            span = slice(start, start + chunk)
            scores = contract(queries[head], keys[head, span, :], 1, 1)
            probs = jnp.exp2(scores * LOG2E - log_total)
            grad_probs = contract(own_upstream, v_ref[span, :], 1, 1)
            grad_scores = (probs * (grad_probs - row_dot)).astype(BF16)
            grad_values_t[heads, span] += contract(
                upstream_t[heads, :], probs.astype(BF16), 1, 0
            )
            grad_keys_t[heads, span] += contract(scaled_t[heads, :], grad_scores, 1, 0)
            grad_query = grad_query + contract(grad_scores, k_ref[span, :], 1, 0)
        grad_queries.append(grad_query)
    grad_query = jnp.where(lane < HD, *grad_queries) * (1.0 / math.sqrt(HD))
    block = grad_query.shape[0]
    grad_ref[0, pl.ds(pl.multiple_of(step * block, block), block), :] = (
        grad_query * cos_row_ref[...] - swap_halves(grad_query) * sin_row_ref[...]
    ).astype(BF16)

    @pl.when(step == pl.num_programs(1) - 1)
    def _():
        grad_key = grad_keys_t[...].T
        grad_ref[1] = (
            grad_key * cos_ref[...] - swap_halves(grad_key) * sin_ref[...]
        ).astype(BF16)
        grad_ref[2] = grad_values_t[...].T.astype(BF16)


def attend_back(
    place, queries, keys, values, mixed, upstream, logs, cosines, sines, pair, grads, block=512, chunk=512
):
    count, columns = queries.shape
    whole = pl.BlockSpec((count, LANES), lambda p, i, _: (0, pair))
    rows = pl.BlockSpec((block, LANES), lambda p, i, _: (i, pair))
    table = pl.BlockSpec((count, LANES), lambda p, i, _: (0, 0))
    table_rows = pl.BlockSpec((block, LANES), lambda p, i, _: (i, 0))
    held = [] if grads is None else [grads]
    return pl.pallas_call(
        functools.partial(attend_back_kernel, chunk=chunk),
        grid_spec=pltpu.PrefetchScalarGridSpec(
            num_scalar_prefetch=1,
            grid=(1, count // block),
            in_specs=[
                rows,
                whole,
                whole,
                rows,
                rows,
                pl.BlockSpec((1, 8, block), lambda p, i, _: (pair, 0, i)),
                table_rows,
                table_rows,
                table,
                table,
            ]
            + [pl.BlockSpec(memory_space=pl.ANY)] * len(held),
            out_specs=pl.BlockSpec((3, count, LANES), lambda p, i, _: (0, 0, pair)),
            scratch_shapes=[
                pltpu.VMEM((2, count, LANES), BF16),
                pltpu.VMEM((LANES, count), F32),
                pltpu.VMEM((LANES, count), F32),
            ],
        ),
        out_shape=jax.ShapeDtypeStruct((3, count, columns), BF16),
        input_output_aliases={11: 0} if held else {},
        cost_estimate=cost(28 * count * count * LANES, 16 * count * LANES, count * count * 2),
        compiler_params=pltpu.CompilerParams(vmem_limit_bytes=60 * MIB),
        name="attention_backward",
    )(place, queries, keys, values, mixed, upstream, logs, cosines, sines, cosines, sines, *held)


def feed_kernel(
    rows_ref,
    target_ref,
    gate_ref,
    up_ref,
    down_ref,
    inner_ref,
    grad_gate_ref,
    grad_up_ref,
    weight_gate_ref,
    weight_up_ref,
    weight_down_ref,
    rows_t,
    target_t,
    *,
    chunk,
):
    @pl.when(pl.program_id(0) == 0)
    def _():
        rows_t[...] = rows_ref[...].T
        target_t[...] = target_ref[...].T

    for start in range(0, rows_ref.shape[0], chunk):
        span = slice(start, start + chunk)
        gate = contract(rows_ref[span, :], gate_ref[...], 1, 0)
        up = contract(rows_ref[span, :], up_ref[...], 1, 0)
        grad_inner = contract(target_ref[span, :], down_ref[...], 1, 1)
        share = jax.nn.sigmoid(gate)
        activated = gate * share
        inner_ref[span, :] = (activated * up).astype(BF16)
        grad_up_ref[span, :] = (grad_inner * activated).astype(BF16)
        grad_gate_ref[span, :] = (
            grad_inner * up * share * (1.0 + gate * (1.0 - share))
        ).astype(BF16)
    weight_gate_ref[...] = contract(rows_t[...], grad_gate_ref[...], 1, 0).astype(BF16)
    weight_up_ref[...] = contract(rows_t[...], grad_up_ref[...], 1, 0).astype(BF16)
    weight_down_ref[...] = contract(target_t[...], inner_ref[...], 1, 0).T.astype(BF16)


def feed(rows, target, gate_weight, up_weight, down_weight, block=256, chunk=512):
    count, width = rows.shape
    units = gate_weight.shape[1]
    block = min(block, units)
    whole = pl.BlockSpec((count, width), lambda i: (0, 0), pipeline_mode=pl.Buffered(1))
    across = pl.BlockSpec((width, block), lambda i: (0, i))
    down = pl.BlockSpec((block, width), lambda i: (i, 0))
    out = pl.BlockSpec((count, block), lambda i: (0, i))
    return pl.pallas_call(
        functools.partial(feed_kernel, chunk=chunk),
        grid=(units // block,),
        in_specs=[whole, whole, across, across, down],
        out_specs=[out, out, out, across, across, down],
        out_shape=[jax.ShapeDtypeStruct((count, units), BF16)] * 3
        + [jax.ShapeDtypeStruct((width, units), BF16)] * 2
        + [jax.ShapeDtypeStruct((units, width), BF16)],
        scratch_shapes=[pltpu.VMEM((width, count), BF16)] * 2,
        cost_estimate=cost(
            12 * count * width * units,
            4 * count * width + 12 * width * units + 6 * count * units,
            2 * count * units,
        ),
        compiler_params=pltpu.CompilerParams(vmem_limit_bytes=60 * MIB),
        name="feed_forward",
    )(rows, target, gate_weight, up_weight, down_weight)


def sum_kernel(*refs, dims):
    total = 0.0
    for index, dim in enumerate(dims):
        total = total + contract(refs[2 * index][...], refs[2 * index + 1][...], 1, dim)
    refs[-1][...] = total.astype(refs[-1].dtype)


def sum_products(terms, start, rows, dtype=F32, block=512):
    block = min(block, rows)
    first = start // block
    operands, specs, dims, flops, moved = [], [], [], 0, 0
    for left, plane, right, part, dim in terms:
        depth = left.shape[-1]
        if plane is None:
            specs.append(pl.BlockSpec((block, depth), lambda i: (first + i, 0)))
        else:
            specs.append(
                pl.BlockSpec((None, block, depth), lambda i, plane=plane: (plane, first + i, 0))
            )
        shape = right.shape if part is None else (right.shape[0], depth)
        column = 0 if part is None else part
        specs.append(pl.BlockSpec(shape, lambda i, column=column: (0, column)))
        operands += [left, right]
        dims.append(dim)
        width = shape[1 - dim]
        flops += 2 * rows * depth * width
        moved += 2 * rows * depth + 2 * depth * width
    return pl.pallas_call(
        functools.partial(sum_kernel, dims=tuple(dims)),
        grid=(rows // block,),
        in_specs=specs,
        out_specs=pl.BlockSpec((block, width), lambda i: (i, 0)),
        out_shape=jax.ShapeDtypeStruct((rows, width), dtype),
        cost_estimate=cost(flops, moved + 4 * rows * width),
        compiler_params=pltpu.CompilerParams(vmem_limit_bytes=58 * MIB),
        name="sum_products",
    )(*operands)


def outer_kernel(left_ref, right_ref, out_ref, left_t):
    @pl.when(pl.program_id(0) == 0)
    def _():
        left_t[...] = left_ref[...].T

    out_ref[...] = contract(left_t[...], right_ref[...], 1, 0).astype(BF16)


def outer(left, right, block):
    count, width = left.shape
    columns = right.shape[-1]
    if right.ndim == 3:
        steps = right.shape[0]
        block = columns
        spec = pl.BlockSpec((None, count, columns), lambda i: (i, 0, 0))
    else:
        steps = columns // block
        spec = pl.BlockSpec((count, block), lambda i: (0, i))
    return pl.pallas_call(
        outer_kernel,
        grid=(steps,),
        in_specs=[
            pl.BlockSpec((count, width), lambda i: (0, 0), pipeline_mode=pl.Buffered(1)),
            spec,
        ],
        out_specs=pl.BlockSpec((width, block), lambda i: (0, i)),
        out_shape=jax.ShapeDtypeStruct((width, steps * block), BF16),
        scratch_shapes=[pltpu.VMEM((width, count), BF16)],
        cost_estimate=cost(
            2 * count * width * steps * block,
            2 * count * (width + steps * block) + 2 * width * steps * block,
        ),
        compiler_params=pltpu.CompilerParams(vmem_limit_bytes=40 * MIB),
        name="outer_product",
    )(left, right)


def standardize(value):
    centred = value - jnp.mean(value, axis=-1, keepdims=True)
    scale = lax.rsqrt(jnp.mean(centred * centred, axis=-1, keepdims=True) + EPSILON)
    return centred * scale, scale


def norm_kernel(*refs, added):
    value = refs[0][...].astype(F32)
    for ref in refs[1 : 1 + added]:
        value = value + ref[...].astype(F32)
    gain_ref, shift_ref = refs[1 + added : 3 + added]
    standard, _ = standardize(value)
    if added:
        refs[-2][...] = value
    refs[-1][...] = (standard * gain_ref[...] + shift_ref[...]).astype(BF16)


def norm(base, terms, gain, shift, pieces=PIECES, block=256):
    count, width = base.shape
    rows = count // pieces
    block = min(block, rows)
    vector = pl.BlockSpec((1, width), lambda i: (0, 0))
    total, out = None, []
    for piece in range(pieces):
        first = piece * rows // block
        whole = pl.BlockSpec((block, width), lambda i, first=first: (first + i, 0))
        shapes = [jax.ShapeDtypeStruct((rows, width), BF16)]
        specs = [pl.BlockSpec((block, width), lambda i: (i, 0))]
        held = []
        if terms:
            shapes = [jax.ShapeDtypeStruct((count, width), F32)] + shapes
            specs = [whole] + specs
            held = [] if total is None else [total]
        results = pl.pallas_call(
            lambda *refs, held=len(held): norm_kernel(
                *refs[: 3 + len(terms)], *refs[3 + len(terms) + held :], added=len(terms)
            ),
            grid=(rows // block,),
            in_specs=[whole] * (1 + len(terms))
            + [vector, vector]
            + [pl.BlockSpec(memory_space=pl.ANY)] * len(held),
            out_specs=specs,
            out_shape=shapes,
            input_output_aliases={3 + len(terms): 0} if held else {},
            cost_estimate=cost(16 * rows * width, 8 * rows * width * len(shapes)),
            name="layer_norm",
        )(base, *terms, gain.reshape(1, width), shift.reshape(1, width), *held)
        out.append(results[-1])
        if terms:
            total = results[0]
    return total, out


def norm_back_kernel(*refs, added, low):
    base_ref, straight_ref, gain_ref = refs[:3]
    upstream = refs[3][...].astype(F32)
    for ref in refs[4 : 3 + added]:
        upstream = upstream + ref[...].astype(F32)
    outs = refs[3 + added :]
    standard, scale = standardize(base_ref[...].astype(F32))
    scaled = upstream * gain_ref[...]
    back = straight_ref[...].astype(F32) + scale * (
        scaled
        - jnp.mean(scaled, axis=-1, keepdims=True)
        - standard * jnp.mean(scaled * standard, axis=-1, keepdims=True)
    )
    outs[0][...] = back.astype(BF16)
    if not low:
        outs[1][...] = back
    sums = jnp.concatenate(
        [
            jnp.sum(upstream * standard, axis=0, keepdims=True),
            jnp.sum(upstream, axis=0, keepdims=True),
        ],
        axis=0,
    )

    @pl.when(pl.program_id(0) == 0)
    def _():
        outs[-1][...] = sums

    @pl.when(pl.program_id(0) > 0)
    def _():
        outs[-1][...] += sums


def norm_back(base, straight, gain, terms, low, pieces=PIECES, block=256):
    count, width = base.shape
    rows = count // pieces
    block = min(block, rows)
    total, out, found = None, [], []
    for piece in range(pieces):
        first = piece * rows // block
        whole = pl.BlockSpec((block, width), lambda i, first=first: (first + i, 0))
        shapes = [jax.ShapeDtypeStruct((rows, width), BF16)]
        specs = [pl.BlockSpec((block, width), lambda i: (i, 0))]
        held = []
        if not low:
            shapes.append(jax.ShapeDtypeStruct((count, width), F32))
            specs.append(whole)
            held = [] if total is None else [total]
        results = pl.pallas_call(
            lambda *refs, held=len(held): norm_back_kernel(
                *refs[: 3 + len(terms)],
                *refs[3 + len(terms) + held :],
                added=len(terms),
                low=low,
            ),
            grid=(rows // block,),
            in_specs=[whole, whole, pl.BlockSpec((1, width), lambda i: (0, 0))]
            + [whole] * len(terms)
            + [pl.BlockSpec(memory_space=pl.ANY)] * len(held),
            out_specs=specs + [pl.BlockSpec((2, width), lambda i: (0, 0))],
            out_shape=shapes + [jax.ShapeDtypeStruct((2, width), F32)],
            input_output_aliases={3 + len(terms): 1} if held else {},
            cost_estimate=cost(30 * rows * width, 16 * rows * width),
            name="layer_norm_backward",
        )(base, straight, gain.reshape(1, width), *terms, *held)
        out.append(results[0])
        found.append(results[-1])
        if not low:
            total = results[1]
    return out, total, sum(found)


def rope_tables(offset):
    position = (jnp.arange(LEN, dtype=jnp.int32) + offset) % LEN
    inverse = 10000.0 ** (-2.0 * jnp.arange(HD // 2, dtype=F32) / HD)
    angles = position.astype(F32)[:, None] * inverse[None, :]
    cosines, sines = jnp.cos(angles), jnp.sin(angles)
    return (
        jnp.concatenate([cosines] * 4, axis=1),
        jnp.concatenate([-sines, sines, -sines, sines], axis=1),
    )


def exchanges(axis, size):
    if size & (size - 1):
        return [lambda value: lax.psum(value, axis)]
    return [
        lambda value, pairs=[(i, i ^ (1 << bit)) for i in range(size)]: value
        + lax.ppermute(value, axis, pairs)
        for bit in range(size.bit_length() - 1)
    ]


def shards(
    dp_size,
    tensor_size,
    tokens,
    lengths,
    gain_first,
    shift_first,
    query_weight,
    key_weight,
    value_weight,
    output_weight,
    gain_second,
    shift_second,
    gate_weight,
    up_weight,
    down_weight,
    cotangent,
):
    windows = lengths.shape[0]
    span = tensor_size // windows
    held = tokens.shape[0]
    width = tokens.shape[1]
    head_cols = query_weight.shape[1]
    here = lax.axis_index("tensor")
    window, seat = here // span, here % span

    def from_seat(value, shift):
        pairs = [
            (w * span + (s + shift) % span, w * span + s)
            for w in range(windows)
            for s in range(span)
        ]
        return lax.ppermute(value, "tensor", pairs)

    def to_seat(value, shift):
        return from_seat(value, span - shift)

    def from_window(value, shift):
        pairs = [((t + shift * span) % tensor_size, t) for t in range(tensor_size)]
        return lax.ppermute(value, "tensor", pairs)

    def to_window(value, shift):
        return from_window(value, windows - shift)

    def gather_rows(value):
        return jnp.concatenate(
            value + [from_seat(piece, s) for s in range(1, span) for piece in value], axis=0
        )

    def scatter(partial):
        sent = [to_seat(partial(s * held, held), s) for s in range(1, span)]
        return [partial(0, held)] + sent

    def all_windows(value):
        return [value] + [from_window(value, shift) for shift in range(1, windows)]

    def spread_windows(values):
        group = lax.axis_index("dp")
        sizes = [value.shape[0] // dp_size for value in values]
        mine = jnp.concatenate(
            [
                lax.dynamic_slice_in_dim(value, group * size, size, axis=0).reshape(-1, width)
                for value, size in zip(values, sizes)
            ],
            axis=0,
        )
        return [mine], [from_window(mine, shift) for shift in range(1, windows)]

    def gather_spread(values, piece):
        gathered = lax.all_gather(piece, "dp", axis=0)
        out, start = [], 0
        for value in values:
            count = value.size // width // dp_size
            out.append(gathered[:, start : start + count].reshape(value.shape))
            start += count
        return out

    def after(value, *others):
        return lax.optimization_barrier((value, *others))[0]

    place = jnp.stack(
        [lax.dynamic_index_in_dim(lengths, window, keepdims=False), seat * held]
    ).astype(jnp.int32)
    cosines, sines = rope_tables(seat * held)

    members = [[s] for s in range(windows)] if head_cols % LANES == 0 else [list(range(windows))]
    feed_weights = [gate_weight, up_weight, down_weight]
    slices_sent, slices = spread_windows(feed_weights)
    _, normed_one = norm(after(tokens, *slices_sent), [], gain_first, shift_first)
    full_one = gather_rows(normed_one)
    qkv_own = jnp.concatenate([query_weight, key_weight, value_weight], axis=1)
    qkv_other = all_windows(after(qkv_own, *slices))[1:]
    qkv_shards = [qkv_own] + qkv_other
    def joined(parts, axis):
        return parts[0] if len(parts) == 1 else jnp.concatenate(parts, axis=axis)

    def part_of(value, part):
        return value[:, part * head_cols : (part + 1) * head_cols]

    qkv_weights = [
        qkv_shards[group[0]]
        if len(group) == 1
        else joined([part_of(qkv_shards[s], part) for part in range(3) for s in group], 1)
        for group in members
    ]
    target = gather_rows([cotangent])
    qkv, attended = [], []
    rows_one = full_one
    for weight in qkv_weights:
        parts = project(rows_one, weight, cosines, sines)
        if not qkv:
            slices = [after(piece, parts[0]) for piece in slices]
            feed_shards = [feed_weights]
            feed_shards += [gather_spread(feed_weights, piece) for piece in slices]
        waits = slices if not qkv else [target]
        qkv.append((after(parts[0], *waits), *parts[1:]))
        attended.append(attend(place, *qkv[-1]))
        if len(attended) == 1:
            sent = after(output_weight, attended[0][0])
            output_shards = [output_weight] + all_windows(sent)[1:]
        rows_one = after(full_one, attended[-1][0])

    out_weights = [joined([output_shards[s] for s in group], 0) for group in members]
    mixer_terms = [
        (mixed, None, weight, None, 0) for (mixed, _), weight in zip(attended, out_weights)
    ]
    hidden_one, normed_two = norm(
        tokens,
        scatter(lambda start, rows: sum_products(mixer_terms, start, rows)),
        gain_second,
        shift_second,
    )
    full_two = gather_rows(normed_two)

    flip = [(d, d ^ 1) for d in range(dp_size)]
    odd = lax.axis_index("dp") % 2

    def half(value, which):
        count = value.shape[0] // 2
        return lax.dynamic_slice_in_dim(value, which * count, count, axis=0)

    def total(pieces, which):
        return sum(half(piece, which).astype(F32) for piece in pieces).astype(BF16)

    def swap_half(pieces, *others):
        pieces = [after(piece, *others) for piece in pieces]
        mine, sent = total(pieces, odd), total(pieces, 1 - odd)
        return (mine, lax.ppermute(sent, "dp", flip)), [mine, sent]

    def add_half(halves, *others):
        mine, received = (after(value, *others) for value in halves)
        return (mine.astype(F32) + received.astype(F32)).astype(BF16)

    def sum_half(value, turn):
        groups = [list(range(0, dp_size, 2)), list(range(1, dp_size, 2))]
        if turn & 1:
            groups = groups[::-1]
        if turn & 2:
            groups = [group[::-1] for group in groups]
        return lax.psum(value, "dp", axis_index_groups=groups)

    def swap_sum(mine, *others):
        mine = after(mine, *others)
        return mine, lax.ppermute(mine, "dp", flip)

    def whole_sum(halves, *others):
        mine, received = (after(value, *others) for value in halves)
        first, second = jnp.where(odd == 0, mine, received), jnp.where(odd == 0, received, mine)
        return jnp.concatenate([first, second], axis=0).astype(F32)

    def send_to_owner(parts):
        return [to_window(parts[shift], shift) for shift in range(1, windows)]

    order = list(range(1, windows)) + [0]
    fed = {}
    rows_two = full_two
    for s in order:
        fed[s] = feed(rows_two, target, *feed_shards[s])
        rows_two = after(full_two, fed[s][0])
    down_pieces, up_pieces, gate_pieces = (
        send_to_owner({s: fed[s][k] for s in order}) + [fed[0][k]] for k in (5, 4, 3)
    )
    two_terms, feed_terms = [], []
    for s in order:
        gate, up, down = feed_shards[s]
        two_terms += [(fed[s][1], None, gate, None, 1), (fed[s][2], None, up, None, 1)]
        feed_terms.append((fed[s][0], None, down, None, 0))

    two_sent = [
        sum_products(two_terms, shift * held, held, BF16) for shift in range(1, span)
    ]
    down_half, marks = swap_half(down_pieces, *two_sent)
    two_terms = [(after(two_terms[0][0], *marks), *two_terms[0][1:])] + two_terms[1:]
    two_kept = sum_products(two_terms, 0, held)
    grad_branch_own, grad_hidden, norm_two = norm_back(
        hidden_one,
        cotangent,
        gain_second,
        [two_kept] + [to_seat(part, shift + 1) for shift, part in enumerate(two_sent)],
        False,
    )
    grad_branch = gather_rows(grad_branch_own)
    down_half = add_half(down_half, *grad_branch_own)
    down_sum = sum_half(down_half, 0)
    grad_branch = after(grad_branch, down_half)

    members = members[::-1]
    out_weights, qkv_weights = out_weights[::-1], qkv_weights[::-1]
    qkv, attended = qkv[::-1], attended[::-1]
    out_grads, grad_mixed = {}, []
    for group, weight, (mixed, _) in zip(members, out_weights, attended):
        grad_mixed.append(sum_products([(grad_branch, None, weight, None, 1)], 0, LEN, BF16))
        out_grad = outer(mixed, grad_branch, min(512, width))
        for spot, s in enumerate(group):
            out_grads[s] = out_grad[spot * head_cols : (spot + 1) * head_cols]
    out_pieces = send_to_owner(out_grads) + [out_grads[0]]

    def up_swap(last):
        sums["up"], waits = swap_half(up_pieces, *last)
        return waits

    def up_sum(last):
        value = add_half(sums["up"], *last)
        sums["up"] = sum_half(value, 1)
        sums["down"] = swap_sum(down_sum, *last)
        return [value, sums["down"][0]]

    def gate_swap(last):
        sums["gate"], waits = swap_half(gate_pieces, *last)
        sums["out"], more = swap_half(out_pieces, *last)
        sums["down"] = whole_sum(sums["down"], *last)
        return waits + more + [sums["down"]]

    def gate_sum(last):
        values = [add_half(sums["gate"], *last), add_half(sums["out"], *last)]
        sums["gate"], sums["out"] = sum_half(tuple(values), 2)
        sums["up"] = swap_sum(sums["up"], *last)
        return values + [sums["up"][0]]

    across, along = (exchanges(axis, size) for axis, size in (("tensor", tensor_size), ("dp", dp_size)))
    norm_steps = across + along[1:]
    sums = {}
    moves = [up_swap, up_sum, gate_swap, gate_sum]
    last = list(out_grads.values()) + grad_mixed
    grad_qkv, qkv_grads = [], {}
    for index, group in enumerate(members):
        mixed, logs = attended[index]
        count = len(group) * head_cols
        grads = None
        for pair in range(count // LANES):
            waits = moves.pop(0)(last) if moves else last
            if norm_steps:
                norm_two = norm_steps.pop(0)(after(norm_two, *last))
                waits = waits + [norm_two]
            grads = attend_back(
                place,
                *qkv[index],
                mixed,
                after(grad_mixed[index], *waits),
                logs,
                cosines,
                sines,
                pair,
                grads,
            )
            last = [grads]
        grad_qkv.append(grads)
        qkv_grad = outer(full_one, grads, count)
        last = [qkv_grad]
        for spot, s in enumerate(group):
            if len(group) == 1:
                qkv_grads[s] = qkv_grad
            else:
                qkv_grads[s] = joined(
                    [
                        lax.slice_in_dim(
                            qkv_grad,
                            part * count + spot * head_cols,
                            part * count + (spot + 1) * head_cols,
                            axis=1,
                        )
                        for part in range(3)
                    ],
                    1,
                )
    for move in moves:
        last = move(last)

    qkv_half, marks = swap_half(send_to_owner(qkv_grads) + [qkv_grads[0]])
    feed_terms[0] = (after(feed_terms[0][0], *marks), *feed_terms[0][1:])
    feed_sent = [sum_products(feed_terms, shift * held, held, BF16) for shift in range(1, span)]
    feed_terms[0] = (after(feed_terms[0][0], *feed_sent), *feed_terms[0][1:])
    feed_parts = [sum_products(feed_terms, 0, held)]
    feed_parts += [to_seat(part, shift + 1) for shift, part in enumerate(feed_sent)]
    qkv_half = add_half(qkv_half, sums["gate"], feed_parts[0])
    qkv_sum = sum_half(qkv_half, 3)
    one_terms = [
        (grad_qkv[index], part, weight, part, 1)
        for index, weight in enumerate(qkv_weights)
        for part in range(3)
    ]
    one_terms[0] = (after(one_terms[0][0], qkv_half), *one_terms[0][1:])
    one_parts = scatter(
        lambda start, rows: sum_products(one_terms, start, rows, BF16 if start else F32)
    )
    (input_grad,), _, norm_one = norm_back(tokens, grad_hidden, gain_first, one_parts, True, 1)
    output = (hidden_one + sum(feed_parts)).astype(BF16)
    grad_down = sums["down"]
    grad_up = whole_sum(sums["up"], input_grad)
    grad_gate = whole_sum(swap_sum(sums["gate"], one_parts[0]), input_grad)
    out_grad = whole_sum(swap_sum(sums["out"], one_parts[0]), input_grad)
    for step in across + along[1:]:
        norm_one = step(norm_one)
    for step in norm_steps:
        norm_two = step(norm_two)
    norms = along[0](jnp.concatenate([norm_one, norm_two], axis=0))
    qkv_grad = whole_sum(swap_sum(qkv_sum, input_grad))

    return (
        output,
        input_grad,
        *(part_of(qkv_grad, part) for part in range(3)),
        out_grad,
        grad_gate,
        grad_up,
        grad_down,
        norms[0],
        norms[1],
        norms[2],
        norms[3],
    )


def solution(mesh):
    rows = P(("dp", "tensor"), None)
    columns = P(None, "tensor")
    depth = P("tensor", None)
    return jax.shard_map(
        functools.partial(shards, mesh.shape["dp"], mesh.shape["tensor"]),
        mesh=mesh,
        in_specs=(
            rows,
            P("dp"),
            P(),
            P(),
            columns,
            columns,
            columns,
            depth,
            P(),
            P(),
            columns,
            columns,
            depth,
            rows,
        ),
        out_specs=(
            rows,
            rows,
            columns,
            columns,
            columns,
            depth,
            columns,
            columns,
            depth,
            P(),
            P(),
            P(),
            P(),
        ),
        check_vma=False,
    )
```

```python
import functools
import math

import jax
import jax.numpy as jnp
from jax import lax
from jax.experimental import pallas as pl
from jax.experimental.pallas import tpu as pltpu
from jax.sharding import PartitionSpec as P

HD = 64
LEN = 2048
EPSILON = 1e-05
MASKED = -1e30
LANES = 128
LOG2E = math.log2(math.e)
BF16 = jnp.bfloat16
F32 = jnp.float32
MIB = 1 << 20
COST_SHARE = 0.1
PIECES = 2


def contract(left, right, left_dim, right_dim):
    return lax.dot_general(
        left, right, (((left_dim,), (right_dim,)), ((), ())), preferred_element_type=F32
    )


def cost(flops, moved, transcendentals=0):
    return pl.CostEstimate(
        flops=int(flops * COST_SHARE),
        bytes_accessed=int(moved * COST_SHARE),
        transcendentals=int(transcendentals * COST_SHARE),
    )


def swap_halves(value):
    columns = value.shape[1]
    lane = lax.broadcasted_iota(jnp.int32, value.shape, 1)
    return jnp.where(
        lane % HD < HD // 2,
        pltpu.roll(value, columns - HD // 2, 1),
        pltpu.roll(value, HD // 2, 1),
    )


def fetch(pieces, rows, sems):
    copies, start = [], 0
    for index, piece in enumerate(pieces):
        count = piece.shape[0]
        copies.append(
            pltpu.make_async_copy(piece, rows.at[pl.ds(start, count), :], sems.at[index])
        )
        start += count
    for copy in copies:
        copy.start()
    return copies


def room(pieces):
    count = sum(piece.shape[0] for piece in pieces)
    return [
        pltpu.VMEM((count, pieces[0].shape[1]), BF16),
        pltpu.SemaphoreType.DMA((len(pieces),)),
    ]


def unpacked(ref):
    value = ref[...]
    return value.reshape(-1, value.shape[-1]) if value.ndim == 3 else value


def packed(weight):
    return isinstance(weight, tuple)


def project_kernel(*refs, count):
    pieces = refs[:count]
    weight_ref, cos_ref, sin_ref, q_ref, k_ref, v_ref, rows, sems = refs[count:]
    columns = q_ref.shape[1]
    block = q_ref.shape[0]

    @pl.when(pl.program_id(0) == 0)
    def _():
        for copy in fetch(pieces, rows, sems):
            copy.wait()

    start = pl.multiple_of(pl.program_id(0) * block, block)
    product = contract(rows[pl.ds(start, block), :], weight_ref[...], 1, 0)
    cosines = jnp.concatenate([cos_ref[...]] * (columns // LANES), axis=1)
    sines = jnp.concatenate([sin_ref[...]] * (columns // LANES), axis=1)
    for part, out_ref in ((0, q_ref), (1, k_ref)):
        value = product[:, part * columns : (part + 1) * columns]
        out_ref[...] = (value * cosines + swap_halves(value) * sines).astype(BF16)
    v_ref[...] = product[:, 2 * columns :].astype(BF16)


def project(pieces, weight, cosines, sines, block=512):
    width = weight.shape[0]
    columns = weight.shape[1] // 3
    count = sum(piece.shape[0] for piece in pieces)
    table = pl.BlockSpec((block, LANES), lambda i: (i, 0))
    out = pl.BlockSpec((block, columns), lambda i: (i, 0))
    return pl.pallas_call(
        functools.partial(project_kernel, count=len(pieces)),
        grid=(count // block,),
        in_specs=[pl.BlockSpec(memory_space=pl.ANY)] * len(pieces)
        + [pl.BlockSpec(weight.shape, lambda i: (0, 0)), table, table],
        out_specs=[out, out, out],
        out_shape=[jax.ShapeDtypeStruct((count, columns), BF16)] * 3,
        scratch_shapes=room(pieces),
        cost_estimate=cost(
            2 * count * width * 3 * columns,
            2 * (count * width + width * 3 * columns + count * 3 * columns),
        ),
        compiler_params=pltpu.CompilerParams(vmem_limit_bytes=40 * MIB),
        name="project_rope",
    )(*pieces, weight, cosines, sines)


def masked_keys(place_ref, key_ref, masked_ref):
    count = key_ref.shape[0]
    lane = lax.broadcasted_iota(jnp.int32, (count, LANES), 1)
    row = lax.broadcasted_iota(jnp.int32, (count, LANES), 0) + place_ref[1]
    position = jnp.where(row >= count, row - count, row)
    bias = jnp.where(position >= place_ref[0], MASKED, 0.0).astype(BF16)
    nothing = jnp.zeros_like(bias)
    key = key_ref[...]
    masked_ref[0] = jnp.where(lane < HD, key, jnp.where(lane == HD, bias, nothing))
    masked_ref[1] = jnp.where(lane >= HD, key, jnp.where(lane == 0, bias, nothing))


def masked_queries(query):
    lane = lax.broadcasted_iota(jnp.int32, query.shape, 1)
    scaled = query * jnp.asarray(1.0 / math.sqrt(HD), BF16)
    one = jnp.ones_like(query)
    nothing = jnp.zeros_like(query)
    return (
        scaled,
        jnp.where(lane < HD, scaled, jnp.where(lane == HD, one, nothing)),
        jnp.where(lane >= HD, scaled, jnp.where(lane == 0, one, nothing)),
    )


def attend_kernel(place_ref, q_ref, k_ref, v_ref, out_ref, log_ref, keys, values_t, *, chunk):
    count = k_ref.shape[0]

    @pl.when(pl.program_id(1) == 0)
    def _():
        masked_keys(place_ref, k_ref, keys)
        values_t[...] = v_ref[...].T

    queries = masked_queries(q_ref[...])[1:]
    mixed, logs = [], []
    for head in range(2):
        scores = [
            contract(keys[head, start : start + chunk, :], queries[head], 1, 1)
            for start in range(0, count, chunk)
        ]
        top = functools.reduce(
            jnp.maximum, [jnp.max(block, axis=0, keepdims=True) for block in scores]
        )
        total = 0.0
        summed = 0.0
        for index, block in enumerate(scores):
            weights = jnp.exp2((block - top) * LOG2E)
            total = total + jnp.sum(weights, axis=0, keepdims=True)
            value = values_t[
                head * HD : (head + 1) * HD, index * chunk : (index + 1) * chunk
            ]
            summed = summed + contract(value, weights.astype(BF16), 1, 0)
        mixed.append(summed / total)
        logs.append(top * LOG2E + jnp.log2(total))
    out_ref[...] = jnp.concatenate(mixed, axis=0).T.astype(BF16)
    log_ref[0] = jnp.concatenate(logs + [jnp.zeros((6, q_ref.shape[0]), F32)], axis=0)


def attend(place, queries, keys, values, block=1024, chunk=512):
    count, columns = queries.shape
    pairs = columns // LANES
    whole = pl.BlockSpec((count, LANES), lambda p, i, _: (0, p))
    rows = pl.BlockSpec((block, LANES), lambda p, i, _: (i, p))
    return pl.pallas_call(
        functools.partial(attend_kernel, chunk=chunk),
        grid_spec=pltpu.PrefetchScalarGridSpec(
            num_scalar_prefetch=1,
            grid=(pairs, count // block),
            in_specs=[rows, whole, whole],
            out_specs=[rows, pl.BlockSpec((1, 8, block), lambda p, i, _: (p, 0, i))],
            scratch_shapes=[
                pltpu.VMEM((2, count, LANES), BF16),
                pltpu.VMEM((LANES, count), BF16),
            ],
        ),
        out_shape=[
            jax.ShapeDtypeStruct((count, columns), BF16),
            jax.ShapeDtypeStruct((pairs, 8, count), F32),
        ],
        cost_estimate=cost(16 * count * count * columns, 8 * count * columns, count * count * columns // HD),
        compiler_params=pltpu.CompilerParams(vmem_limit_bytes=56 * MIB),
        name="attention_forward",
    )(place, queries, keys, values)


def attend_back_kernel(
    place_ref,
    q_ref,
    k_ref,
    v_ref,
    out_ref,
    up_ref,
    log_ref,
    cos_row_ref,
    sin_row_ref,
    cos_ref,
    sin_ref,
    *rest,
    chunk,
):
    grad_ref, keys, grad_keys_t, grad_values_t = rest[-4:]
    count = k_ref.shape[0]
    step = pl.program_id(1)

    @pl.when(step == 0)
    def _():
        masked_keys(place_ref, k_ref, keys)
        grad_keys_t[...] = jnp.zeros_like(grad_keys_t)
        grad_values_t[...] = jnp.zeros_like(grad_values_t)

    scaled, *queries = masked_queries(q_ref[...])
    upstream = up_ref[...]
    lane = lax.broadcasted_iota(jnp.int32, upstream.shape, 1)
    nothing = jnp.zeros_like(upstream)
    products = upstream.astype(F32) * out_ref[...].astype(F32)
    scaled_t = scaled.T
    upstream_t = upstream.T
    logs = log_ref[0].T
    grad_queries = []
    for head in range(2):
        mine = (lane < HD) == (head == 0)
        own_upstream = jnp.where(mine, upstream, nothing)
        row_dot = jnp.sum(jnp.where(mine, products, 0.0), axis=1, keepdims=True)
        log_total = logs[:, head : head + 1]
        heads = slice(head * HD, (head + 1) * HD)
        grad_query = 0.0
        for start in range(0, count, chunk):
            span = slice(start, start + chunk)
            scores = contract(queries[head], keys[head, span, :], 1, 1)
            probs = jnp.exp2(scores * LOG2E - log_total)
            grad_probs = contract(own_upstream, v_ref[span, :], 1, 1)
            grad_scores = (probs * (grad_probs - row_dot)).astype(BF16)
            grad_values_t[heads, span] += contract(
                upstream_t[heads, :], probs.astype(BF16), 1, 0
            )
            grad_keys_t[heads, span] += contract(scaled_t[heads, :], grad_scores, 1, 0)
            grad_query = grad_query + contract(grad_scores, k_ref[span, :], 1, 0)
        grad_queries.append(grad_query)
    grad_query = jnp.where(lane < HD, *grad_queries) * (1.0 / math.sqrt(HD))
    block = grad_query.shape[0]
    grad_ref[0, pl.ds(pl.multiple_of(step * block, block), block), :] = (
        grad_query * cos_row_ref[...] - swap_halves(grad_query) * sin_row_ref[...]
    ).astype(BF16)

    @pl.when(step == pl.num_programs(1) - 1)
    def _():
        grad_key = grad_keys_t[...].T
        grad_ref[1] = (
            grad_key * cos_ref[...] - swap_halves(grad_key) * sin_ref[...]
        ).astype(BF16)
        grad_ref[2] = grad_values_t[...].T.astype(BF16)


def attend_back(
    place, queries, keys, values, mixed, upstream, logs, cosines, sines, pair, grads, block=512, chunk=512
):
    count, columns = queries.shape
    whole = pl.BlockSpec((count, LANES), lambda p, i, _: (0, pair))
    rows = pl.BlockSpec((block, LANES), lambda p, i, _: (i, pair))
    table = pl.BlockSpec((count, LANES), lambda p, i, _: (0, 0))
    table_rows = pl.BlockSpec((block, LANES), lambda p, i, _: (i, 0))
    held = [] if grads is None else [grads]
    return pl.pallas_call(
        functools.partial(attend_back_kernel, chunk=chunk),
        grid_spec=pltpu.PrefetchScalarGridSpec(
            num_scalar_prefetch=1,
            grid=(1, count // block),
            in_specs=[
                rows,
                whole,
                whole,
                rows,
                rows,
                pl.BlockSpec((1, 8, block), lambda p, i, _: (pair, 0, i)),
                table_rows,
                table_rows,
                table,
                table,
            ]
            + [pl.BlockSpec(memory_space=pl.ANY)] * len(held),
            out_specs=pl.BlockSpec((3, count, LANES), lambda p, i, _: (0, 0, pair)),
            scratch_shapes=[
                pltpu.VMEM((2, count, LANES), BF16),
                pltpu.VMEM((LANES, count), F32),
                pltpu.VMEM((LANES, count), F32),
            ],
        ),
        out_shape=jax.ShapeDtypeStruct((3, count, columns), BF16),
        input_output_aliases={11: 0} if held else {},
        cost_estimate=cost(28 * count * count * LANES, 16 * count * LANES, count * count * 2),
        compiler_params=pltpu.CompilerParams(vmem_limit_bytes=60 * MIB),
        name="attention_backward",
    )(place, queries, keys, values, mixed, upstream, logs, cosines, sines, cosines, sines, *held)


def feed_kernel(*refs, counts, chunk):
    row_pieces, target_pieces = refs[: counts[0]], refs[counts[0] : sum(counts)]
    refs = refs[sum(counts) :]
    gate_ref, up_ref, down_ref, inner_ref, grad_gate_ref, grad_up_ref = refs[:6]
    weight_gate_ref, weight_up_ref, weight_down_ref = refs[6:9]
    rows, row_sems, target, target_sems, rows_t, target_t = refs[9:]

    @pl.when(pl.program_id(0) == 0)
    def _():
        copies = fetch(row_pieces, rows, row_sems) + fetch(target_pieces, target, target_sems)
        for copy in copies:
            copy.wait()
        rows_t[...] = rows[...].T
        target_t[...] = target[...].T

    gate_weight, up_weight, down_weight = unpacked(gate_ref), unpacked(up_ref), unpacked(down_ref)
    for start in range(0, rows.shape[0], chunk):
        span = slice(start, start + chunk)
        gate = contract(rows[span, :], gate_weight, 1, 0)
        up = contract(rows[span, :], up_weight, 1, 0)
        grad_inner = contract(target[span, :], down_weight, 1, 1)
        share = jax.nn.sigmoid(gate)
        activated = gate * share
        inner_ref[span, :] = (activated * up).astype(BF16)
        grad_up_ref[span, :] = (grad_inner * activated).astype(BF16)
        grad_gate_ref[span, :] = (
            grad_inner * up * share * (1.0 + gate * (1.0 - share))
        ).astype(BF16)
    weight_gate_ref[...] = contract(rows_t[...], grad_gate_ref[...], 1, 0).astype(BF16)
    weight_up_ref[...] = contract(rows_t[...], grad_up_ref[...], 1, 0).astype(BF16)
    weight_down_ref[...] = contract(target_t[...], inner_ref[...], 1, 0).T.astype(BF16)


def feed(rows, target, weights, block=256, chunk=512):
    count = sum(piece.shape[0] for piece in rows)
    width = rows[0].shape[1]
    across_spec = lambda units: pl.BlockSpec((width, min(block, units)), lambda i: (0, i))
    down_spec = lambda units: pl.BlockSpec((min(block, units), width), lambda i: (i, 0))
    if packed(weights[0]):
        units = width
        replicas, deep = weights[0][0].shape[0], width // weights[0][0].shape[0]
        specs = [
            pl.BlockSpec((replicas, deep, block), lambda i, plane=weights[k][1]: (0, plane, i))
            for k in range(2)
        ] + [
            pl.BlockSpec(
                (block // deep, deep, width), lambda i, plane=weights[2][1]: (i, plane, 0)
            )
        ]
        weights = [weight for weight, _ in weights]
    else:
        units = weights[0].shape[1]
        specs = [across_spec(units)] * 2 + [down_spec(units)]
    block = min(block, units)
    out = pl.BlockSpec((count, block), lambda i: (0, i))
    return pl.pallas_call(
        functools.partial(feed_kernel, counts=(len(rows), len(target)), chunk=chunk),
        grid=(units // block,),
        in_specs=[pl.BlockSpec(memory_space=pl.ANY)] * (len(rows) + len(target)) + specs,
        out_specs=[out, out, out] + [across_spec(units)] * 2 + [down_spec(units)],
        out_shape=[jax.ShapeDtypeStruct((count, units), BF16)] * 3
        + [jax.ShapeDtypeStruct((width, units), BF16)] * 2
        + [jax.ShapeDtypeStruct((units, width), BF16)],
        scratch_shapes=room(rows) + room(target) + [pltpu.VMEM((width, count), BF16)] * 2,
        cost_estimate=cost(
            12 * count * width * units,
            4 * count * width + 12 * width * units + 6 * count * units,
            2 * count * units,
        ),
        compiler_params=pltpu.CompilerParams(vmem_limit_bytes=60 * MIB),
        name="feed_forward",
    )(*rows, *target, *weights)


def sum_kernel(*refs, dims):
    total = 0.0
    for index, dim in enumerate(dims):
        total = total + contract(refs[2 * index][...], unpacked(refs[2 * index + 1]), 1, dim)
    refs[-1][...] = total.astype(refs[-1].dtype)


def sum_products(terms, start, rows, dtype=F32, block=512):
    block = min(block, rows)
    first = start // block
    operands, specs, dims, flops, moved = [], [], [], 0, 0
    for left, plane, right, part, dim in terms:
        depth = left.shape[-1]
        if plane is None:
            specs.append(pl.BlockSpec((block, depth), lambda i: (first + i, 0)))
        else:
            specs.append(
                pl.BlockSpec((None, block, depth), lambda i, plane=plane: (plane, first + i, 0))
            )
        if packed(right):
            right, plane = right
            replicas, deep = right.shape[0], right.shape[2] // right.shape[0]
            shape = (right.shape[2], right.shape[2])
            specs.append(
                pl.BlockSpec(
                    (replicas, deep, right.shape[2]), lambda i, plane=plane: (0, plane, 0)
                )
            )
        else:
            shape = right.shape if part is None else (right.shape[0], depth)
            column = 0 if part is None else part
            specs.append(pl.BlockSpec(shape, lambda i, column=column: (0, column)))
        operands += [left, right]
        dims.append(dim)
        width = shape[1 - dim]
        flops += 2 * rows * depth * width
        moved += 2 * rows * depth + 2 * depth * width
    return pl.pallas_call(
        functools.partial(sum_kernel, dims=tuple(dims)),
        grid=(rows // block,),
        in_specs=specs,
        out_specs=pl.BlockSpec((block, width), lambda i: (i, 0)),
        out_shape=jax.ShapeDtypeStruct((rows, width), dtype),
        cost_estimate=cost(flops, moved + 4 * rows * width),
        compiler_params=pltpu.CompilerParams(vmem_limit_bytes=58 * MIB),
        name="sum_products",
    )(*operands)


def outer_kernel(*refs, count):
    right_ref, out_ref, left, sems, left_t = refs[count:]

    @pl.when(pl.program_id(0) == 0)
    def _():
        for copy in fetch(refs[:count], left, sems):
            copy.wait()
        left_t[...] = left[...].T

    out_ref[...] = contract(left_t[...], right_ref[...], 1, 0).astype(BF16)


def outer(pieces, right):
    width = pieces[0].shape[1]
    planes, count, columns = right.shape
    return pl.pallas_call(
        functools.partial(outer_kernel, count=len(pieces)),
        grid=(planes,),
        in_specs=[pl.BlockSpec(memory_space=pl.ANY)] * len(pieces)
        + [pl.BlockSpec((None, count, columns), lambda i: (i, 0, 0))],
        out_specs=pl.BlockSpec((width, columns), lambda i: (0, i)),
        out_shape=jax.ShapeDtypeStruct((width, planes * columns), BF16),
        scratch_shapes=room(pieces) + [pltpu.VMEM((width, count), BF16)],
        cost_estimate=cost(
            2 * count * width * planes * columns,
            2 * count * (width + planes * columns) + 2 * width * planes * columns,
        ),
        compiler_params=pltpu.CompilerParams(vmem_limit_bytes=40 * MIB),
        name="outer_product",
    )(*pieces, right)


def branch_kernel(*refs, count, groups, chunk):
    weights = refs[count : count + groups]
    mixed = refs[count + groups : count + 2 * groups]
    outs = refs[count + 2 * groups : count + 4 * groups]
    rows, sems = refs[count + 4 * groups :]
    for copy in fetch(refs[:count], rows, sems):
        copy.wait()
    for index in range(groups):
        outs[groups + index][...] = contract(mixed[index][...].T, rows[...], 1, 0).astype(BF16)
        for start in range(0, rows.shape[0], chunk):
            span = slice(start, start + chunk)
            outs[index][span, :] = contract(rows[span, :], weights[index][...], 1, 1).astype(BF16)


def branch_back(pieces, weights, mixed, chunk=512):
    count = sum(piece.shape[0] for piece in pieces)
    width = pieces[0].shape[1]
    groups = len(weights)
    vmem = pl.BlockSpec(memory_space=pltpu.VMEM)
    columns = [weight.shape[0] for weight in weights]
    results = pl.pallas_call(
        functools.partial(branch_kernel, count=len(pieces), groups=groups, chunk=chunk),
        in_specs=[pl.BlockSpec(memory_space=pl.ANY)] * len(pieces) + [vmem] * (2 * groups),
        out_specs=[vmem] * (2 * groups),
        out_shape=[jax.ShapeDtypeStruct((count, size), BF16) for size in columns]
        + [jax.ShapeDtypeStruct((size, width), BF16) for size in columns],
        scratch_shapes=room(pieces),
        cost_estimate=cost(4 * count * width * sum(columns), 6 * count * width),
        compiler_params=pltpu.CompilerParams(vmem_limit_bytes=48 * MIB),
        name="branch_backward",
    )(*pieces, *weights, *mixed)
    return results[:groups], results[groups:]


def standardize(value):
    centred = value - jnp.mean(value, axis=-1, keepdims=True)
    scale = lax.rsqrt(jnp.mean(centred * centred, axis=-1, keepdims=True) + EPSILON)
    return centred * scale, scale


def norm_kernel(*refs, added):
    value = refs[0][...].astype(F32)
    for ref in refs[1 : 1 + added]:
        value = value + ref[...].astype(F32)
    gain_ref, shift_ref = refs[1 + added : 3 + added]
    standard, _ = standardize(value)
    if added:
        refs[-2][...] = value
    refs[-1][...] = (standard * gain_ref[...] + shift_ref[...]).astype(BF16)


def norm(base, terms, gain, shift, pieces=PIECES, block=256):
    count, width = base.shape
    rows = count // pieces
    block = min(block, rows)
    vector = pl.BlockSpec((1, width), lambda i: (0, 0))
    total, out = None, []
    for piece in range(pieces):
        first = piece * rows // block
        whole = pl.BlockSpec((block, width), lambda i, first=first: (first + i, 0))
        shapes = [jax.ShapeDtypeStruct((rows, width), BF16)]
        specs = [pl.BlockSpec((block, width), lambda i: (i, 0))]
        held = []
        if terms:
            shapes = [jax.ShapeDtypeStruct((count, width), F32)] + shapes
            specs = [whole] + specs
            held = [] if total is None else [total]
        results = pl.pallas_call(
            lambda *refs, held=len(held): norm_kernel(
                *refs[: 3 + len(terms)], *refs[3 + len(terms) + held :], added=len(terms)
            ),
            grid=(rows // block,),
            in_specs=[whole] * (1 + len(terms))
            + [vector, vector]
            + [pl.BlockSpec(memory_space=pl.ANY)] * len(held),
            out_specs=specs,
            out_shape=shapes,
            input_output_aliases={3 + len(terms): 0} if held else {},
            cost_estimate=cost(16 * rows * width, 8 * rows * width * len(shapes)),
            name="layer_norm",
        )(base, *terms, gain.reshape(1, width), shift.reshape(1, width), *held)
        out.append(results[-1])
        if terms:
            total = results[0]
    return total, out


def norm_back_kernel(*refs, added, low):
    base_ref, straight_ref, gain_ref = refs[:3]
    upstream = refs[3][...].astype(F32)
    for ref in refs[4 : 3 + added]:
        upstream = upstream + ref[...].astype(F32)
    outs = refs[3 + added :]
    standard, scale = standardize(base_ref[...].astype(F32))
    scaled = upstream * gain_ref[...]
    back = straight_ref[...].astype(F32) + scale * (
        scaled
        - jnp.mean(scaled, axis=-1, keepdims=True)
        - standard * jnp.mean(scaled * standard, axis=-1, keepdims=True)
    )
    outs[0][...] = back.astype(BF16)
    if not low:
        outs[1][...] = back
    sums = jnp.concatenate(
        [
            jnp.sum(upstream * standard, axis=0, keepdims=True),
            jnp.sum(upstream, axis=0, keepdims=True),
        ],
        axis=0,
    )

    @pl.when(pl.program_id(0) == 0)
    def _():
        outs[-1][...] = sums

    @pl.when(pl.program_id(0) > 0)
    def _():
        outs[-1][...] += sums


def norm_back(base, straight, gain, terms, low, pieces=PIECES, block=256):
    count, width = base.shape
    rows = count // pieces
    block = min(block, rows)
    total, out, found = None, [], []
    for piece in range(pieces):
        first = piece * rows // block
        whole = pl.BlockSpec((block, width), lambda i, first=first: (first + i, 0))
        shapes = [jax.ShapeDtypeStruct((rows, width), BF16)]
        specs = [pl.BlockSpec((block, width), lambda i: (i, 0))]
        held = []
        if not low:
            shapes.append(jax.ShapeDtypeStruct((count, width), F32))
            specs.append(whole)
            held = [] if total is None else [total]
        results = pl.pallas_call(
            lambda *refs, held=len(held): norm_back_kernel(
                *refs[: 3 + len(terms)],
                *refs[3 + len(terms) + held :],
                added=len(terms),
                low=low,
            ),
            grid=(rows // block,),
            in_specs=[whole, whole, pl.BlockSpec((1, width), lambda i: (0, 0))]
            + [whole] * len(terms)
            + [pl.BlockSpec(memory_space=pl.ANY)] * len(held),
            out_specs=specs + [pl.BlockSpec((2, width), lambda i: (0, 0))],
            out_shape=shapes + [jax.ShapeDtypeStruct((2, width), F32)],
            input_output_aliases={3 + len(terms): 1} if held else {},
            cost_estimate=cost(30 * rows * width, 16 * rows * width),
            name="layer_norm_backward",
        )(base, straight, gain.reshape(1, width), *terms, *held)
        out.append(results[0])
        found.append(results[-1])
        if not low:
            total = results[1]
    return out, total, sum(found)


def rope_tables(offset):
    position = (jnp.arange(LEN, dtype=jnp.int32) + offset) % LEN
    inverse = 10000.0 ** (-2.0 * jnp.arange(HD // 2, dtype=F32) / HD)
    angles = position.astype(F32)[:, None] * inverse[None, :]
    cosines, sines = jnp.cos(angles), jnp.sin(angles)
    return (
        jnp.concatenate([cosines] * 4, axis=1),
        jnp.concatenate([-sines, sines, -sines, sines], axis=1),
    )


def exchanges(axis, size):
    if size & (size - 1):
        return [lambda value: lax.psum(value, axis)]
    return [
        lambda value, pairs=[(i, i ^ (1 << bit)) for i in range(size)]: value
        + lax.ppermute(value, axis, pairs)
        for bit in range(size.bit_length() - 1)
    ]


def shards(
    dp_size,
    tensor_size,
    tokens,
    lengths,
    gain_first,
    shift_first,
    query_weight,
    key_weight,
    value_weight,
    output_weight,
    gain_second,
    shift_second,
    gate_weight,
    up_weight,
    down_weight,
    cotangent,
):
    windows = lengths.shape[0]
    span = tensor_size // windows
    held = tokens.shape[0]
    width = tokens.shape[1]
    head_cols = query_weight.shape[1]
    here = lax.axis_index("tensor")
    window, seat = here // span, here % span

    def from_seat(value, shift):
        pairs = [
            (w * span + (s + shift) % span, w * span + s)
            for w in range(windows)
            for s in range(span)
        ]
        return lax.ppermute(value, "tensor", pairs)

    def to_seat(value, shift):
        return from_seat(value, span - shift)

    def from_window(value, shift):
        pairs = [((t + shift * span) % tensor_size, t) for t in range(tensor_size)]
        return lax.ppermute(value, "tensor", pairs)

    def to_window(value, shift):
        return from_window(value, windows - shift)

    def gather_rows(value):
        return value + [from_seat(piece, s) for s in range(1, span) for piece in value]

    def scatter(partial):
        sent = [to_seat(partial(s * held, held), s) for s in range(1, span)]
        return [partial(0, held)] + sent

    def all_windows(value):
        return [value] + [from_window(value, shift) for shift in range(1, windows)]

    def spread_windows(values):
        group = lax.axis_index("dp")
        sizes = [value.shape[0] // dp_size for value in values]
        mine = jnp.concatenate(
            [
                lax.dynamic_slice_in_dim(value, group * size, size, axis=0).reshape(-1, width)
                for value, size in zip(values, sizes)
            ],
            axis=0,
        )
        return [mine], [from_window(mine, shift) for shift in range(1, windows)]

    def gather_spread(values, piece):
        gathered = lax.all_gather(piece, "dp", axis=0)
        if all(value.shape == (width, width) for value in values):
            return [(gathered, plane) for plane in range(len(values))]
        out, start = [], 0
        for value in values:
            count = value.size // width // dp_size
            out.append(gathered[:, start : start + count].reshape(value.shape))
            start += count
        return out

    def after(value, *others):
        return lax.optimization_barrier((value, *others))[0]

    def pieces_after(pieces, *others):
        return [after(pieces[0], *others)] + pieces[1:]

    place = jnp.stack(
        [lax.dynamic_index_in_dim(lengths, window, keepdims=False), seat * held]
    ).astype(jnp.int32)
    cosines, sines = rope_tables(seat * held)

    members = [[s] for s in range(windows)] if head_cols % LANES == 0 else [list(range(windows))]
    feed_weights = [gate_weight, up_weight, down_weight]
    slices_sent, slices = spread_windows(feed_weights)
    _, normed_one = norm(after(tokens, *slices_sent), [], gain_first, shift_first)
    full_one = gather_rows(normed_one)
    qkv_own = jnp.concatenate([query_weight, key_weight, value_weight], axis=1)
    qkv_other = all_windows(after(qkv_own, *slices))[1:]
    qkv_shards = [qkv_own] + qkv_other
    def joined(parts, axis):
        return parts[0] if len(parts) == 1 else jnp.concatenate(parts, axis=axis)

    def part_of(value, part):
        return value[:, part * head_cols : (part + 1) * head_cols]

    qkv_weights = [
        qkv_shards[group[0]]
        if len(group) == 1
        else joined([part_of(qkv_shards[s], part) for part in range(3) for s in group], 1)
        for group in members
    ]
    target = gather_rows([cotangent])
    qkv, attended = [], []
    rows_one = full_one
    for weight in qkv_weights:
        parts = project(rows_one, weight, cosines, sines)
        if not qkv:
            slices = [after(piece, parts[0]) for piece in slices]
            feed_shards = [feed_weights]
            feed_shards += [gather_spread(feed_weights, piece) for piece in slices]
        waits = slices if not qkv else target
        qkv.append((after(parts[0], *waits), *parts[1:]))
        attended.append(attend(place, *qkv[-1]))
        if len(attended) == 1:
            sent = after(output_weight, attended[0][0])
            output_shards = [output_weight] + all_windows(sent)[1:]
        rows_one = pieces_after(full_one, attended[-1][0])

    out_weights = [joined([output_shards[s] for s in group], 0) for group in members]
    mixer_terms = [
        (mixed, None, weight, None, 0) for (mixed, _), weight in zip(attended, out_weights)
    ]
    hidden_one, normed_two = norm(
        tokens,
        scatter(lambda start, rows: sum_products(mixer_terms, start, rows)),
        gain_second,
        shift_second,
    )
    full_two = gather_rows(normed_two)

    flip = [(d, d ^ 1) for d in range(dp_size)]
    odd = lax.axis_index("dp") % 2

    def half(value, which):
        count = value.shape[0] // 2
        return lax.dynamic_slice_in_dim(value, which * count, count, axis=0)

    def total(pieces, which):
        return sum(half(piece, which).astype(F32) for piece in pieces).astype(BF16)

    def swap_half(pieces, *others):
        pieces = [after(piece, *others) for piece in pieces]
        mine, sent = total(pieces, odd), total(pieces, 1 - odd)
        return (mine, lax.ppermute(sent, "dp", flip)), [mine, sent]

    def add_half(halves, *others):
        mine, received = (after(value, *others) for value in halves)
        return (mine.astype(F32) + received.astype(F32)).astype(BF16)

    def sum_half(value, turn):
        groups = [list(range(0, dp_size, 2)), list(range(1, dp_size, 2))]
        if turn & 1:
            groups = groups[::-1]
        if turn & 2:
            groups = [group[::-1] for group in groups]
        return lax.psum(value, "dp", axis_index_groups=groups)

    def swap_sum(mine, *others):
        mine = after(mine, *others)
        return mine, lax.ppermute(mine, "dp", flip)

    def whole_sum(halves, *others):
        mine, received = (after(value, *others) for value in halves)
        first, second = jnp.where(odd == 0, mine, received), jnp.where(odd == 0, received, mine)
        return jnp.concatenate([first, second], axis=0).astype(F32)

    def send_to_owner(parts):
        return [to_window(parts[shift], shift) for shift in range(1, windows)]

    order = list(range(1, windows)) + [0]
    fed = {}
    rows_two = full_two
    for s in order:
        fed[s] = feed(rows_two, target, feed_shards[s])
        rows_two = pieces_after(full_two, fed[s][0])
    down_pieces, up_pieces, gate_pieces = (
        send_to_owner({s: fed[s][k] for s in order}) + [fed[0][k]] for k in (5, 4, 3)
    )
    two_terms, feed_terms = [], []
    for s in order:
        gate, up, down = feed_shards[s]
        two_terms += [(fed[s][1], None, gate, None, 1), (fed[s][2], None, up, None, 1)]
        feed_terms.append((fed[s][0], None, down, None, 0))

    two_sent = [
        sum_products(two_terms, shift * held, held, BF16) for shift in range(1, span)
    ]
    down_half, marks = swap_half(down_pieces, *two_sent)
    two_terms = [(after(two_terms[0][0], *marks), *two_terms[0][1:])] + two_terms[1:]
    two_kept = sum_products(two_terms, 0, held)
    grad_branch_own, grad_hidden, norm_two = norm_back(
        hidden_one,
        cotangent,
        gain_second,
        [two_kept] + [to_seat(part, shift + 1) for shift, part in enumerate(two_sent)],
        False,
    )
    grad_branch = gather_rows(grad_branch_own)
    down_half = add_half(down_half, *grad_branch_own)
    down_sum = sum_half(down_half, 0)
    grad_branch = pieces_after(grad_branch, down_half)

    members = members[::-1]
    out_weights, qkv_weights = out_weights[::-1], qkv_weights[::-1]
    qkv, attended = qkv[::-1], attended[::-1]
    grad_mixed, found = branch_back(grad_branch, out_weights, [mixed for mixed, _ in attended])
    out_grads = {
        s: out_grad[spot * head_cols : (spot + 1) * head_cols]
        for group, out_grad in zip(members, found)
        for spot, s in enumerate(group)
    }
    out_pieces = send_to_owner(out_grads) + [out_grads[0]]

    def up_swap(last):
        sums["up"], waits = swap_half(up_pieces, *last)
        return waits

    def up_sum(last):
        value = add_half(sums["up"], *last)
        sums["up"] = sum_half(value, 1)
        sums["down"] = swap_sum(down_sum, *last)
        return [value, sums["down"][0]]

    def gate_swap(last):
        sums["gate"], waits = swap_half(gate_pieces, *last)
        sums["out"], more = swap_half(out_pieces, *last)
        sums["down"] = whole_sum(sums["down"], *last)
        return waits + more + [sums["down"]]

    def gate_sum(last):
        values = [add_half(sums["gate"], *last), add_half(sums["out"], *last)]
        sums["gate"], sums["out"] = sum_half(tuple(values), 2)
        sums["up"] = swap_sum(sums["up"], *last)
        return values + [sums["up"][0]]

    across, along = (exchanges(axis, size) for axis, size in (("tensor", tensor_size), ("dp", dp_size)))
    norm_steps = across + along[1:]
    sums = {}
    moves = [up_swap, up_sum, gate_swap, gate_sum]
    last = list(grad_mixed)
    grad_qkv, qkv_grads = [], {}
    for index, group in enumerate(members):
        mixed, logs = attended[index]
        count = len(group) * head_cols
        grads = None
        for pair in range(count // LANES):
            waits = moves.pop(0)(last) if moves else last
            if norm_steps:
                norm_two = norm_steps.pop(0)(after(norm_two, *last))
                waits = waits + [norm_two]
            grads = attend_back(
                place,
                *qkv[index],
                mixed,
                after(grad_mixed[index], *waits),
                logs,
                cosines,
                sines,
                pair,
                grads,
            )
            last = [grads]
        grad_qkv.append(grads)
        qkv_grad = outer(full_one, grads)
        last = [qkv_grad]
        for spot, s in enumerate(group):
            if len(group) == 1:
                qkv_grads[s] = qkv_grad
            else:
                qkv_grads[s] = joined(
                    [
                        lax.slice_in_dim(
                            qkv_grad,
                            part * count + spot * head_cols,
                            part * count + (spot + 1) * head_cols,
                            axis=1,
                        )
                        for part in range(3)
                    ],
                    1,
                )
    for move in moves:
        last = move(last)

    qkv_half, marks = swap_half(send_to_owner(qkv_grads) + [qkv_grads[0]])
    grad_down = sums["down"]
    grad_up = whole_sum(sums["up"], *marks)
    feed_terms[0] = (after(feed_terms[0][0], grad_up), *feed_terms[0][1:])
    feed_sent = [sum_products(feed_terms, shift * held, held, BF16) for shift in range(1, span)]
    feed_terms[0] = (after(feed_terms[0][0], *feed_sent), *feed_terms[0][1:])
    feed_parts = [sum_products(feed_terms, 0, held)]
    feed_parts += [to_seat(part, shift + 1) for shift, part in enumerate(feed_sent)]
    qkv_half = add_half(qkv_half, sums["gate"], feed_parts[0])
    qkv_sum = sum_half(qkv_half, 3)
    gate_halves = swap_sum(sums["gate"], qkv_half)
    out_halves = swap_sum(sums["out"], qkv_half)
    one_terms = [
        (grad_qkv[index], part, weight, part, 1)
        for index, weight in enumerate(qkv_weights)
        for part in range(3)
    ]
    one_terms[0] = (after(one_terms[0][0], qkv_half), *one_terms[0][1:])
    one_parts = scatter(
        lambda start, rows: sum_products(one_terms, start, rows, BF16 if start else F32)
    )
    output = (hidden_one + sum(feed_parts)).astype(BF16)
    qkv_halves = swap_sum(qkv_sum, one_parts[0], output)
    one_parts[0] = after(one_parts[0], qkv_halves[0])
    (input_grad,), _, norm_one = norm_back(tokens, grad_hidden, gain_first, one_parts, True, 1)
    grad_gate = whole_sum(gate_halves, qkv_halves[0])
    out_grad = whole_sum(out_halves, qkv_halves[0])
    qkv_grad = whole_sum(qkv_halves, input_grad)

    for step in across + along[1:]:
        norm_one = step(norm_one)
    for step in norm_steps:
        norm_two = step(norm_two)
    norms = along[0](jnp.concatenate([norm_one, norm_two], axis=0))
    qkv_grad = whole_sum(swap_sum(qkv_sum, input_grad))

    return (
        output,
        input_grad,
        *(part_of(qkv_grad, part) for part in range(3)),
        out_grad,
        grad_gate,
        grad_up,
        grad_down,
        norms[0],
        norms[1],
        norms[2],
        norms[3],
    )


def solution(mesh):
    rows = P(("dp", "tensor"), None)
    columns = P(None, "tensor")
    depth = P("tensor", None)
    return jax.shard_map(
        functools.partial(shards, mesh.shape["dp"], mesh.shape["tensor"]),
        mesh=mesh,
        in_specs=(
            rows,
            P("dp"),
            P(),
            P(),
            columns,
            columns,
            columns,
            depth,
            P(),
            P(),
            columns,
            columns,
            depth,
            rows,
        ),
        out_specs=(
            rows,
            rows,
            columns,
            columns,
            columns,
            depth,
            columns,
            columns,
            depth,
            P(),
            P(),
            P(),
            P(),
        ),
        check_vma=False,
    )
```

```python
import functools
import math

import jax
import jax.numpy as jnp
from jax import lax
from jax.experimental import pallas as pl
from jax.experimental.pallas import tpu as pltpu
from jax.sharding import PartitionSpec as P

HD = 64
LEN = 2048
EPSILON = 1e-05
MASKED = -1e30
LANES = 128
LOG2E = math.log2(math.e)
BF16 = jnp.bfloat16
F32 = jnp.float32
MIB = 1 << 20
COST_SHARE = 0.1
PIECES = 2


def contract(left, right, left_dim, right_dim):
    return lax.dot_general(
        left, right, (((left_dim,), (right_dim,)), ((), ())), preferred_element_type=F32
    )


def cost(flops, moved, transcendentals=0):
    return pl.CostEstimate(
        flops=int(flops * COST_SHARE),
        bytes_accessed=int(moved * COST_SHARE),
        transcendentals=int(transcendentals * COST_SHARE),
    )


def swap_halves(value):
    columns = value.shape[1]
    lane = lax.broadcasted_iota(jnp.int32, value.shape, 1)
    return jnp.where(
        lane % HD < HD // 2,
        pltpu.roll(value, columns - HD // 2, 1),
        pltpu.roll(value, HD // 2, 1),
    )


def fetch(pieces, rows, sems):
    copies, start = [], 0
    for index, piece in enumerate(pieces):
        count = piece.shape[0]
        copies.append(
            pltpu.make_async_copy(piece, rows.at[pl.ds(start, count), :], sems.at[index])
        )
        start += count
    for copy in copies:
        copy.start()
    return copies


def room(pieces):
    count = sum(piece.shape[0] for piece in pieces)
    return [
        pltpu.VMEM((count, pieces[0].shape[1]), BF16),
        pltpu.SemaphoreType.DMA((len(pieces),)),
    ]


def unpacked(ref):
    value = ref[...]
    return value.reshape(-1, value.shape[-1]) if value.ndim == 3 else value


def packed(weight):
    return isinstance(weight, tuple)


def project_kernel(*refs, count):
    pieces = refs[:count]
    weight_ref, cos_ref, sin_ref, q_ref, k_ref, v_ref, rows, sems = refs[count:]
    columns = q_ref.shape[1]
    block = q_ref.shape[0]

    @pl.when(pl.program_id(0) == 0)
    def _():
        for copy in fetch(pieces, rows, sems):
            copy.wait()

    start = pl.multiple_of(pl.program_id(0) * block, block)
    product = contract(rows[pl.ds(start, block), :], weight_ref[...], 1, 0)
    cosines = jnp.concatenate([cos_ref[...]] * (columns // LANES), axis=1)
    sines = jnp.concatenate([sin_ref[...]] * (columns // LANES), axis=1)
    for part, out_ref in ((0, q_ref), (1, k_ref)):
        value = product[:, part * columns : (part + 1) * columns]
        out_ref[...] = (value * cosines + swap_halves(value) * sines).astype(BF16)
    v_ref[...] = product[:, 2 * columns :].astype(BF16)


def project(pieces, weight, cosines, sines, block=512):
    width = weight.shape[0]
    columns = weight.shape[1] // 3
    count = sum(piece.shape[0] for piece in pieces)
    table = pl.BlockSpec((block, LANES), lambda i: (i, 0))
    out = pl.BlockSpec((block, columns), lambda i: (i, 0))
    return pl.pallas_call(
        functools.partial(project_kernel, count=len(pieces)),
        grid=(count // block,),
        in_specs=[pl.BlockSpec(memory_space=pl.ANY)] * len(pieces)
        + [pl.BlockSpec(weight.shape, lambda i: (0, 0)), table, table],
        out_specs=[out, out, out],
        out_shape=[jax.ShapeDtypeStruct((count, columns), BF16)] * 3,
        scratch_shapes=room(pieces),
        cost_estimate=cost(
            2 * count * width * 3 * columns,
            2 * (count * width + width * 3 * columns + count * 3 * columns),
        ),
        compiler_params=pltpu.CompilerParams(vmem_limit_bytes=40 * MIB),
        name="project_rope",
    )(*pieces, weight, cosines, sines)


def masked_keys(place_ref, key_ref, masked_ref):
    count = key_ref.shape[0]
    lane = lax.broadcasted_iota(jnp.int32, (count, LANES), 1)
    row = lax.broadcasted_iota(jnp.int32, (count, LANES), 0) + place_ref[1]
    position = jnp.where(row >= count, row - count, row)
    bias = jnp.where(position >= place_ref[0], MASKED, 0.0).astype(BF16)
    nothing = jnp.zeros_like(bias)
    key = key_ref[...]
    masked_ref[0] = jnp.where(lane < HD, key, jnp.where(lane == HD, bias, nothing))
    masked_ref[1] = jnp.where(lane >= HD, key, jnp.where(lane == 0, bias, nothing))


def masked_queries(query):
    lane = lax.broadcasted_iota(jnp.int32, query.shape, 1)
    scaled = query * jnp.asarray(1.0 / math.sqrt(HD), BF16)
    one = jnp.ones_like(query)
    nothing = jnp.zeros_like(query)
    return (
        scaled,
        jnp.where(lane < HD, scaled, jnp.where(lane == HD, one, nothing)),
        jnp.where(lane >= HD, scaled, jnp.where(lane == 0, one, nothing)),
    )


def attend_kernel(place_ref, q_ref, k_ref, v_ref, out_ref, log_ref, keys, values_t, *, chunk):
    count = k_ref.shape[0]

    @pl.when(pl.program_id(1) == 0)
    def _():
        masked_keys(place_ref, k_ref, keys)
        values_t[...] = v_ref[...].T

    queries = masked_queries(q_ref[...])[1:]
    mixed, logs = [], []
    for head in range(2):
        scores = [
            contract(keys[head, start : start + chunk, :], queries[head], 1, 1)
            for start in range(0, count, chunk)
        ]
        top = functools.reduce(
            jnp.maximum, [jnp.max(block, axis=0, keepdims=True) for block in scores]
        )
        total = 0.0
        summed = 0.0
        for index, block in enumerate(scores):
            weights = jnp.exp2((block - top) * LOG2E)
            total = total + jnp.sum(weights, axis=0, keepdims=True)
            value = values_t[
                head * HD : (head + 1) * HD, index * chunk : (index + 1) * chunk
            ]
            summed = summed + contract(value, weights.astype(BF16), 1, 0)
        mixed.append(summed / total)
        logs.append(top * LOG2E + jnp.log2(total))
    out_ref[...] = jnp.concatenate(mixed, axis=0).T.astype(BF16)
    log_ref[0] = jnp.concatenate(logs + [jnp.zeros((6, q_ref.shape[0]), F32)], axis=0)


def attend(place, queries, keys, values, block=1024, chunk=512):
    count, columns = queries.shape
    pairs = columns // LANES
    whole = pl.BlockSpec((count, LANES), lambda p, i, _: (0, p))
    rows = pl.BlockSpec((block, LANES), lambda p, i, _: (i, p))
    return pl.pallas_call(
        functools.partial(attend_kernel, chunk=chunk),
        grid_spec=pltpu.PrefetchScalarGridSpec(
            num_scalar_prefetch=1,
            grid=(pairs, count // block),
            in_specs=[rows, whole, whole],
            out_specs=[rows, pl.BlockSpec((1, 8, block), lambda p, i, _: (p, 0, i))],
            scratch_shapes=[
                pltpu.VMEM((2, count, LANES), BF16),
                pltpu.VMEM((LANES, count), BF16),
            ],
        ),
        out_shape=[
            jax.ShapeDtypeStruct((count, columns), BF16),
            jax.ShapeDtypeStruct((pairs, 8, count), F32),
        ],
        cost_estimate=cost(16 * count * count * columns, 8 * count * columns, count * count * columns // HD),
        compiler_params=pltpu.CompilerParams(vmem_limit_bytes=56 * MIB),
        name="attention_forward",
    )(place, queries, keys, values)


def attend_back_kernel(
    place_ref,
    q_ref,
    k_ref,
    v_ref,
    out_ref,
    up_ref,
    log_ref,
    cos_row_ref,
    sin_row_ref,
    cos_ref,
    sin_ref,
    *rest,
    chunk,
):
    grad_ref, keys, grad_keys_t, grad_values_t = rest[-4:]
    count = k_ref.shape[0]
    step = pl.program_id(1)

    @pl.when(step == 0)
    def _():
        masked_keys(place_ref, k_ref, keys)
        grad_keys_t[...] = jnp.zeros_like(grad_keys_t)
        grad_values_t[...] = jnp.zeros_like(grad_values_t)

    scaled, *queries = masked_queries(q_ref[...])
    upstream = up_ref[...]
    lane = lax.broadcasted_iota(jnp.int32, upstream.shape, 1)
    nothing = jnp.zeros_like(upstream)
    products = upstream.astype(F32) * out_ref[...].astype(F32)
    scaled_t = scaled.T
    upstream_t = upstream.T
    logs = log_ref[0].T
    grad_queries = []
    for head in range(2):
        mine = (lane < HD) == (head == 0)
        own_upstream = jnp.where(mine, upstream, nothing)
        row_dot = jnp.sum(jnp.where(mine, products, 0.0), axis=1, keepdims=True)
        log_total = logs[:, head : head + 1]
        heads = slice(head * HD, (head + 1) * HD)
        grad_query = 0.0
        for start in range(0, count, chunk):
            span = slice(start, start + chunk)
            scores = contract(queries[head], keys[head, span, :], 1, 1)
            probs = jnp.exp2(scores * LOG2E - log_total)
            grad_probs = contract(own_upstream, v_ref[span, :], 1, 1)
            grad_scores = (probs * (grad_probs - row_dot)).astype(BF16)
            grad_values_t[heads, span] += contract(
                upstream_t[heads, :], probs.astype(BF16), 1, 0
            )
            grad_keys_t[heads, span] += contract(scaled_t[heads, :], grad_scores, 1, 0)
            grad_query = grad_query + contract(grad_scores, k_ref[span, :], 1, 0)
        grad_queries.append(grad_query)
    grad_query = jnp.where(lane < HD, *grad_queries) * (1.0 / math.sqrt(HD))
    block = grad_query.shape[0]
    grad_ref[0, pl.ds(pl.multiple_of(step * block, block), block), :] = (
        grad_query * cos_row_ref[...] - swap_halves(grad_query) * sin_row_ref[...]
    ).astype(BF16)

    @pl.when(step == pl.num_programs(1) - 1)
    def _():
        grad_key = grad_keys_t[...].T
        grad_ref[1] = (
            grad_key * cos_ref[...] - swap_halves(grad_key) * sin_ref[...]
        ).astype(BF16)
        grad_ref[2] = grad_values_t[...].T.astype(BF16)


def attend_back(
    place, queries, keys, values, mixed, upstream, logs, cosines, sines, pair, grads, block=512, chunk=512
):
    count, columns = queries.shape
    whole = pl.BlockSpec((count, LANES), lambda p, i, _: (0, pair))
    rows = pl.BlockSpec((block, LANES), lambda p, i, _: (i, pair))
    table = pl.BlockSpec((count, LANES), lambda p, i, _: (0, 0))
    table_rows = pl.BlockSpec((block, LANES), lambda p, i, _: (i, 0))
    held = [] if grads is None else [grads]
    return pl.pallas_call(
        functools.partial(attend_back_kernel, chunk=chunk),
        grid_spec=pltpu.PrefetchScalarGridSpec(
            num_scalar_prefetch=1,
            grid=(1, count // block),
            in_specs=[
                rows,
                whole,
                whole,
                rows,
                rows,
                pl.BlockSpec((1, 8, block), lambda p, i, _: (pair, 0, i)),
                table_rows,
                table_rows,
                table,
                table,
            ]
            + [pl.BlockSpec(memory_space=pl.ANY)] * len(held),
            out_specs=pl.BlockSpec((3, count, LANES), lambda p, i, _: (0, 0, pair)),
            scratch_shapes=[
                pltpu.VMEM((2, count, LANES), BF16),
                pltpu.VMEM((LANES, count), F32),
                pltpu.VMEM((LANES, count), F32),
            ],
        ),
        out_shape=jax.ShapeDtypeStruct((3, count, columns), BF16),
        input_output_aliases={11: 0} if held else {},
        cost_estimate=cost(28 * count * count * LANES, 16 * count * LANES, count * count * 2),
        compiler_params=pltpu.CompilerParams(vmem_limit_bytes=60 * MIB),
        name="attention_backward",
    )(place, queries, keys, values, mixed, upstream, logs, cosines, sines, cosines, sines, *held)


def feed_kernel(*refs, counts, chunk):
    row_pieces, target_pieces = refs[: counts[0]], refs[counts[0] : sum(counts)]
    refs = refs[sum(counts) :]
    gate_ref, up_ref, down_ref, inner_ref, grad_gate_ref, grad_up_ref = refs[:6]
    weight_gate_ref, weight_up_ref, weight_down_ref = refs[6:9]
    rows, row_sems, target, target_sems, rows_t, target_t = refs[9:]

    @pl.when(pl.program_id(0) == 0)
    def _():
        copies = fetch(row_pieces, rows, row_sems) + fetch(target_pieces, target, target_sems)
        for copy in copies:
            copy.wait()
        rows_t[...] = rows[...].T
        target_t[...] = target[...].T

    gate_weight, up_weight, down_weight = unpacked(gate_ref), unpacked(up_ref), unpacked(down_ref)
    for start in range(0, rows.shape[0], chunk):
        span = slice(start, start + chunk)
        gate = contract(rows[span, :], gate_weight, 1, 0)
        up = contract(rows[span, :], up_weight, 1, 0)
        grad_inner = contract(target[span, :], down_weight, 1, 1)
        share = jax.nn.sigmoid(gate)
        activated = gate * share
        inner_ref[span, :] = (activated * up).astype(BF16)
        grad_up_ref[span, :] = (grad_inner * activated).astype(BF16)
        grad_gate_ref[span, :] = (
            grad_inner * up * share * (1.0 + gate * (1.0 - share))
        ).astype(BF16)
    weight_gate_ref[...] = contract(rows_t[...], grad_gate_ref[...], 1, 0).astype(BF16)
    weight_up_ref[...] = contract(rows_t[...], grad_up_ref[...], 1, 0).astype(BF16)
    weight_down_ref[...] = contract(target_t[...], inner_ref[...], 1, 0).T.astype(BF16)


def feed(rows, target, weights, block=256, chunk=512):
    count = sum(piece.shape[0] for piece in rows)
    width = rows[0].shape[1]
    across_spec = lambda units: pl.BlockSpec((width, min(block, units)), lambda i: (0, i))
    down_spec = lambda units: pl.BlockSpec((min(block, units), width), lambda i: (i, 0))
    if packed(weights[0]):
        units = width
        replicas, deep = weights[0][0].shape[0], width // weights[0][0].shape[0]
        specs = [
            pl.BlockSpec((replicas, deep, block), lambda i, plane=weights[k][1]: (0, plane, i))
            for k in range(2)
        ] + [
            pl.BlockSpec(
                (block // deep, deep, width), lambda i, plane=weights[2][1]: (i, plane, 0)
            )
        ]
        weights = [weight for weight, _ in weights]
    else:
        units = weights[0].shape[1]
        specs = [across_spec(units)] * 2 + [down_spec(units)]
    block = min(block, units)
    out = pl.BlockSpec((count, block), lambda i: (0, i))
    return pl.pallas_call(
        functools.partial(feed_kernel, counts=(len(rows), len(target)), chunk=chunk),
        grid=(units // block,),
        in_specs=[pl.BlockSpec(memory_space=pl.ANY)] * (len(rows) + len(target)) + specs,
        out_specs=[out, out, out] + [across_spec(units)] * 2 + [down_spec(units)],
        out_shape=[jax.ShapeDtypeStruct((count, units), BF16)] * 3
        + [jax.ShapeDtypeStruct((width, units), BF16)] * 2
        + [jax.ShapeDtypeStruct((units, width), BF16)],
        scratch_shapes=room(rows) + room(target) + [pltpu.VMEM((width, count), BF16)] * 2,
        cost_estimate=cost(
            12 * count * width * units,
            4 * count * width + 12 * width * units + 6 * count * units,
            2 * count * units,
        ),
        compiler_params=pltpu.CompilerParams(vmem_limit_bytes=60 * MIB),
        name="feed_forward",
    )(*rows, *target, *weights)


def sum_kernel(*refs, places, dims, start, chunk):
    terms = len(dims)
    operands, out_ref = refs[: 2 * terms], refs[2 * terms]
    buffers = refs[2 * terms + 1 : 4 * terms + 1]
    total, result, sems, out_sems = refs[4 * terms + 1 :]
    rows = total.shape[0]
    copies = []
    for index, (ref, place) in enumerate(zip(operands, places)):
        copy = pltpu.make_async_copy(ref.at[place], buffers[index], sems.at[index])
        copy.start()
        copies.append(copy)
    sent = []
    for index, dim in enumerate(dims):
        copies[2 * index].wait()
        copies[2 * index + 1].wait()
        right = unpacked(buffers[2 * index + 1])
        for first in range(0, rows, chunk):
            span = slice(first, first + chunk)
            product = contract(buffers[2 * index][span, :], right, 1, dim)
            if index:
                product = total[span, :] + product
            if index + 1 < terms:
                total[span, :] = product
                continue
            result[span, :] = product.astype(result.dtype)
            copy = pltpu.make_async_copy(
                result.at[pl.ds(first, chunk), :],
                out_ref.at[pl.ds(first, chunk), :],
                out_sems.at[first // chunk],
            )
            copy.start()
            sent.append(copy)
    for copy in sent:
        copy.wait()


def sum_products(terms, start, rows, dtype=F32, chunk=256):
    chunk = min(chunk, rows)
    operands, places, shapes, dims, flops, moved = [], [], [], [], 0, 0
    for left, plane, right, part, dim in terms:
        depth = left.shape[-1]
        span = pl.ds(start, rows)
        places.append((span, slice(None)) if plane is None else (plane, span, slice(None)))
        shapes.append((rows, depth))
        if packed(right):
            right, plane = right
            width = right.shape[2]
            deep = width // right.shape[0]
            places.append((slice(None), pl.ds(plane * deep, deep), slice(None)))
            shapes.append((right.shape[0], deep, width))
        else:
            column = pl.ds(0, right.shape[1]) if part is None else pl.ds(part * depth, depth)
            places.append((slice(None), column))
            shapes.append((right.shape[0], column.size))
            width = shapes[-1][1 - dim]
        operands += [left, right]
        dims.append(dim)
        flops += 2 * rows * depth * width
        moved += 2 * rows * depth + 2 * depth * width
    anywhere = pl.BlockSpec(memory_space=pl.ANY)
    return pl.pallas_call(
        functools.partial(
            sum_kernel, places=places, dims=tuple(dims), start=start, chunk=chunk
        ),
        in_specs=[anywhere] * len(operands),
        out_specs=anywhere,
        out_shape=jax.ShapeDtypeStruct((rows, width), dtype),
        scratch_shapes=[pltpu.VMEM(shape, BF16) for shape in shapes]
        + [
            pltpu.VMEM((rows, width), F32),
            pltpu.VMEM((rows, width), dtype),
            pltpu.SemaphoreType.DMA((len(operands),)),
            pltpu.SemaphoreType.DMA((rows // chunk,)),
        ],
        cost_estimate=cost(flops, moved + 4 * rows * width),
        compiler_params=pltpu.CompilerParams(vmem_limit_bytes=58 * MIB),
        name="sum_products",
    )(*operands)


def outer_kernel(*refs, count):
    right_ref, out_ref, left, sems, left_t = refs[count:]

    @pl.when(pl.program_id(0) == 0)
    def _():
        for copy in fetch(refs[:count], left, sems):
            copy.wait()
        left_t[...] = left[...].T

    out_ref[...] = contract(left_t[...], right_ref[...], 1, 0).astype(BF16)


def outer(pieces, right):
    width = pieces[0].shape[1]
    planes, count, columns = right.shape
    return pl.pallas_call(
        functools.partial(outer_kernel, count=len(pieces)),
        grid=(planes,),
        in_specs=[pl.BlockSpec(memory_space=pl.ANY)] * len(pieces)
        + [pl.BlockSpec((None, count, columns), lambda i: (i, 0, 0))],
        out_specs=pl.BlockSpec((width, columns), lambda i: (0, i)),
        out_shape=jax.ShapeDtypeStruct((width, planes * columns), BF16),
        scratch_shapes=room(pieces) + [pltpu.VMEM((width, count), BF16)],
        cost_estimate=cost(
            2 * count * width * planes * columns,
            2 * count * (width + planes * columns) + 2 * width * planes * columns,
        ),
        compiler_params=pltpu.CompilerParams(vmem_limit_bytes=40 * MIB),
        name="outer_product",
    )(*pieces, right)


def branch_kernel(*refs, count, groups, chunk):
    weights = refs[count : count + groups]
    mixed = refs[count + groups : count + 2 * groups]
    outs = refs[count + 2 * groups : count + 4 * groups]
    rows, sems = refs[count + 4 * groups :]
    for copy in fetch(refs[:count], rows, sems):
        copy.wait()
    for index in range(groups):
        outs[groups + index][...] = contract(mixed[index][...].T, rows[...], 1, 0).astype(BF16)
        for start in range(0, rows.shape[0], chunk):
            span = slice(start, start + chunk)
            outs[index][span, :] = contract(rows[span, :], weights[index][...], 1, 1).astype(BF16)


def branch_back(pieces, weights, mixed, chunk=512):
    count = sum(piece.shape[0] for piece in pieces)
    width = pieces[0].shape[1]
    groups = len(weights)
    vmem = pl.BlockSpec(memory_space=pltpu.VMEM)
    columns = [weight.shape[0] for weight in weights]
    results = pl.pallas_call(
        functools.partial(branch_kernel, count=len(pieces), groups=groups, chunk=chunk),
        in_specs=[pl.BlockSpec(memory_space=pl.ANY)] * len(pieces) + [vmem] * (2 * groups),
        out_specs=[vmem] * (2 * groups),
        out_shape=[jax.ShapeDtypeStruct((count, size), BF16) for size in columns]
        + [jax.ShapeDtypeStruct((size, width), BF16) for size in columns],
        scratch_shapes=room(pieces),
        cost_estimate=cost(4 * count * width * sum(columns), 6 * count * width),
        compiler_params=pltpu.CompilerParams(vmem_limit_bytes=48 * MIB),
        name="branch_backward",
    )(*pieces, *weights, *mixed)
    return results[:groups], results[groups:]


def standardize(value):
    centred = value - jnp.mean(value, axis=-1, keepdims=True)
    scale = lax.rsqrt(jnp.mean(centred * centred, axis=-1, keepdims=True) + EPSILON)
    return centred * scale, scale


def norm_kernel(*refs, added):
    value = refs[0][...].astype(F32)
    for ref in refs[1 : 1 + added]:
        value = value + ref[...].astype(F32)
    gain_ref, shift_ref = refs[1 + added : 3 + added]
    standard, _ = standardize(value)
    if added:
        refs[-2][...] = value
    refs[-1][...] = (standard * gain_ref[...] + shift_ref[...]).astype(BF16)


def norm(base, terms, gain, shift, pieces=PIECES, block=256):
    count, width = base.shape
    rows = count // pieces
    block = min(block, rows)
    vector = pl.BlockSpec((1, width), lambda i: (0, 0))
    total, out = None, []
    for piece in range(pieces):
        first = piece * rows // block
        whole = pl.BlockSpec((block, width), lambda i, first=first: (first + i, 0))
        shapes = [jax.ShapeDtypeStruct((rows, width), BF16)]
        specs = [pl.BlockSpec((block, width), lambda i: (i, 0))]
        held = []
        if terms:
            shapes = [jax.ShapeDtypeStruct((count, width), F32)] + shapes
            specs = [whole] + specs
            held = [] if total is None else [total]
        results = pl.pallas_call(
            lambda *refs, held=len(held): norm_kernel(
                *refs[: 3 + len(terms)], *refs[3 + len(terms) + held :], added=len(terms)
            ),
            grid=(rows // block,),
            in_specs=[whole] * (1 + len(terms))
            + [vector, vector]
            + [pl.BlockSpec(memory_space=pl.ANY)] * len(held),
            out_specs=specs,
            out_shape=shapes,
            input_output_aliases={3 + len(terms): 0} if held else {},
            cost_estimate=cost(16 * rows * width, 8 * rows * width * len(shapes)),
            name="layer_norm",
        )(base, *terms, gain.reshape(1, width), shift.reshape(1, width), *held)
        out.append(results[-1])
        if terms:
            total = results[0]
    return total, out


def norm_back_kernel(*refs, added, low):
    base_ref, straight_ref, gain_ref = refs[:3]
    upstream = refs[3][...].astype(F32)
    for ref in refs[4 : 3 + added]:
        upstream = upstream + ref[...].astype(F32)
    outs = refs[3 + added :]
    standard, scale = standardize(base_ref[...].astype(F32))
    scaled = upstream * gain_ref[...]
    back = straight_ref[...].astype(F32) + scale * (
        scaled
        - jnp.mean(scaled, axis=-1, keepdims=True)
        - standard * jnp.mean(scaled * standard, axis=-1, keepdims=True)
    )
    outs[0][...] = back.astype(BF16)
    if not low:
        outs[1][...] = back
    sums = jnp.concatenate(
        [
            jnp.sum(upstream * standard, axis=0, keepdims=True),
            jnp.sum(upstream, axis=0, keepdims=True),
        ],
        axis=0,
    )

    @pl.when(pl.program_id(0) == 0)
    def _():
        outs[-1][...] = sums

    @pl.when(pl.program_id(0) > 0)
    def _():
        outs[-1][...] += sums


def norm_back(base, straight, gain, terms, low, pieces=PIECES, block=256):
    count, width = base.shape
    rows = count // pieces
    block = min(block, rows)
    total, out, found = None, [], []
    for piece in range(pieces):
        first = piece * rows // block
        whole = pl.BlockSpec((block, width), lambda i, first=first: (first + i, 0))
        shapes = [jax.ShapeDtypeStruct((rows, width), BF16)]
        specs = [pl.BlockSpec((block, width), lambda i: (i, 0))]
        held = []
        if not low:
            shapes.append(jax.ShapeDtypeStruct((count, width), F32))
            specs.append(whole)
            held = [] if total is None else [total]
        results = pl.pallas_call(
            lambda *refs, held=len(held): norm_back_kernel(
                *refs[: 3 + len(terms)],
                *refs[3 + len(terms) + held :],
                added=len(terms),
                low=low,
            ),
            grid=(rows // block,),
            in_specs=[whole, whole, pl.BlockSpec((1, width), lambda i: (0, 0))]
            + [whole] * len(terms)
            + [pl.BlockSpec(memory_space=pl.ANY)] * len(held),
            out_specs=specs + [pl.BlockSpec((2, width), lambda i: (0, 0))],
            out_shape=shapes + [jax.ShapeDtypeStruct((2, width), F32)],
            input_output_aliases={3 + len(terms): 1} if held else {},
            cost_estimate=cost(30 * rows * width, 16 * rows * width),
            name="layer_norm_backward",
        )(base, straight, gain.reshape(1, width), *terms, *held)
        out.append(results[0])
        found.append(results[-1])
        if not low:
            total = results[1]
    return out, total, sum(found)


def rope_tables(offset):
    half = HD // 2
    groups = LANES // half
    count = LEN // groups
    lane = jnp.arange(LANES, dtype=jnp.int32)
    position = jnp.arange(count, dtype=jnp.int32)[:, None] + lane[None, :] // half * count
    position = (position + offset) % LEN
    inverse = 10000.0 ** (-2.0 * (lane % half).astype(F32) / HD)
    angles = position.astype(F32) * inverse[None, :]
    cosines, sines = lax.optimization_barrier((jnp.cos(angles), jnp.sin(angles)))

    def rows(table, signs):
        parts = [table[:, g * half : (g + 1) * half] for g in range(groups)]
        return jnp.concatenate(
            [jnp.concatenate([sign * part for sign in signs], axis=1) for part in parts], axis=0
        )

    return rows(cosines, (1, 1, 1, 1)), rows(sines, (-1, 1, -1, 1))


def exchanges(axis, size):
    if size & (size - 1):
        return [lambda value: lax.psum(value, axis)]
    return [
        lambda value, pairs=[(i, i ^ (1 << bit)) for i in range(size)]: value
        + lax.ppermute(value, axis, pairs)
        for bit in range(size.bit_length() - 1)
    ]


def shards(
    dp_size,
    tensor_size,
    tokens,
    lengths,
    gain_first,
    shift_first,
    query_weight,
    key_weight,
    value_weight,
    output_weight,
    gain_second,
    shift_second,
    gate_weight,
    up_weight,
    down_weight,
    cotangent,
):
    windows = lengths.shape[0]
    span = tensor_size // windows
    held = tokens.shape[0]
    width = tokens.shape[1]
    head_cols = query_weight.shape[1]
    here = lax.axis_index("tensor")
    window, seat = here // span, here % span

    def from_seat(value, shift):
        pairs = [
            (w * span + (s + shift) % span, w * span + s)
            for w in range(windows)
            for s in range(span)
        ]
        return lax.ppermute(value, "tensor", pairs)

    def to_seat(value, shift):
        return from_seat(value, span - shift)

    def from_window(value, shift):
        pairs = [((t + shift * span) % tensor_size, t) for t in range(tensor_size)]
        return lax.ppermute(value, "tensor", pairs)

    def to_window(value, shift):
        return from_window(value, windows - shift)

    def gather_rows(value):
        return value + [from_seat(piece, s) for s in range(1, span) for piece in value]

    def scatter(partial):
        sent = [to_seat(partial(s * held, held), s) for s in range(1, span)]
        return [partial(0, held)] + sent

    def all_windows(value):
        return [value] + [from_window(value, shift) for shift in range(1, windows)]

    def spread_windows(values):
        group = lax.axis_index("dp")
        sizes = [value.shape[0] // dp_size for value in values]
        mine = jnp.concatenate(
            [
                lax.dynamic_slice_in_dim(value, group * size, size, axis=0).reshape(-1, width)
                for value, size in zip(values, sizes)
            ],
            axis=0,
        )
        return [mine], [from_window(mine, shift) for shift in range(1, windows)]

    def gather_spread(values, piece):
        gathered = lax.all_gather(piece, "dp", axis=0)
        if all(value.shape == (width, width) for value in values):
            return [(gathered, plane) for plane in range(len(values))]
        out, start = [], 0
        for value in values:
            count = value.size // width // dp_size
            out.append(gathered[:, start : start + count].reshape(value.shape))
            start += count
        return out

    def after(value, *others):
        return lax.optimization_barrier((value, *others))[0]

    def pieces_after(pieces, *others):
        return [after(pieces[0], *others)] + pieces[1:]

    place = jnp.stack(
        [lax.dynamic_index_in_dim(lengths, window, keepdims=False), seat * held]
    ).astype(jnp.int32)
    cosines, sines = rope_tables(seat * held)

    members = [[s] for s in range(windows)] if head_cols % LANES == 0 else [list(range(windows))]
    feed_weights = [gate_weight, up_weight, down_weight]
    slices_sent, slices = spread_windows(feed_weights)
    _, normed_one = norm(after(tokens, *slices_sent), [], gain_first, shift_first)
    full_one = gather_rows(normed_one)
    qkv_own = jnp.concatenate([query_weight, key_weight, value_weight], axis=1)
    qkv_other = all_windows(after(qkv_own, *slices))[1:]
    qkv_shards = [qkv_own] + qkv_other
    def joined(parts, axis):
        return parts[0] if len(parts) == 1 else jnp.concatenate(parts, axis=axis)

    def part_of(value, part):
        return value[:, part * head_cols : (part + 1) * head_cols]

    qkv_weights = [
        qkv_shards[group[0]]
        if len(group) == 1
        else joined([part_of(qkv_shards[s], part) for part in range(3) for s in group], 1)
        for group in members
    ]
    target = gather_rows([cotangent])
    qkv, attended = [], []
    rows_one = full_one
    for weight in qkv_weights:
        parts = project(rows_one, weight, cosines, sines)
        if not qkv:
            slices = [after(piece, parts[0]) for piece in slices]
            feed_shards = [feed_weights]
            feed_shards += [gather_spread(feed_weights, piece) for piece in slices]
        waits = slices if not qkv else target
        qkv.append((after(parts[0], *waits), *parts[1:]))
        attended.append(attend(place, *qkv[-1]))
        if len(attended) == 1:
            sent = after(output_weight, attended[0][0])
            output_shards = [output_weight] + all_windows(sent)[1:]
        rows_one = pieces_after(full_one, attended[-1][0])

    out_weights = [joined([output_shards[s] for s in group], 0) for group in members]
    mixer_terms = [
        (mixed, None, weight, None, 0) for (mixed, _), weight in zip(attended, out_weights)
    ]
    hidden_one, normed_two = norm(
        tokens,
        scatter(lambda start, rows: sum_products(mixer_terms, start, rows)),
        gain_second,
        shift_second,
    )
    full_two = gather_rows(normed_two)

    flip = [(d, d ^ 1) for d in range(dp_size)]
    odd = lax.axis_index("dp") % 2

    def half(value, which):
        count = value.shape[0] // 2
        return lax.dynamic_slice_in_dim(value, which * count, count, axis=0)

    def total(pieces, which):
        return sum(half(piece, which).astype(F32) for piece in pieces).astype(BF16)

    def swap_half(pieces, *others):
        pieces = [after(piece, *others) for piece in pieces]
        mine, sent = total(pieces, odd), total(pieces, 1 - odd)
        return (mine, lax.ppermute(sent, "dp", flip)), [mine, sent]

    def add_half(halves, *others):
        mine, received = (after(value, *others) for value in halves)
        return (mine.astype(F32) + received.astype(F32)).astype(BF16)

    def sum_half(value, turn):
        groups = [list(range(0, dp_size, 2)), list(range(1, dp_size, 2))]
        if turn & 1:
            groups = groups[::-1]
        if turn & 2:
            groups = [group[::-1] for group in groups]
        return lax.psum(value, "dp", axis_index_groups=groups)

    def swap_sum(mine, *others):
        mine = after(mine, *others)
        return mine, lax.ppermute(mine, "dp", flip)

    def whole_sum(halves, *others):
        mine, received = (after(value, *others) for value in halves)
        first, second = jnp.where(odd == 0, mine, received), jnp.where(odd == 0, received, mine)
        return jnp.concatenate([first, second], axis=0).astype(F32)

    def send_to_owner(parts):
        return [to_window(parts[shift], shift) for shift in range(1, windows)]

    order = list(range(1, windows)) + [0]
    fed = {}
    rows_two = full_two
    for s in order:
        fed[s] = feed(rows_two, target, feed_shards[s])
        rows_two = pieces_after(full_two, fed[s][0])
    down_pieces, up_pieces, gate_pieces = (
        send_to_owner({s: fed[s][k] for s in order}) + [fed[0][k]] for k in (5, 4, 3)
    )
    two_terms, feed_terms = [], []
    for s in order:
        gate, up, down = feed_shards[s]
        two_terms += [(fed[s][1], None, gate, None, 1), (fed[s][2], None, up, None, 1)]
        feed_terms.append((fed[s][0], None, down, None, 0))

    two_sent = [
        sum_products(two_terms, shift * held, held, BF16) for shift in range(1, span)
    ]
    down_half, marks = swap_half(down_pieces, *two_sent)
    two_terms = [(after(two_terms[0][0], *marks), *two_terms[0][1:])] + two_terms[1:]
    two_kept = sum_products(two_terms, 0, held)
    grad_branch_own, grad_hidden, norm_two = norm_back(
        hidden_one,
        cotangent,
        gain_second,
        [two_kept] + [to_seat(part, shift + 1) for shift, part in enumerate(two_sent)],
        False,
    )
    grad_branch = gather_rows(grad_branch_own)
    down_half = add_half(down_half, *grad_branch_own)
    down_sum = sum_half(down_half, 0)
    grad_branch = pieces_after(grad_branch, down_half)

    members = members[::-1]
    out_weights, qkv_weights = out_weights[::-1], qkv_weights[::-1]
    qkv, attended = qkv[::-1], attended[::-1]
    grad_mixed, found = branch_back(grad_branch, out_weights, [mixed for mixed, _ in attended])
    out_grads = {
        s: out_grad[spot * head_cols : (spot + 1) * head_cols]
        for group, out_grad in zip(members, found)
        for spot, s in enumerate(group)
    }
    out_pieces = send_to_owner(out_grads) + [out_grads[0]]

    def up_swap(last):
        sums["up"], waits = swap_half(up_pieces, *last)
        return waits

    def up_sum(last):
        value = add_half(sums["up"], *last)
        sums["up"] = sum_half(value, 1)
        sums["gate"], waits = swap_half(gate_pieces, value)
        return [value] + waits

    def gate_sum(last):
        sums["gate"] = value = add_half(sums["gate"], *last)
        sums["out"], waits = swap_half(out_pieces, *last)
        sums["down"] = swap_sum(down_sum, *last)
        return [value, sums["down"][0]] + waits

    def down_whole(last):
        sums["down"] = whole_sum(sums["down"], *last)
        value = add_half(sums["out"], *last)
        sums["gate"], sums["out"] = sum_half((sums["gate"], value), 2)
        sums["up"] = swap_sum(sums["up"], *last)
        return [sums["down"], value, sums["up"][0]]

    across, along = (exchanges(axis, size) for axis, size in (("tensor", tensor_size), ("dp", dp_size)))
    norm_steps = across + along[1:]
    sums = {}
    moves = [up_swap, up_sum, gate_sum, down_whole]
    last = list(grad_mixed)
    grad_qkv, qkv_grads = [], {}
    for index, group in enumerate(members):
        mixed, logs = attended[index]
        count = len(group) * head_cols
        grads = None
        for pair in range(count // LANES):
            waits = moves.pop(0)(last) if moves else last
            if norm_steps:
                norm_two = norm_steps.pop(0)(after(norm_two, *last))
                waits = waits + [norm_two]
            grads = attend_back(
                place,
                *qkv[index],
                mixed,
                after(grad_mixed[index], *waits),
                logs,
                cosines,
                sines,
                pair,
                grads,
            )
            last = [grads]
        grad_qkv.append(grads)
        qkv_grad = outer(full_one, grads)
        last = [qkv_grad]
        for spot, s in enumerate(group):
            if len(group) == 1:
                qkv_grads[s] = qkv_grad
            else:
                qkv_grads[s] = joined(
                    [
                        lax.slice_in_dim(
                            qkv_grad,
                            part * count + spot * head_cols,
                            part * count + (spot + 1) * head_cols,
                            axis=1,
                        )
                        for part in range(3)
                    ],
                    1,
                )
    for move in moves:
        last = move(last)

    qkv_half, marks = swap_half(send_to_owner(qkv_grads) + [qkv_grads[0]])
    grad_up = whole_sum(sums["up"], *marks)
    feed_terms[0] = (after(feed_terms[0][0], grad_up), *feed_terms[0][1:])
    one_terms = [
        (grad_qkv[index], part, weight, part, 1)
        for index, weight in enumerate(qkv_weights)
        for part in range(3)
    ]

    def later(terms, *others):
        return [(after(terms[0][0], *others), *terms[0][1:])] + terms[1:]

    shifts = range(1, span)
    feed_sent = [sum_products(feed_terms, shift * held, held, BF16) for shift in shifts]
    qkv_half = add_half(qkv_half, *feed_sent)
    gate_halves = swap_sum(sums["gate"], *feed_sent)
    out_halves = swap_sum(sums["out"], *feed_sent)
    qkv_sum = sum_half(after(qkv_half, gate_halves[0], out_halves[0]), 3)
    one_terms = later(one_terms, qkv_half, gate_halves[0])
    one_sent = [sum_products(one_terms, shift * held, held, BF16) for shift in shifts]
    feed_parts = [sum_products(later(feed_terms, *one_sent), 0, held)]
    one_parts = [sum_products(later(one_terms, feed_parts[0]), 0, held)]
    feed_parts += [to_seat(part, shift) for shift, part in zip(shifts, feed_sent)]
    one_parts += [to_seat(part, shift) for shift, part in zip(shifts, one_sent)]
    output = (hidden_one + sum(feed_parts)).astype(BF16)
    (input_grad,), _, norm_one = norm_back(tokens, grad_hidden, gain_first, one_parts, True, 1)
    for step in norm_steps:
        norm_two = step(norm_two)
    grad_down = sums["down"]
    window = [input_grad, output]
    qkv_halves = swap_sum(qkv_sum, *window)
    norm_one = after(norm_one, qkv_halves[0])
    for step in across + along[1:]:
        norm_one = step(norm_one)
    norms = along[0](jnp.concatenate([norm_one, norm_two], axis=0))
    norm_one, norm_two = norms[:2], norms[2:]
    grad_gate = whole_sum(gate_halves, qkv_halves[0])
    out_grad = whole_sum(out_halves, qkv_halves[0])
    qkv_grad = whole_sum(qkv_halves)
    return (
        output,
        input_grad,
        *(part_of(qkv_grad, part) for part in range(3)),
        out_grad,
        grad_gate,
        grad_up,
        grad_down,
        norm_one[0],
        norm_one[1],
        norm_two[0],
        norm_two[1],
    )


def solution(mesh):
    rows = P(("dp", "tensor"), None)
    columns = P(None, "tensor")
    depth = P("tensor", None)
    return jax.shard_map(
        functools.partial(shards, mesh.shape["dp"], mesh.shape["tensor"]),
        mesh=mesh,
        in_specs=(
            rows,
            P("dp"),
            P(),
            P(),
            columns,
            columns,
            columns,
            depth,
            P(),
            P(),
            columns,
            columns,
            depth,
            rows,
        ),
        out_specs=(
            rows,
            rows,
            columns,
            columns,
            columns,
            depth,
            columns,
            columns,
            depth,
            P(),
            P(),
            P(),
            P(),
        ),
        check_vma=False,
    )
```

```python
import functools
import math

import jax
import jax.numpy as jnp
from jax import lax
from jax.experimental import pallas as pl
from jax.experimental.pallas import tpu as pltpu
from jax.sharding import PartitionSpec as P

HD = 64
LEN = 2048
EPSILON = 1e-05
MASKED = -1e30
LANES = 128
LOG2E = math.log2(math.e)
BF16 = jnp.bfloat16
F32 = jnp.float32
MIB = 1 << 20
COST_SHARE = 0.01
PIECES = 2


def contract(left, right, left_dim, right_dim):
    return lax.dot_general(
        left, right, (((left_dim,), (right_dim,)), ((), ())), preferred_element_type=F32
    )


def cost(flops, moved, transcendentals=0):
    return pl.CostEstimate(
        flops=int(flops * COST_SHARE),
        bytes_accessed=int(moved * COST_SHARE),
        transcendentals=int(transcendentals * COST_SHARE),
    )


def swap_halves(value):
    columns = value.shape[1]
    lane = lax.broadcasted_iota(jnp.int32, value.shape, 1)
    return jnp.where(
        lane % HD < HD // 2,
        pltpu.roll(value, columns - HD // 2, 1),
        pltpu.roll(value, HD // 2, 1),
    )


def fetch(pieces, rows, sems):
    copies, start = [], 0
    for index, piece in enumerate(pieces):
        count = piece.shape[0]
        copies.append(
            pltpu.make_async_copy(piece, rows.at[pl.ds(start, count), :], sems.at[index])
        )
        start += count
    for copy in copies:
        copy.start()
    return copies


def room(pieces):
    count = sum(piece.shape[0] for piece in pieces)
    return [
        pltpu.VMEM((count, pieces[0].shape[1]), BF16),
        pltpu.SemaphoreType.DMA((len(pieces),)),
    ]


def unpacked(ref):
    value = ref[...]
    return value.reshape(-1, value.shape[-1]) if value.ndim == 3 else value


def packed(weight):
    return isinstance(weight, tuple)


def project_kernel(*refs, count):
    pieces = refs[:count]
    weight_ref, cos_ref, sin_ref, q_ref, k_ref, v_ref, rows, sems = refs[count:]
    columns = q_ref.shape[1]
    block = q_ref.shape[0]

    @pl.when(pl.program_id(0) == 0)
    def _():
        for copy in fetch(pieces, rows, sems):
            copy.wait()

    start = pl.multiple_of(pl.program_id(0) * block, block)
    product = contract(rows[pl.ds(start, block), :], weight_ref[...], 1, 0)
    cosines = jnp.concatenate([cos_ref[...]] * (columns // LANES), axis=1)
    sines = jnp.concatenate([sin_ref[...]] * (columns // LANES), axis=1)
    for part, out_ref in ((0, q_ref), (1, k_ref)):
        value = product[:, part * columns : (part + 1) * columns]
        out_ref[...] = (value * cosines + swap_halves(value) * sines).astype(BF16)
    v_ref[...] = product[:, 2 * columns :].astype(BF16)


def project(pieces, weight, cosines, sines, block=512):
    width = weight.shape[0]
    columns = weight.shape[1] // 3
    count = sum(piece.shape[0] for piece in pieces)
    table = pl.BlockSpec((block, LANES), lambda i: (i, 0))
    out = pl.BlockSpec((block, columns), lambda i: (i, 0))
    return pl.pallas_call(
        functools.partial(project_kernel, count=len(pieces)),
        grid=(count // block,),
        in_specs=[pl.BlockSpec(memory_space=pl.ANY)] * len(pieces)
        + [pl.BlockSpec(weight.shape, lambda i: (0, 0)), table, table],
        out_specs=[out, out, out],
        out_shape=[jax.ShapeDtypeStruct((count, columns), BF16)] * 3,
        scratch_shapes=room(pieces),
        cost_estimate=cost(
            2 * count * width * 3 * columns,
            2 * (count * width + width * 3 * columns + count * 3 * columns),
        ),
        compiler_params=pltpu.CompilerParams(vmem_limit_bytes=40 * MIB),
        name="project_rope",
    )(*pieces, weight, cosines, sines)


def masked_keys(place_ref, key_ref, masked_ref):
    count = key_ref.shape[0]
    lane = lax.broadcasted_iota(jnp.int32, (count, LANES), 1)
    row = lax.broadcasted_iota(jnp.int32, (count, LANES), 0) + place_ref[1]
    position = jnp.where(row >= count, row - count, row)
    bias = jnp.where(position >= place_ref[0], MASKED, 0.0).astype(BF16)
    nothing = jnp.zeros_like(bias)
    key = key_ref[...]
    masked_ref[0] = jnp.where(lane < HD, key, jnp.where(lane == HD, bias, nothing))
    masked_ref[1] = jnp.where(lane >= HD, key, jnp.where(lane == 0, bias, nothing))


def masked_queries(query):
    lane = lax.broadcasted_iota(jnp.int32, query.shape, 1)
    scaled = query * jnp.asarray(1.0 / math.sqrt(HD), BF16)
    one = jnp.ones_like(query)
    nothing = jnp.zeros_like(query)
    return (
        scaled,
        jnp.where(lane < HD, scaled, jnp.where(lane == HD, one, nothing)),
        jnp.where(lane >= HD, scaled, jnp.where(lane == 0, one, nothing)),
    )


def attend_kernel(place_ref, q_ref, k_ref, v_ref, out_ref, log_ref, keys, values_t, *, chunk):
    count = k_ref.shape[0]

    @pl.when(pl.program_id(1) == 0)
    def _():
        masked_keys(place_ref, k_ref, keys)
        values_t[...] = v_ref[...].T

    queries = masked_queries(q_ref[...])[1:]
    mixed, logs = [], []
    for head in range(2):
        scores = [
            contract(keys[head, start : start + chunk, :], queries[head], 1, 1)
            for start in range(0, count, chunk)
        ]
        top = functools.reduce(
            jnp.maximum, [jnp.max(block, axis=0, keepdims=True) for block in scores]
        )
        total = 0.0
        summed = 0.0
        for index, block in enumerate(scores):
            weights = jnp.exp2((block - top) * LOG2E)
            total = total + jnp.sum(weights, axis=0, keepdims=True)
            value = values_t[
                head * HD : (head + 1) * HD, index * chunk : (index + 1) * chunk
            ]
            summed = summed + contract(value, weights.astype(BF16), 1, 0)
        mixed.append(summed / total)
        logs.append(top * LOG2E + jnp.log2(total))
    out_ref[...] = jnp.concatenate(mixed, axis=0).T.astype(BF16)
    log_ref[0] = jnp.concatenate(logs + [jnp.zeros((6, q_ref.shape[0]), F32)], axis=0)


def attend(place, queries, keys, values, block=1024, chunk=512):
    count, columns = queries.shape
    pairs = columns // LANES
    whole = pl.BlockSpec((count, LANES), lambda p, i, _: (0, p))
    rows = pl.BlockSpec((block, LANES), lambda p, i, _: (i, p))
    return pl.pallas_call(
        functools.partial(attend_kernel, chunk=chunk),
        grid_spec=pltpu.PrefetchScalarGridSpec(
            num_scalar_prefetch=1,
            grid=(pairs, count // block),
            in_specs=[rows, whole, whole],
            out_specs=[rows, pl.BlockSpec((1, 8, block), lambda p, i, _: (p, 0, i))],
            scratch_shapes=[
                pltpu.VMEM((2, count, LANES), BF16),
                pltpu.VMEM((LANES, count), BF16),
            ],
        ),
        out_shape=[
            jax.ShapeDtypeStruct((count, columns), BF16),
            jax.ShapeDtypeStruct((pairs, 8, count), F32),
        ],
        cost_estimate=cost(16 * count * count * columns, 8 * count * columns, count * count * columns // HD),
        compiler_params=pltpu.CompilerParams(vmem_limit_bytes=56 * MIB),
        name="attention_forward",
    )(place, queries, keys, values)


def attend_back_kernel(
    place_ref,
    q_ref,
    k_ref,
    v_ref,
    out_ref,
    up_ref,
    log_ref,
    cos_row_ref,
    sin_row_ref,
    cos_ref,
    sin_ref,
    *rest,
    chunk,
):
    grad_ref, keys, grad_keys_t, grad_values_t = rest[-4:]
    count = k_ref.shape[0]
    step = pl.program_id(1)

    @pl.when(step == 0)
    def _():
        masked_keys(place_ref, k_ref, keys)
        grad_keys_t[...] = jnp.zeros_like(grad_keys_t)
        grad_values_t[...] = jnp.zeros_like(grad_values_t)

    scaled, *queries = masked_queries(q_ref[...])
    upstream = up_ref[...]
    lane = lax.broadcasted_iota(jnp.int32, upstream.shape, 1)
    nothing = jnp.zeros_like(upstream)
    products = upstream.astype(F32) * out_ref[...].astype(F32)
    scaled_t = scaled.T
    upstream_t = upstream.T
    logs = log_ref[0].T
    grad_queries = []
    for head in range(2):
        mine = (lane < HD) == (head == 0)
        own_upstream = jnp.where(mine, upstream, nothing)
        row_dot = jnp.sum(jnp.where(mine, products, 0.0), axis=1, keepdims=True)
        log_total = logs[:, head : head + 1]
        heads = slice(head * HD, (head + 1) * HD)
        grad_query = 0.0
        for start in range(0, count, chunk):
            span = slice(start, start + chunk)
            scores = contract(queries[head], keys[head, span, :], 1, 1)
            probs = jnp.exp2(scores * LOG2E - log_total)
            grad_probs = contract(own_upstream, v_ref[span, :], 1, 1)
            grad_scores = (probs * (grad_probs - row_dot)).astype(BF16)
            grad_values_t[heads, span] += contract(
                upstream_t[heads, :], probs.astype(BF16), 1, 0
            )
            grad_keys_t[heads, span] += contract(scaled_t[heads, :], grad_scores, 1, 0)
            grad_query = grad_query + contract(grad_scores, k_ref[span, :], 1, 0)
        grad_queries.append(grad_query)
    grad_query = jnp.where(lane < HD, *grad_queries) * (1.0 / math.sqrt(HD))
    block = grad_query.shape[0]
    grad_ref[0, pl.ds(pl.multiple_of(step * block, block), block), :] = (
        grad_query * cos_row_ref[...] - swap_halves(grad_query) * sin_row_ref[...]
    ).astype(BF16)

    @pl.when(step == pl.num_programs(1) - 1)
    def _():
        grad_key = grad_keys_t[...].T
        grad_ref[1] = (
            grad_key * cos_ref[...] - swap_halves(grad_key) * sin_ref[...]
        ).astype(BF16)
        grad_ref[2] = grad_values_t[...].T.astype(BF16)


def attend_back(
    place, queries, keys, values, mixed, upstream, logs, cosines, sines, pair, grads, block=512, chunk=512
):
    count, columns = queries.shape
    whole = pl.BlockSpec((count, LANES), lambda p, i, _: (0, pair))
    rows = pl.BlockSpec((block, LANES), lambda p, i, _: (i, pair))
    table = pl.BlockSpec((count, LANES), lambda p, i, _: (0, 0))
    table_rows = pl.BlockSpec((block, LANES), lambda p, i, _: (i, 0))
    held = [] if grads is None else [grads]
    return pl.pallas_call(
        functools.partial(attend_back_kernel, chunk=chunk),
        grid_spec=pltpu.PrefetchScalarGridSpec(
            num_scalar_prefetch=1,
            grid=(1, count // block),
            in_specs=[
                rows,
                whole,
                whole,
                rows,
                rows,
                pl.BlockSpec((1, 8, block), lambda p, i, _: (pair, 0, i)),
                table_rows,
                table_rows,
                table,
                table,
            ]
            + [pl.BlockSpec(memory_space=pl.ANY)] * len(held),
            out_specs=pl.BlockSpec((3, count, LANES), lambda p, i, _: (0, 0, pair)),
            scratch_shapes=[
                pltpu.VMEM((2, count, LANES), BF16),
                pltpu.VMEM((LANES, count), F32),
                pltpu.VMEM((LANES, count), F32),
            ],
        ),
        out_shape=jax.ShapeDtypeStruct((3, count, columns), BF16),
        input_output_aliases={11: 0} if held else {},
        cost_estimate=cost(28 * count * count * LANES, 16 * count * LANES, count * count * 2),
        compiler_params=pltpu.CompilerParams(vmem_limit_bytes=60 * MIB),
        name="attention_backward",
    )(place, queries, keys, values, mixed, upstream, logs, cosines, sines, cosines, sines, *held)


def feed_kernel(*refs, counts, chunk):
    row_pieces, target_pieces = refs[: counts[0]], refs[counts[0] : sum(counts)]
    refs = refs[sum(counts) :]
    gate_ref, up_ref, down_ref, inner_ref, grad_gate_ref, grad_up_ref = refs[:6]
    weight_gate_ref, weight_up_ref, weight_down_ref = refs[6:9]
    rows, row_sems, target, target_sems, rows_t, target_t = refs[9:]

    @pl.when(pl.program_id(0) == 0)
    def _():
        copies = fetch(row_pieces, rows, row_sems) + fetch(target_pieces, target, target_sems)
        for copy in copies:
            copy.wait()
        rows_t[...] = rows[...].T
        target_t[...] = target[...].T

    gate_weight, up_weight, down_weight = unpacked(gate_ref), unpacked(up_ref), unpacked(down_ref)
    for start in range(0, rows.shape[0], chunk):
        span = slice(start, start + chunk)
        gate = contract(rows[span, :], gate_weight, 1, 0)
        up = contract(rows[span, :], up_weight, 1, 0)
        grad_inner = contract(target[span, :], down_weight, 1, 1)
        share = jax.nn.sigmoid(gate)
        activated = gate * share
        inner_ref[span, :] = (activated * up).astype(BF16)
        grad_up_ref[span, :] = (grad_inner * activated).astype(BF16)
        grad_gate_ref[span, :] = (
            grad_inner * up * share * (1.0 + gate * (1.0 - share))
        ).astype(BF16)
    weight_gate_ref[...] = contract(rows_t[...], grad_gate_ref[...], 1, 0).astype(BF16)
    weight_up_ref[...] = contract(rows_t[...], grad_up_ref[...], 1, 0).astype(BF16)
    weight_down_ref[...] = contract(target_t[...], inner_ref[...], 1, 0).T.astype(BF16)


def feed(rows, target, weights, block=256, chunk=512):
    count = sum(piece.shape[0] for piece in rows)
    width = rows[0].shape[1]
    across_spec = lambda units: pl.BlockSpec((width, min(block, units)), lambda i: (0, i))
    down_spec = lambda units: pl.BlockSpec((min(block, units), width), lambda i: (i, 0))
    if packed(weights[0]):
        units = width
        replicas, deep = weights[0][0].shape[0], width // weights[0][0].shape[0]
        specs = [
            pl.BlockSpec((replicas, deep, block), lambda i, plane=weights[k][1]: (0, plane, i))
            for k in range(2)
        ] + [
            pl.BlockSpec(
                (block // deep, deep, width), lambda i, plane=weights[2][1]: (i, plane, 0)
            )
        ]
        weights = [weight for weight, _ in weights]
    else:
        units = weights[0].shape[1]
        specs = [across_spec(units)] * 2 + [down_spec(units)]
    block = min(block, units)
    out = pl.BlockSpec((count, block), lambda i: (0, i))
    return pl.pallas_call(
        functools.partial(feed_kernel, counts=(len(rows), len(target)), chunk=chunk),
        grid=(units // block,),
        in_specs=[pl.BlockSpec(memory_space=pl.ANY)] * (len(rows) + len(target)) + specs,
        out_specs=[out, out, out] + [across_spec(units)] * 2 + [down_spec(units)],
        out_shape=[jax.ShapeDtypeStruct((count, units), BF16)] * 3
        + [jax.ShapeDtypeStruct((width, units), BF16)] * 2
        + [jax.ShapeDtypeStruct((units, width), BF16)],
        scratch_shapes=room(rows) + room(target) + [pltpu.VMEM((width, count), BF16)] * 2,
        cost_estimate=cost(
            12 * count * width * units,
            4 * count * width + 12 * width * units + 6 * count * units,
            2 * count * units,
        ),
        compiler_params=pltpu.CompilerParams(vmem_limit_bytes=60 * MIB),
        name="feed_forward",
    )(*rows, *target, *weights)


def sum_kernel(*refs, places, dims, start, chunk):
    terms = len(dims)
    operands, out_ref = refs[: 2 * terms], refs[2 * terms]
    buffers = refs[2 * terms + 1 : 4 * terms + 1]
    total, result, sems, out_sems = refs[4 * terms + 1 :]
    rows = total.shape[0]
    copies = []
    for index, (ref, place) in enumerate(zip(operands, places)):
        copy = pltpu.make_async_copy(ref.at[place], buffers[index], sems.at[index])
        copy.start()
        copies.append(copy)
    sent = []
    for index, dim in enumerate(dims):
        copies[2 * index].wait()
        copies[2 * index + 1].wait()
        right = unpacked(buffers[2 * index + 1])
        for first in range(0, rows, chunk):
            span = slice(first, first + chunk)
            product = contract(buffers[2 * index][span, :], right, 1, dim)
            if index:
                product = total[span, :] + product
            if index + 1 < terms:
                total[span, :] = product
                continue
            result[span, :] = product.astype(result.dtype)
            copy = pltpu.make_async_copy(
                result.at[pl.ds(first, chunk), :],
                out_ref.at[pl.ds(first, chunk), :],
                out_sems.at[first // chunk],
            )
            copy.start()
            sent.append(copy)
    for copy in sent:
        copy.wait()


def sum_products(terms, start, rows, dtype=F32, chunk=256):
    chunk = min(chunk, rows)
    operands, places, shapes, dims, flops, moved = [], [], [], [], 0, 0
    for left, plane, right, part, dim in terms:
        depth = left.shape[-1]
        span = pl.ds(start, rows)
        places.append((span, slice(None)) if plane is None else (plane, span, slice(None)))
        shapes.append((rows, depth))
        if packed(right):
            right, plane = right
            width = right.shape[2]
            deep = width // right.shape[0]
            places.append((slice(None), pl.ds(plane * deep, deep), slice(None)))
            shapes.append((right.shape[0], deep, width))
        else:
            column = pl.ds(0, right.shape[1]) if part is None else pl.ds(part * depth, depth)
            places.append((slice(None), column))
            shapes.append((right.shape[0], column.size))
            width = shapes[-1][1 - dim]
        operands += [left, right]
        dims.append(dim)
        flops += 2 * rows * depth * width
        moved += 2 * rows * depth + 2 * depth * width
    anywhere = pl.BlockSpec(memory_space=pl.ANY)
    return pl.pallas_call(
        functools.partial(
            sum_kernel, places=places, dims=tuple(dims), start=start, chunk=chunk
        ),
        in_specs=[anywhere] * len(operands),
        out_specs=anywhere,
        out_shape=jax.ShapeDtypeStruct((rows, width), dtype),
        scratch_shapes=[pltpu.VMEM(shape, BF16) for shape in shapes]
        + [
            pltpu.VMEM((rows, width), F32),
            pltpu.VMEM((rows, width), dtype),
            pltpu.SemaphoreType.DMA((len(operands),)),
            pltpu.SemaphoreType.DMA((rows // chunk,)),
        ],
        cost_estimate=cost(flops, moved + 4 * rows * width),
        compiler_params=pltpu.CompilerParams(vmem_limit_bytes=58 * MIB),
        name="sum_products",
    )(*operands)


def outer_kernel(*refs, count):
    right_ref, out_ref, left, sems, left_t = refs[count:]

    @pl.when(pl.program_id(0) == 0)
    def _():
        for copy in fetch(refs[:count], left, sems):
            copy.wait()
        left_t[...] = left[...].T

    out_ref[...] = contract(left_t[...], right_ref[...], 1, 0).astype(BF16)


def outer(pieces, right):
    width = pieces[0].shape[1]
    planes, count, columns = right.shape
    return pl.pallas_call(
        functools.partial(outer_kernel, count=len(pieces)),
        grid=(planes,),
        in_specs=[pl.BlockSpec(memory_space=pl.ANY)] * len(pieces)
        + [pl.BlockSpec((None, count, columns), lambda i: (i, 0, 0))],
        out_specs=pl.BlockSpec((width, columns), lambda i: (0, i)),
        out_shape=jax.ShapeDtypeStruct((width, planes * columns), BF16),
        scratch_shapes=room(pieces) + [pltpu.VMEM((width, count), BF16)],
        cost_estimate=cost(
            2 * count * width * planes * columns,
            2 * count * (width + planes * columns) + 2 * width * planes * columns,
        ),
        compiler_params=pltpu.CompilerParams(vmem_limit_bytes=40 * MIB),
        name="outer_product",
    )(*pieces, right)


def branch_kernel(*refs, count, groups, chunk):
    weights = refs[count : count + groups]
    mixed = refs[count + groups : count + 2 * groups]
    outs = refs[count + 2 * groups : count + 4 * groups]
    rows, sems = refs[count + 4 * groups :]
    for copy in fetch(refs[:count], rows, sems):
        copy.wait()
    for index in range(groups):
        outs[groups + index][...] = contract(mixed[index][...].T, rows[...], 1, 0).astype(BF16)
        for start in range(0, rows.shape[0], chunk):
            span = slice(start, start + chunk)
            outs[index][span, :] = contract(rows[span, :], weights[index][...], 1, 1).astype(BF16)


def branch_back(pieces, weights, mixed, chunk=512):
    count = sum(piece.shape[0] for piece in pieces)
    width = pieces[0].shape[1]
    groups = len(weights)
    vmem = pl.BlockSpec(memory_space=pltpu.VMEM)
    columns = [weight.shape[0] for weight in weights]
    results = pl.pallas_call(
        functools.partial(branch_kernel, count=len(pieces), groups=groups, chunk=chunk),
        in_specs=[pl.BlockSpec(memory_space=pl.ANY)] * len(pieces) + [vmem] * (2 * groups),
        out_specs=[vmem] * (2 * groups),
        out_shape=[jax.ShapeDtypeStruct((count, size), BF16) for size in columns]
        + [jax.ShapeDtypeStruct((size, width), BF16) for size in columns],
        scratch_shapes=room(pieces),
        cost_estimate=cost(4 * count * width * sum(columns), 6 * count * width),
        compiler_params=pltpu.CompilerParams(vmem_limit_bytes=48 * MIB),
        name="branch_backward",
    )(*pieces, *weights, *mixed)
    return results[:groups], results[groups:]


def standardize(value):
    centred = value - jnp.mean(value, axis=-1, keepdims=True)
    scale = lax.rsqrt(jnp.mean(centred * centred, axis=-1, keepdims=True) + EPSILON)
    return centred * scale, scale


def norm_kernel(*refs, added):
    value = refs[0][...].astype(F32)
    for ref in refs[1 : 1 + added]:
        value = value + ref[...].astype(F32)
    gain_ref, shift_ref = refs[1 + added : 3 + added]
    standard, _ = standardize(value)
    if added:
        refs[-2][...] = value
    refs[-1][...] = (standard * gain_ref[...] + shift_ref[...]).astype(BF16)


def norm(base, terms, gain, shift, pieces=PIECES, block=256):
    count, width = base.shape
    rows = count // pieces
    block = min(block, rows)
    vector = pl.BlockSpec((1, width), lambda i: (0, 0))
    total, out = None, []
    for piece in range(pieces):
        first = piece * rows // block
        whole = pl.BlockSpec((block, width), lambda i, first=first: (first + i, 0))
        shapes = [jax.ShapeDtypeStruct((rows, width), BF16)]
        specs = [pl.BlockSpec((block, width), lambda i: (i, 0))]
        held = []
        if terms:
            shapes = [jax.ShapeDtypeStruct((count, width), F32)] + shapes
            specs = [whole] + specs
            held = [] if total is None else [total]
        results = pl.pallas_call(
            lambda *refs, held=len(held): norm_kernel(
                *refs[: 3 + len(terms)], *refs[3 + len(terms) + held :], added=len(terms)
            ),
            grid=(rows // block,),
            in_specs=[whole] * (1 + len(terms))
            + [vector, vector]
            + [pl.BlockSpec(memory_space=pl.ANY)] * len(held),
            out_specs=specs,
            out_shape=shapes,
            input_output_aliases={3 + len(terms): 0} if held else {},
            cost_estimate=cost(16 * rows * width, 8 * rows * width * len(shapes)),
            name="layer_norm",
        )(base, *terms, gain.reshape(1, width), shift.reshape(1, width), *held)
        out.append(results[-1])
        if terms:
            total = results[0]
    return total, out


def norm_back_kernel(*refs, added, low):
    base_ref, straight_ref, gain_ref = refs[:3]
    upstream = refs[3][...].astype(F32)
    for ref in refs[4 : 3 + added]:
        upstream = upstream + ref[...].astype(F32)
    outs = refs[3 + added :]
    standard, scale = standardize(base_ref[...].astype(F32))
    scaled = upstream * gain_ref[...]
    back = straight_ref[...].astype(F32) + scale * (
        scaled
        - jnp.mean(scaled, axis=-1, keepdims=True)
        - standard * jnp.mean(scaled * standard, axis=-1, keepdims=True)
    )
    outs[0][...] = back.astype(BF16)
    if not low:
        outs[1][...] = back
    sums = jnp.concatenate(
        [
            jnp.sum(upstream * standard, axis=0, keepdims=True),
            jnp.sum(upstream, axis=0, keepdims=True),
        ],
        axis=0,
    )

    @pl.when(pl.program_id(0) == 0)
    def _():
        outs[-1][...] = sums

    @pl.when(pl.program_id(0) > 0)
    def _():
        outs[-1][...] += sums


def norm_back(base, straight, gain, terms, low, pieces=PIECES, block=256):
    count, width = base.shape
    rows = count // pieces
    block = min(block, rows)
    total, out, found = None, [], []
    for piece in range(pieces):
        first = piece * rows // block
        whole = pl.BlockSpec((block, width), lambda i, first=first: (first + i, 0))
        shapes = [jax.ShapeDtypeStruct((rows, width), BF16)]
        specs = [pl.BlockSpec((block, width), lambda i: (i, 0))]
        held = []
        if not low:
            shapes.append(jax.ShapeDtypeStruct((count, width), F32))
            specs.append(whole)
            held = [] if total is None else [total]
        results = pl.pallas_call(
            lambda *refs, held=len(held): norm_back_kernel(
                *refs[: 3 + len(terms)],
                *refs[3 + len(terms) + held :],
                added=len(terms),
                low=low,
            ),
            grid=(rows // block,),
            in_specs=[whole, whole, pl.BlockSpec((1, width), lambda i: (0, 0))]
            + [whole] * len(terms)
            + [pl.BlockSpec(memory_space=pl.ANY)] * len(held),
            out_specs=specs + [pl.BlockSpec((2, width), lambda i: (0, 0))],
            out_shape=shapes + [jax.ShapeDtypeStruct((2, width), F32)],
            input_output_aliases={3 + len(terms): 1} if held else {},
            cost_estimate=cost(30 * rows * width, 16 * rows * width),
            name="layer_norm_backward",
        )(base, straight, gain.reshape(1, width), *terms, *held)
        out.append(results[0])
        found.append(results[-1])
        if not low:
            total = results[1]
    return out, total, sum(found)


def rope_tables(offset):
    half = HD // 2
    groups = LANES // half
    count = LEN // groups
    lane = jnp.arange(LANES, dtype=jnp.int32)
    position = jnp.arange(count, dtype=jnp.int32)[:, None] + lane[None, :] // half * count
    position = (position + offset) % LEN
    inverse = 10000.0 ** (-2.0 * (lane % half).astype(F32) / HD)
    angles = position.astype(F32) * inverse[None, :]
    cosines, sines = lax.optimization_barrier((jnp.cos(angles), jnp.sin(angles)))

    def rows(table, signs):
        parts = [table[:, g * half : (g + 1) * half] for g in range(groups)]
        return jnp.concatenate(
            [jnp.concatenate([sign * part for sign in signs], axis=1) for part in parts], axis=0
        )

    return rows(cosines, (1, 1, 1, 1)), rows(sines, (-1, 1, -1, 1))


def exchanges(axis, size):
    if size & (size - 1):
        return [lambda value: lax.psum(value, axis)]
    return [
        lambda value, pairs=[(i, i ^ (1 << bit)) for i in range(size)]: value
        + lax.ppermute(value, axis, pairs)
        for bit in range(size.bit_length() - 1)
    ]


def shards(
    dp_size,
    tensor_size,
    tokens,
    lengths,
    gain_first,
    shift_first,
    query_weight,
    key_weight,
    value_weight,
    output_weight,
    gain_second,
    shift_second,
    gate_weight,
    up_weight,
    down_weight,
    cotangent,
):
    windows = lengths.shape[0]
    span = tensor_size // windows
    held = tokens.shape[0]
    width = tokens.shape[1]
    head_cols = query_weight.shape[1]
    here = lax.axis_index("tensor")
    window, seat = here // span, here % span

    def from_seat(value, shift):
        pairs = [
            (w * span + (s + shift) % span, w * span + s)
            for w in range(windows)
            for s in range(span)
        ]
        return lax.ppermute(value, "tensor", pairs)

    def to_seat(value, shift):
        return from_seat(value, span - shift)

    def from_window(value, shift):
        pairs = [((t + shift * span) % tensor_size, t) for t in range(tensor_size)]
        return lax.ppermute(value, "tensor", pairs)

    def to_window(value, shift):
        return from_window(value, windows - shift)

    def gather_rows(value):
        return value + [from_seat(piece, s) for s in range(1, span) for piece in value]

    def scatter(partial):
        sent = [to_seat(partial(s * held, held), s) for s in range(1, span)]
        return [partial(0, held)] + sent

    def all_windows(value):
        return [value] + [from_window(value, shift) for shift in range(1, windows)]

    def spread_windows(values):
        group = lax.axis_index("dp")
        sizes = [value.shape[0] // dp_size for value in values]
        mine = jnp.concatenate(
            [
                lax.dynamic_slice_in_dim(value, group * size, size, axis=0).reshape(-1, width)
                for value, size in zip(values, sizes)
            ],
            axis=0,
        )
        return [mine], [from_window(mine, shift) for shift in range(1, windows)]

    def gather_spread(values, piece):
        gathered = lax.all_gather(piece, "dp", axis=0)
        if all(value.shape == (width, width) for value in values):
            return [(gathered, plane) for plane in range(len(values))]
        out, start = [], 0
        for value in values:
            count = value.size // width // dp_size
            out.append(gathered[:, start : start + count].reshape(value.shape))
            start += count
        return out

    def after(value, *others):
        return lax.optimization_barrier((value, *others))[0]

    def pieces_after(pieces, *others):
        return [after(pieces[0], *others)] + pieces[1:]

    place = jnp.stack(
        [lax.dynamic_index_in_dim(lengths, window, keepdims=False), seat * held]
    ).astype(jnp.int32)
    cosines, sines = rope_tables(seat * held)

    members = [[s] for s in range(windows)] if head_cols % LANES == 0 else [list(range(windows))]
    feed_weights = [gate_weight, up_weight, down_weight]
    slices_sent, slices = spread_windows(feed_weights)
    _, normed_one = norm(after(tokens, *slices_sent), [], gain_first, shift_first)
    full_one = gather_rows(normed_one)
    qkv_own = jnp.concatenate([query_weight, key_weight, value_weight], axis=1)
    qkv_other = all_windows(after(qkv_own, *slices))[1:]
    qkv_shards = [qkv_own] + qkv_other
    def joined(parts, axis):
        return parts[0] if len(parts) == 1 else jnp.concatenate(parts, axis=axis)

    def part_of(value, part):
        return value[:, part * head_cols : (part + 1) * head_cols]

    qkv_weights = [
        qkv_shards[group[0]]
        if len(group) == 1
        else joined([part_of(qkv_shards[s], part) for part in range(3) for s in group], 1)
        for group in members
    ]
    target = gather_rows([cotangent])
    qkv, attended = [], []
    rows_one = full_one
    for weight in qkv_weights:
        parts = project(rows_one, weight, cosines, sines)
        if not qkv:
            slices = [after(piece, parts[0]) for piece in slices]
            feed_shards = [feed_weights]
            feed_shards += [gather_spread(feed_weights, piece) for piece in slices]
        waits = slices if not qkv else target
        qkv.append((after(parts[0], *waits), *parts[1:]))
        attended.append(attend(place, *qkv[-1]))
        if len(attended) == 1:
            sent = after(output_weight, attended[0][0])
            output_shards = [output_weight] + all_windows(sent)[1:]
        rows_one = pieces_after(full_one, attended[-1][0])

    out_weights = [joined([output_shards[s] for s in group], 0) for group in members]
    mixer_terms = [
        (mixed, None, weight, None, 0) for (mixed, _), weight in zip(attended, out_weights)
    ]
    hidden_one, normed_two = norm(
        tokens,
        scatter(lambda start, rows: sum_products(mixer_terms, start, rows)),
        gain_second,
        shift_second,
    )
    full_two = gather_rows(normed_two)

    flip = [(d, d ^ 1) for d in range(dp_size)]
    odd = lax.axis_index("dp") % 2

    def half(value, which):
        count = value.shape[0] // 2
        return lax.dynamic_slice_in_dim(value, which * count, count, axis=0)

    def total(pieces, which):
        return sum(half(piece, which).astype(F32) for piece in pieces).astype(BF16)

    def swap_half(pieces, *others):
        pieces = [after(piece, *others) for piece in pieces]
        mine, sent = total(pieces, odd), total(pieces, 1 - odd)
        return (mine, lax.ppermute(sent, "dp", flip)), [mine, sent]

    def add_half(halves, *others):
        mine, received = (after(value, *others) for value in halves)
        return (mine.astype(F32) + received.astype(F32)).astype(BF16)

    def sum_half(value, turn):
        groups = [list(range(0, dp_size, 2)), list(range(1, dp_size, 2))]
        if turn & 1:
            groups = groups[::-1]
        if turn & 2:
            groups = [group[::-1] for group in groups]
        return lax.psum(value, "dp", axis_index_groups=groups)

    def swap_sum(mine, *others):
        mine = after(mine, *others)
        return mine, lax.ppermute(mine, "dp", flip)

    def whole_sum(halves, *others):
        mine, received = (after(value, *others) for value in halves)
        first, second = jnp.where(odd == 0, mine, received), jnp.where(odd == 0, received, mine)
        return jnp.concatenate([first, second], axis=0).astype(F32)

    def send_to_owner(parts):
        return [to_window(parts[shift], shift) for shift in range(1, windows)]

    order = list(range(1, windows)) + [0]
    fed = {}
    rows_two = full_two
    for s in order:
        fed[s] = feed(rows_two, target, feed_shards[s])
        rows_two = pieces_after(full_two, fed[s][0])
    down_pieces, up_pieces, gate_pieces = (
        send_to_owner({s: fed[s][k] for s in order}) + [fed[0][k]] for k in (5, 4, 3)
    )
    two_terms, feed_terms = [], []
    for s in order:
        gate, up, down = feed_shards[s]
        two_terms += [(fed[s][1], None, gate, None, 1), (fed[s][2], None, up, None, 1)]
        feed_terms.append((fed[s][0], None, down, None, 0))

    two_sent = [
        sum_products(two_terms, shift * held, held, BF16) for shift in range(1, span)
    ]
    down_half, marks = swap_half(down_pieces, *two_sent)
    two_terms = [(after(two_terms[0][0], *marks), *two_terms[0][1:])] + two_terms[1:]
    two_kept = sum_products(two_terms, 0, held)
    grad_branch_own, grad_hidden, norm_two = norm_back(
        hidden_one,
        cotangent,
        gain_second,
        [two_kept] + [to_seat(part, shift + 1) for shift, part in enumerate(two_sent)],
        False,
    )
    grad_branch = gather_rows(grad_branch_own)
    down_half = add_half(down_half, *grad_branch_own)
    down_sum = sum_half(down_half, 0)
    grad_branch = pieces_after(grad_branch, down_half)

    members = members[::-1]
    out_weights, qkv_weights = out_weights[::-1], qkv_weights[::-1]
    qkv, attended = qkv[::-1], attended[::-1]
    grad_mixed, found = branch_back(grad_branch, out_weights, [mixed for mixed, _ in attended])
    out_grads = {
        s: out_grad[spot * head_cols : (spot + 1) * head_cols]
        for group, out_grad in zip(members, found)
        for spot, s in enumerate(group)
    }
    out_pieces = send_to_owner(out_grads) + [out_grads[0]]

    def up_swap(last):
        sums["up"], waits = swap_half(up_pieces, *last)
        return waits

    def up_sum(last):
        value = add_half(sums["up"], *last)
        sums["up"] = sum_half(value, 1)
        return [value]

    def gate_swap(last):
        sums["gate"], waits = swap_half(gate_pieces, *last)
        sums["out"], more = swap_half(out_pieces, *last)
        sums["down"] = after(down_sum, *waits, *more)
        return waits + more + [sums["down"]]

    def gate_sum(last):
        values = add_half(sums["gate"], *last), add_half(sums["out"], *last)
        sums["gate"], sums["out"] = sum_half(values, 2)
        sums["up"] = swap_sum(sums["up"], *last)
        return [*values, sums["up"][0]]

    across, along = (exchanges(axis, size) for axis, size in (("tensor", tensor_size), ("dp", dp_size)))
    norm_steps = across + along[1:]
    sums = {}
    moves = [up_swap, up_sum, gate_swap, gate_sum]
    last = list(grad_mixed)
    grad_qkv, qkv_grads = [], {}
    for index, group in enumerate(members):
        mixed, logs = attended[index]
        count = len(group) * head_cols
        grads = None
        for pair in range(count // LANES):
            waits = moves.pop(0)(last) if moves else last
            if norm_steps:
                norm_two = norm_steps.pop(0)(after(norm_two, *last))
                waits = waits + [norm_two]
            grads = attend_back(
                place,
                *qkv[index],
                mixed,
                after(grad_mixed[index], *waits),
                logs,
                cosines,
                sines,
                pair,
                grads,
            )
            last = [grads]
        grad_qkv.append(grads)
        qkv_grad = outer(full_one, grads)
        last = [qkv_grad]
        for spot, s in enumerate(group):
            if len(group) == 1:
                qkv_grads[s] = qkv_grad
            else:
                qkv_grads[s] = joined(
                    [
                        lax.slice_in_dim(
                            qkv_grad,
                            part * count + spot * head_cols,
                            part * count + (spot + 1) * head_cols,
                            axis=1,
                        )
                        for part in range(3)
                    ],
                    1,
                )
    for move in moves:
        last = move(last)

    qkv_half, marks = swap_half(send_to_owner(qkv_grads) + [qkv_grads[0]])
    grad_up = whole_sum(sums["up"], *marks)
    down_halves = swap_sum(sums["down"], *marks)
    feed_terms[0] = (after(feed_terms[0][0], grad_up, down_halves[0]), *feed_terms[0][1:])
    one_terms = [
        (grad_qkv[index], part, weight, part, 1)
        for index, weight in enumerate(qkv_weights)
        for part in range(3)
    ]

    def later(terms, *others):
        return [(after(terms[0][0], *others), *terms[0][1:])] + terms[1:]

    shifts = range(1, span)
    feed_sent = [sum_products(feed_terms, shift * held, held, BF16) for shift in shifts]
    qkv_half = add_half(qkv_half, *feed_sent)
    gate_halves = swap_sum(sums["gate"], *feed_sent)
    out_halves = swap_sum(sums["out"], *feed_sent)
    qkv_sum = sum_half(after(qkv_half, gate_halves[0], out_halves[0]), 3)
    one_terms = later(one_terms, qkv_half, gate_halves[0])
    one_sent = [sum_products(one_terms, shift * held, held, BF16) for shift in shifts]
    feed_parts = [sum_products(later(feed_terms, *one_sent), 0, held)]
    one_parts = [sum_products(later(one_terms, feed_parts[0]), 0, held)]
    feed_parts += [to_seat(part, shift) for shift, part in zip(shifts, feed_sent)]
    one_parts += [to_seat(part, shift) for shift, part in zip(shifts, one_sent)]
    output = (hidden_one + sum(feed_parts)).astype(BF16)
    (input_grad,), _, norm_one = norm_back(tokens, grad_hidden, gain_first, one_parts, True, 1)
    for step in norm_steps:
        norm_two = step(norm_two)
    window = [input_grad, output]
    qkv_halves = swap_sum(qkv_sum, *window)
    norm_one = after(norm_one, qkv_halves[0])
    for step in across + along[1:]:
        norm_one = step(norm_one)
    norms = along[0](jnp.concatenate([norm_one, norm_two], axis=0))
    norm_one, norm_two = norms[:2], norms[2:]
    grad_down = whole_sum(down_halves, qkv_halves[0])
    grad_gate = whole_sum(gate_halves, qkv_halves[0])
    out_grad = whole_sum(out_halves, qkv_halves[0])
    qkv_grad = whole_sum(qkv_halves)
    return (
        output,
        input_grad,
        *(part_of(qkv_grad, part) for part in range(3)),
        out_grad,
        grad_gate,
        grad_up,
        grad_down,
        norm_one[0],
        norm_one[1],
        norm_two[0],
        norm_two[1],
    )


def solution(mesh):
    rows = P(("dp", "tensor"), None)
    columns = P(None, "tensor")
    depth = P("tensor", None)
    return jax.shard_map(
        functools.partial(shards, mesh.shape["dp"], mesh.shape["tensor"]),
        mesh=mesh,
        in_specs=(
            rows,
            P("dp"),
            P(),
            P(),
            columns,
            columns,
            columns,
            depth,
            P(),
            P(),
            columns,
            columns,
            depth,
            rows,
        ),
        out_specs=(
            rows,
            rows,
            columns,
            columns,
            columns,
            depth,
            columns,
            columns,
            depth,
            P(),
            P(),
            P(),
            P(),
        ),
        check_vma=False,
    )
```

```python
import functools
import math

import jax
import jax.numpy as jnp
from jax import lax
from jax.experimental import pallas as pl
from jax.experimental.pallas import tpu as pltpu
from jax.sharding import PartitionSpec as P

HD = 64
LEN = 2048
EPSILON = 1e-05
MASKED = -1e30
LANES = 128
LOG2E = math.log2(math.e)
BF16 = jnp.bfloat16
F32 = jnp.float32
MIB = 1 << 20
COST_SHARE = 0.01
PIECES = 2


def contract(left, right, left_dim, right_dim):
    return lax.dot_general(
        left, right, (((left_dim,), (right_dim,)), ((), ())), preferred_element_type=F32
    )


def cost(flops, moved, transcendentals=0):
    return pl.CostEstimate(
        flops=int(flops * COST_SHARE),
        bytes_accessed=int(moved * COST_SHARE),
        transcendentals=int(transcendentals * COST_SHARE),
    )


def swap_halves(value):
    columns = value.shape[1]
    lane = lax.broadcasted_iota(jnp.int32, value.shape, 1)
    return jnp.where(
        lane % HD < HD // 2,
        pltpu.roll(value, columns - HD // 2, 1),
        pltpu.roll(value, HD // 2, 1),
    )


def fetch(pieces, rows, sems):
    copies, start = [], 0
    for index, piece in enumerate(pieces):
        count = piece.shape[0]
        copies.append(
            pltpu.make_async_copy(piece, rows.at[pl.ds(start, count), :], sems.at[index])
        )
        start += count
    for copy in copies:
        copy.start()
    return copies


def room(pieces):
    count = sum(piece.shape[0] for piece in pieces)
    return [
        pltpu.VMEM((count, pieces[0].shape[1]), BF16),
        pltpu.SemaphoreType.DMA((len(pieces),)),
    ]


def unpacked(ref):
    value = ref[...]
    return value.reshape(-1, value.shape[-1]) if value.ndim == 3 else value


def packed(weight):
    return isinstance(weight, tuple)


def project_kernel(*refs, count):
    pieces = refs[:count]
    weight_ref, cos_ref, sin_ref, q_ref, k_ref, v_ref, rows, sems = refs[count:]
    columns = q_ref.shape[1]
    block = q_ref.shape[0]

    @pl.when(pl.program_id(0) == 0)
    def _():
        for copy in fetch(pieces, rows, sems):
            copy.wait()

    start = pl.multiple_of(pl.program_id(0) * block, block)
    product = contract(rows[pl.ds(start, block), :], weight_ref[...], 1, 0)
    cosines = jnp.concatenate([cos_ref[...]] * (columns // LANES), axis=1)
    sines = jnp.concatenate([sin_ref[...]] * (columns // LANES), axis=1)
    for part, out_ref in ((0, q_ref), (1, k_ref)):
        value = product[:, part * columns : (part + 1) * columns]
        out_ref[...] = (value * cosines + swap_halves(value) * sines).astype(BF16)
    v_ref[...] = product[:, 2 * columns :].astype(BF16)


def project(pieces, weight, cosines, sines, block=512):
    width = weight.shape[0]
    columns = weight.shape[1] // 3
    count = sum(piece.shape[0] for piece in pieces)
    table = pl.BlockSpec((block, LANES), lambda i: (i, 0))
    out = pl.BlockSpec((block, columns), lambda i: (i, 0))
    return pl.pallas_call(
        functools.partial(project_kernel, count=len(pieces)),
        grid=(count // block,),
        in_specs=[pl.BlockSpec(memory_space=pl.ANY)] * len(pieces)
        + [pl.BlockSpec(weight.shape, lambda i: (0, 0)), table, table],
        out_specs=[out, out, out],
        out_shape=[jax.ShapeDtypeStruct((count, columns), BF16)] * 3,
        scratch_shapes=room(pieces),
        cost_estimate=cost(
            2 * count * width * 3 * columns,
            2 * (count * width + width * 3 * columns + count * 3 * columns),
        ),
        compiler_params=pltpu.CompilerParams(vmem_limit_bytes=40 * MIB),
        name="project_rope",
    )(*pieces, weight, cosines, sines)


def masked_keys(place_ref, key_ref, masked_ref):
    count = key_ref.shape[0]
    lane = lax.broadcasted_iota(jnp.int32, (count, LANES), 1)
    row = lax.broadcasted_iota(jnp.int32, (count, LANES), 0) + place_ref[1]
    position = jnp.where(row >= count, row - count, row)
    bias = jnp.where(position >= place_ref[0], MASKED, 0.0).astype(BF16)
    nothing = jnp.zeros_like(bias)
    key = key_ref[...]
    masked_ref[0] = jnp.where(lane < HD, key, jnp.where(lane == HD, bias, nothing))
    masked_ref[1] = jnp.where(lane >= HD, key, jnp.where(lane == 0, bias, nothing))


def masked_queries(query):
    lane = lax.broadcasted_iota(jnp.int32, query.shape, 1)
    scaled = query * jnp.asarray(1.0 / math.sqrt(HD), BF16)
    one = jnp.ones_like(query)
    nothing = jnp.zeros_like(query)
    return (
        scaled,
        jnp.where(lane < HD, scaled, jnp.where(lane == HD, one, nothing)),
        jnp.where(lane >= HD, scaled, jnp.where(lane == 0, one, nothing)),
    )


def attend_kernel(place_ref, q_ref, k_ref, v_ref, out_ref, log_ref, keys, values_t, *, chunk):
    count = k_ref.shape[0]

    @pl.when(pl.program_id(1) == 0)
    def _():
        masked_keys(place_ref, k_ref, keys)
        values_t[...] = v_ref[...].T

    queries = masked_queries(q_ref[...])[1:]
    mixed, logs = [], []
    for head in range(2):
        scores = [
            contract(keys[head, start : start + chunk, :], queries[head], 1, 1)
            for start in range(0, count, chunk)
        ]
        top = functools.reduce(
            jnp.maximum, [jnp.max(block, axis=0, keepdims=True) for block in scores]
        )
        total = 0.0
        summed = 0.0
        for index, block in enumerate(scores):
            weights = jnp.exp2((block - top) * LOG2E)
            total = total + jnp.sum(weights, axis=0, keepdims=True)
            value = values_t[
                head * HD : (head + 1) * HD, index * chunk : (index + 1) * chunk
            ]
            summed = summed + contract(value, weights.astype(BF16), 1, 0)
        mixed.append(summed / total)
        logs.append(top * LOG2E + jnp.log2(total))
    out_ref[...] = jnp.concatenate(mixed, axis=0).T.astype(BF16)
    log_ref[0] = jnp.concatenate(logs + [jnp.zeros((6, q_ref.shape[0]), F32)], axis=0)


def attend(place, queries, keys, values, block=1024, chunk=512):
    count, columns = queries.shape
    pairs = columns // LANES
    whole = pl.BlockSpec((count, LANES), lambda p, i, _: (0, p))
    rows = pl.BlockSpec((block, LANES), lambda p, i, _: (i, p))
    return pl.pallas_call(
        functools.partial(attend_kernel, chunk=chunk),
        grid_spec=pltpu.PrefetchScalarGridSpec(
            num_scalar_prefetch=1,
            grid=(pairs, count // block),
            in_specs=[rows, whole, whole],
            out_specs=[rows, pl.BlockSpec((1, 8, block), lambda p, i, _: (p, 0, i))],
            scratch_shapes=[
                pltpu.VMEM((2, count, LANES), BF16),
                pltpu.VMEM((LANES, count), BF16),
            ],
        ),
        out_shape=[
            jax.ShapeDtypeStruct((count, columns), BF16),
            jax.ShapeDtypeStruct((pairs, 8, count), F32),
        ],
        cost_estimate=cost(16 * count * count * columns, 8 * count * columns, count * count * columns // HD),
        compiler_params=pltpu.CompilerParams(vmem_limit_bytes=56 * MIB),
        name="attention_forward",
    )(place, queries, keys, values)


def attend_back_kernel(
    place_ref,
    q_ref,
    k_ref,
    v_ref,
    out_ref,
    up_ref,
    log_ref,
    cos_row_ref,
    sin_row_ref,
    cos_ref,
    sin_ref,
    *rest,
    chunk,
):
    grad_ref, keys, grad_keys_t, grad_values_t = rest[-4:]
    count = k_ref.shape[0]
    step = pl.program_id(1)

    @pl.when(step == 0)
    def _():
        masked_keys(place_ref, k_ref, keys)
        grad_keys_t[...] = jnp.zeros_like(grad_keys_t)
        grad_values_t[...] = jnp.zeros_like(grad_values_t)

    scaled, *queries = masked_queries(q_ref[...])
    upstream = up_ref[...]
    lane = lax.broadcasted_iota(jnp.int32, upstream.shape, 1)
    nothing = jnp.zeros_like(upstream)
    products = upstream.astype(F32) * out_ref[...].astype(F32)
    scaled_t = scaled.T
    upstream_t = upstream.T
    logs = log_ref[0].T
    grad_queries = []
    for head in range(2):
        mine = (lane < HD) == (head == 0)
        own_upstream = jnp.where(mine, upstream, nothing)
        row_dot = jnp.sum(jnp.where(mine, products, 0.0), axis=1, keepdims=True)
        log_total = logs[:, head : head + 1]
        heads = slice(head * HD, (head + 1) * HD)
        grad_query = 0.0
        for start in range(0, count, chunk):
            span = slice(start, start + chunk)
            scores = contract(queries[head], keys[head, span, :], 1, 1)
            probs = jnp.exp2(scores * LOG2E - log_total)
            grad_probs = contract(own_upstream, v_ref[span, :], 1, 1)
            grad_scores = (probs * (grad_probs - row_dot)).astype(BF16)
            grad_values_t[heads, span] += contract(
                upstream_t[heads, :], probs.astype(BF16), 1, 0
            )
            grad_keys_t[heads, span] += contract(scaled_t[heads, :], grad_scores, 1, 0)
            grad_query = grad_query + contract(grad_scores, k_ref[span, :], 1, 0)
        grad_queries.append(grad_query)
    grad_query = jnp.where(lane < HD, *grad_queries) * (1.0 / math.sqrt(HD))
    block = grad_query.shape[0]
    grad_ref[0, pl.ds(pl.multiple_of(step * block, block), block), :] = (
        grad_query * cos_row_ref[...] - swap_halves(grad_query) * sin_row_ref[...]
    ).astype(BF16)

    @pl.when(step == pl.num_programs(1) - 1)
    def _():
        grad_key = grad_keys_t[...].T
        grad_ref[1] = (
            grad_key * cos_ref[...] - swap_halves(grad_key) * sin_ref[...]
        ).astype(BF16)
        grad_ref[2] = grad_values_t[...].T.astype(BF16)


def attend_back(
    place, queries, keys, values, mixed, upstream, logs, cosines, sines, pair, grads, block=512, chunk=512
):
    count, columns = queries.shape
    whole = pl.BlockSpec((count, LANES), lambda p, i, _: (0, pair))
    rows = pl.BlockSpec((block, LANES), lambda p, i, _: (i, pair))
    table = pl.BlockSpec((count, LANES), lambda p, i, _: (0, 0))
    table_rows = pl.BlockSpec((block, LANES), lambda p, i, _: (i, 0))
    held = [] if grads is None else [grads]
    return pl.pallas_call(
        functools.partial(attend_back_kernel, chunk=chunk),
        grid_spec=pltpu.PrefetchScalarGridSpec(
            num_scalar_prefetch=1,
            grid=(1, count // block),
            in_specs=[
                rows,
                whole,
                whole,
                rows,
                rows,
                pl.BlockSpec((1, 8, block), lambda p, i, _: (pair, 0, i)),
                table_rows,
                table_rows,
                table,
                table,
            ]
            + [pl.BlockSpec(memory_space=pl.ANY)] * len(held),
            out_specs=pl.BlockSpec((3, count, LANES), lambda p, i, _: (0, 0, pair)),
            scratch_shapes=[
                pltpu.VMEM((2, count, LANES), BF16),
                pltpu.VMEM((LANES, count), F32),
                pltpu.VMEM((LANES, count), F32),
            ],
        ),
        out_shape=jax.ShapeDtypeStruct((3, count, columns), BF16),
        input_output_aliases={11: 0} if held else {},
        cost_estimate=cost(28 * count * count * LANES, 16 * count * LANES, count * count * 2),
        compiler_params=pltpu.CompilerParams(vmem_limit_bytes=60 * MIB),
        name="attention_backward",
    )(place, queries, keys, values, mixed, upstream, logs, cosines, sines, cosines, sines, *held)


def feed_kernel(*refs, counts, chunk):
    row_pieces, target_pieces = refs[: counts[0]], refs[counts[0] : sum(counts)]
    refs = refs[sum(counts) :]
    gate_ref, up_ref, down_ref, inner_ref, grad_gate_ref, grad_up_ref = refs[:6]
    weight_gate_ref, weight_up_ref, weight_down_ref = refs[6:9]
    rows, row_sems, target, target_sems, rows_t, target_t = refs[9:]

    @pl.when(pl.program_id(0) == 0)
    def _():
        copies = fetch(row_pieces, rows, row_sems) + fetch(target_pieces, target, target_sems)
        for copy in copies:
            copy.wait()
        rows_t[...] = rows[...].T
        target_t[...] = target[...].T

    gate_weight, up_weight, down_weight = unpacked(gate_ref), unpacked(up_ref), unpacked(down_ref)
    for start in range(0, rows.shape[0], chunk):
        span = slice(start, start + chunk)
        gate = contract(rows[span, :], gate_weight, 1, 0)
        up = contract(rows[span, :], up_weight, 1, 0)
        grad_inner = contract(target[span, :], down_weight, 1, 1)
        share = jax.nn.sigmoid(gate)
        activated = gate * share
        inner_ref[span, :] = (activated * up).astype(BF16)
        grad_up_ref[span, :] = (grad_inner * activated).astype(BF16)
        grad_gate_ref[span, :] = (
            grad_inner * up * share * (1.0 + gate * (1.0 - share))
        ).astype(BF16)
    weight_gate_ref[...] = contract(rows_t[...], grad_gate_ref[...], 1, 0).astype(BF16)
    weight_up_ref[...] = contract(rows_t[...], grad_up_ref[...], 1, 0).astype(BF16)
    weight_down_ref[...] = contract(target_t[...], inner_ref[...], 1, 0).T.astype(BF16)


def feed(rows, target, weights, block=256, chunk=512):
    count = sum(piece.shape[0] for piece in rows)
    width = rows[0].shape[1]
    across_spec = lambda units: pl.BlockSpec((width, min(block, units)), lambda i: (0, i))
    down_spec = lambda units: pl.BlockSpec((min(block, units), width), lambda i: (i, 0))
    if packed(weights[0]):
        units = width
        replicas, deep = weights[0][0].shape[0], width // weights[0][0].shape[0]
        specs = [
            pl.BlockSpec((replicas, deep, block), lambda i, plane=weights[k][1]: (0, plane, i))
            for k in range(2)
        ] + [
            pl.BlockSpec(
                (block // deep, deep, width), lambda i, plane=weights[2][1]: (i, plane, 0)
            )
        ]
        weights = [weight for weight, _ in weights]
    else:
        units = weights[0].shape[1]
        specs = [across_spec(units)] * 2 + [down_spec(units)]
    block = min(block, units)
    out = pl.BlockSpec((count, block), lambda i: (0, i))
    return pl.pallas_call(
        functools.partial(feed_kernel, counts=(len(rows), len(target)), chunk=chunk),
        grid=(units // block,),
        in_specs=[pl.BlockSpec(memory_space=pl.ANY)] * (len(rows) + len(target)) + specs,
        out_specs=[out, out, out] + [across_spec(units)] * 2 + [down_spec(units)],
        out_shape=[jax.ShapeDtypeStruct((count, units), BF16)] * 3
        + [jax.ShapeDtypeStruct((width, units), BF16)] * 2
        + [jax.ShapeDtypeStruct((units, width), BF16)],
        scratch_shapes=room(rows) + room(target) + [pltpu.VMEM((width, count), BF16)] * 2,
        cost_estimate=cost(
            12 * count * width * units,
            4 * count * width + 12 * width * units + 6 * count * units,
            2 * count * units,
        ),
        compiler_params=pltpu.CompilerParams(vmem_limit_bytes=60 * MIB),
        name="feed_forward",
    )(*rows, *target, *weights)


def sum_kernel(*refs, places, dims, start, chunk):
    terms = len(dims)
    operands, out_ref = refs[: 2 * terms], refs[2 * terms]
    buffers = refs[2 * terms + 1 : 4 * terms + 1]
    total, result, sems, out_sems = refs[4 * terms + 1 :]
    rows = total.shape[0]
    copies = []
    for index, (ref, place) in enumerate(zip(operands, places)):
        copy = pltpu.make_async_copy(ref.at[place], buffers[index], sems.at[index])
        copy.start()
        copies.append(copy)
    sent = []
    for index, dim in enumerate(dims):
        copies[2 * index].wait()
        copies[2 * index + 1].wait()
        right = unpacked(buffers[2 * index + 1])
        for first in range(0, rows, chunk):
            span = slice(first, first + chunk)
            product = contract(buffers[2 * index][span, :], right, 1, dim)
            if index:
                product = total[span, :] + product
            if index + 1 < terms:
                total[span, :] = product
                continue
            result[span, :] = product.astype(result.dtype)
            copy = pltpu.make_async_copy(
                result.at[pl.ds(first, chunk), :],
                out_ref.at[pl.ds(first, chunk), :],
                out_sems.at[first // chunk],
            )
            copy.start()
            sent.append(copy)
    for copy in sent:
        copy.wait()


def sum_products(terms, start, rows, dtype=F32, chunk=256):
    chunk = min(chunk, rows)
    operands, places, shapes, dims, flops, moved = [], [], [], [], 0, 0
    for left, plane, right, part, dim in terms:
        depth = left.shape[-1]
        span = pl.ds(start, rows)
        places.append((span, slice(None)) if plane is None else (plane, span, slice(None)))
        shapes.append((rows, depth))
        if packed(right):
            right, plane = right
            width = right.shape[2]
            deep = width // right.shape[0]
            places.append((slice(None), pl.ds(plane * deep, deep), slice(None)))
            shapes.append((right.shape[0], deep, width))
        else:
            column = pl.ds(0, right.shape[1]) if part is None else pl.ds(part * depth, depth)
            places.append((slice(None), column))
            shapes.append((right.shape[0], column.size))
            width = shapes[-1][1 - dim]
        operands += [left, right]
        dims.append(dim)
        flops += 2 * rows * depth * width
        moved += 2 * rows * depth + 2 * depth * width
    anywhere = pl.BlockSpec(memory_space=pl.ANY)
    return pl.pallas_call(
        functools.partial(
            sum_kernel, places=places, dims=tuple(dims), start=start, chunk=chunk
        ),
        in_specs=[anywhere] * len(operands),
        out_specs=anywhere,
        out_shape=jax.ShapeDtypeStruct((rows, width), dtype),
        scratch_shapes=[pltpu.VMEM(shape, BF16) for shape in shapes]
        + [
            pltpu.VMEM((rows, width), F32),
            pltpu.VMEM((rows, width), dtype),
            pltpu.SemaphoreType.DMA((len(operands),)),
            pltpu.SemaphoreType.DMA((rows // chunk,)),
        ],
        cost_estimate=cost(flops, moved + 4 * rows * width),
        compiler_params=pltpu.CompilerParams(vmem_limit_bytes=58 * MIB),
        name="sum_products",
    )(*operands)


def outer_kernel(*refs, count):
    right_ref, out_ref, left, sems, left_t = refs[count:]

    @pl.when(pl.program_id(0) == 0)
    def _():
        for copy in fetch(refs[:count], left, sems):
            copy.wait()
        left_t[...] = left[...].T

    out_ref[...] = contract(left_t[...], right_ref[...], 1, 0).astype(BF16)


def outer(pieces, right):
    width = pieces[0].shape[1]
    planes, count, columns = right.shape
    return pl.pallas_call(
        functools.partial(outer_kernel, count=len(pieces)),
        grid=(planes,),
        in_specs=[pl.BlockSpec(memory_space=pl.ANY)] * len(pieces)
        + [pl.BlockSpec((None, count, columns), lambda i: (i, 0, 0))],
        out_specs=pl.BlockSpec((width, columns), lambda i: (0, i)),
        out_shape=jax.ShapeDtypeStruct((width, planes * columns), BF16),
        scratch_shapes=room(pieces) + [pltpu.VMEM((width, count), BF16)],
        cost_estimate=cost(
            2 * count * width * planes * columns,
            2 * count * (width + planes * columns) + 2 * width * planes * columns,
        ),
        compiler_params=pltpu.CompilerParams(vmem_limit_bytes=40 * MIB),
        name="outer_product",
    )(*pieces, right)


def branch_kernel(*refs, count, groups, chunk):
    weights = refs[count : count + groups]
    mixed = refs[count + groups : count + 2 * groups]
    outs = refs[count + 2 * groups : count + 4 * groups]
    rows, sems = refs[count + 4 * groups :]
    for copy in fetch(refs[:count], rows, sems):
        copy.wait()
    for index in range(groups):
        outs[groups + index][...] = contract(mixed[index][...].T, rows[...], 1, 0).astype(BF16)
        for start in range(0, rows.shape[0], chunk):
            span = slice(start, start + chunk)
            outs[index][span, :] = contract(rows[span, :], weights[index][...], 1, 1).astype(BF16)


def branch_back(pieces, weights, mixed, chunk=512):
    count = sum(piece.shape[0] for piece in pieces)
    width = pieces[0].shape[1]
    groups = len(weights)
    vmem = pl.BlockSpec(memory_space=pltpu.VMEM)
    columns = [weight.shape[0] for weight in weights]
    results = pl.pallas_call(
        functools.partial(branch_kernel, count=len(pieces), groups=groups, chunk=chunk),
        in_specs=[pl.BlockSpec(memory_space=pl.ANY)] * len(pieces) + [vmem] * (2 * groups),
        out_specs=[vmem] * (2 * groups),
        out_shape=[jax.ShapeDtypeStruct((count, size), BF16) for size in columns]
        + [jax.ShapeDtypeStruct((size, width), BF16) for size in columns],
        scratch_shapes=room(pieces),
        cost_estimate=cost(4 * count * width * sum(columns), 6 * count * width),
        compiler_params=pltpu.CompilerParams(vmem_limit_bytes=48 * MIB),
        name="branch_backward",
    )(*pieces, *weights, *mixed)
    return results[:groups], results[groups:]


def standardize(value):
    centred = value - jnp.mean(value, axis=-1, keepdims=True)
    scale = lax.rsqrt(jnp.mean(centred * centred, axis=-1, keepdims=True) + EPSILON)
    return centred * scale, scale


def norm_kernel(*refs, added):
    value = refs[0][...].astype(F32)
    for ref in refs[1 : 1 + added]:
        value = value + ref[...].astype(F32)
    gain_ref, shift_ref = refs[1 + added : 3 + added]
    standard, _ = standardize(value)
    if added:
        refs[-2][...] = value
    refs[-1][...] = (standard * gain_ref[...] + shift_ref[...]).astype(BF16)


def norm(base, terms, gain, shift, pieces=PIECES, block=256):
    count, width = base.shape
    rows = count // pieces
    block = min(block, rows)
    vector = pl.BlockSpec((1, width), lambda i: (0, 0))
    total, out = None, []
    for piece in range(pieces):
        first = piece * rows // block
        whole = pl.BlockSpec((block, width), lambda i, first=first: (first + i, 0))
        shapes = [jax.ShapeDtypeStruct((rows, width), BF16)]
        specs = [pl.BlockSpec((block, width), lambda i: (i, 0))]
        held = []
        if terms:
            shapes = [jax.ShapeDtypeStruct((count, width), F32)] + shapes
            specs = [whole] + specs
            held = [] if total is None else [total]
        results = pl.pallas_call(
            lambda *refs, held=len(held): norm_kernel(
                *refs[: 3 + len(terms)], *refs[3 + len(terms) + held :], added=len(terms)
            ),
            grid=(rows // block,),
            in_specs=[whole] * (1 + len(terms))
            + [vector, vector]
            + [pl.BlockSpec(memory_space=pl.ANY)] * len(held),
            out_specs=specs,
            out_shape=shapes,
            input_output_aliases={3 + len(terms): 0} if held else {},
            cost_estimate=cost(16 * rows * width, 8 * rows * width * len(shapes)),
            name="layer_norm",
        )(base, *terms, gain.reshape(1, width), shift.reshape(1, width), *held)
        out.append(results[-1])
        if terms:
            total = results[0]
    return total, out


def norm_back_kernel(*refs, added, low):
    base_ref, straight_ref, gain_ref = refs[:3]
    upstream = refs[3][...].astype(F32)
    for ref in refs[4 : 3 + added]:
        upstream = upstream + ref[...].astype(F32)
    outs = refs[3 + added :]
    standard, scale = standardize(base_ref[...].astype(F32))
    scaled = upstream * gain_ref[...]
    back = straight_ref[...].astype(F32) + scale * (
        scaled
        - jnp.mean(scaled, axis=-1, keepdims=True)
        - standard * jnp.mean(scaled * standard, axis=-1, keepdims=True)
    )
    outs[0][...] = back.astype(BF16)
    if not low:
        outs[1][...] = back
    sums = jnp.concatenate(
        [
            jnp.sum(upstream * standard, axis=0, keepdims=True),
            jnp.sum(upstream, axis=0, keepdims=True),
        ],
        axis=0,
    )

    @pl.when(pl.program_id(0) == 0)
    def _():
        outs[-1][...] = sums

    @pl.when(pl.program_id(0) > 0)
    def _():
        outs[-1][...] += sums


def norm_back(base, straight, gain, terms, low, pieces=PIECES, block=256):
    count, width = base.shape
    rows = count // pieces
    block = min(block, rows)
    total, out, found = None, [], []
    for piece in range(pieces):
        first = piece * rows // block
        whole = pl.BlockSpec((block, width), lambda i, first=first: (first + i, 0))
        shapes = [jax.ShapeDtypeStruct((rows, width), BF16)]
        specs = [pl.BlockSpec((block, width), lambda i: (i, 0))]
        held = []
        if not low:
            shapes.append(jax.ShapeDtypeStruct((count, width), F32))
            specs.append(whole)
            held = [] if total is None else [total]
        results = pl.pallas_call(
            lambda *refs, held=len(held): norm_back_kernel(
                *refs[: 3 + len(terms)],
                *refs[3 + len(terms) + held :],
                added=len(terms),
                low=low,
            ),
            grid=(rows // block,),
            in_specs=[whole, whole, pl.BlockSpec((1, width), lambda i: (0, 0))]
            + [whole] * len(terms)
            + [pl.BlockSpec(memory_space=pl.ANY)] * len(held),
            out_specs=specs + [pl.BlockSpec((2, width), lambda i: (0, 0))],
            out_shape=shapes + [jax.ShapeDtypeStruct((2, width), F32)],
            input_output_aliases={3 + len(terms): 1} if held else {},
            cost_estimate=cost(30 * rows * width, 16 * rows * width),
            name="layer_norm_backward",
        )(base, straight, gain.reshape(1, width), *terms, *held)
        out.append(results[0])
        found.append(results[-1])
        if not low:
            total = results[1]
    return out, total, sum(found)


def rope_tables(offset):
    half = HD // 2
    groups = LANES // half
    count = LEN // groups
    lane = jnp.arange(LANES, dtype=jnp.int32)
    position = jnp.arange(count, dtype=jnp.int32)[:, None] + lane[None, :] // half * count
    position = (position + offset) % LEN
    inverse = 10000.0 ** (-2.0 * (lane % half).astype(F32) / HD)
    angles = position.astype(F32) * inverse[None, :]
    cosines, sines = lax.optimization_barrier((jnp.cos(angles), jnp.sin(angles)))

    def rows(table, signs):
        parts = [table[:, g * half : (g + 1) * half] for g in range(groups)]
        return jnp.concatenate(
            [jnp.concatenate([sign * part for sign in signs], axis=1) for part in parts], axis=0
        )

    return rows(cosines, (1, 1, 1, 1)), rows(sines, (-1, 1, -1, 1))


def exchanges(axis, size):
    if size & (size - 1):
        return [lambda value: lax.psum(value, axis)]
    return [
        lambda value, pairs=[(i, i ^ (1 << bit)) for i in range(size)]: value
        + lax.ppermute(value, axis, pairs)
        for bit in range(size.bit_length() - 1)
    ]


def shards(
    dp_size,
    tensor_size,
    tokens,
    lengths,
    gain_first,
    shift_first,
    query_weight,
    key_weight,
    value_weight,
    output_weight,
    gain_second,
    shift_second,
    gate_weight,
    up_weight,
    down_weight,
    cotangent,
):
    windows = lengths.shape[0]
    span = tensor_size // windows
    held = tokens.shape[0]
    width = tokens.shape[1]
    head_cols = query_weight.shape[1]
    here = lax.axis_index("tensor")
    window, seat = here // span, here % span

    def from_seat(value, shift):
        pairs = [
            (w * span + (s + shift) % span, w * span + s)
            for w in range(windows)
            for s in range(span)
        ]
        return lax.ppermute(value, "tensor", pairs)

    def to_seat(value, shift):
        return from_seat(value, span - shift)

    def from_window(value, shift):
        pairs = [((t + shift * span) % tensor_size, t) for t in range(tensor_size)]
        return lax.ppermute(value, "tensor", pairs)

    def to_window(value, shift):
        return from_window(value, windows - shift)

    def gather_rows(value):
        return value + [from_seat(piece, s) for s in range(1, span) for piece in value]

    def scatter(partial):
        sent = [to_seat(partial(s * held, held), s) for s in range(1, span)]
        return [partial(0, held)] + sent

    def all_windows(value):
        return [value] + [from_window(value, shift) for shift in range(1, windows)]

    def spread_windows(values):
        group = lax.axis_index("dp")
        sizes = [value.shape[0] // dp_size for value in values]
        mine = jnp.concatenate(
            [
                lax.dynamic_slice_in_dim(value, group * size, size, axis=0).reshape(-1, width)
                for value, size in zip(values, sizes)
            ],
            axis=0,
        )
        return [mine], [from_window(mine, shift) for shift in range(1, windows)]

    def gather_spread(values, piece):
        gathered = lax.all_gather(piece, "dp", axis=0)
        if all(value.shape == (width, width) for value in values):
            return [(gathered, plane) for plane in range(len(values))]
        out, start = [], 0
        for value in values:
            count = value.size // width // dp_size
            out.append(gathered[:, start : start + count].reshape(value.shape))
            start += count
        return out

    def after(value, *others):
        return lax.optimization_barrier((value, *others))[0]

    def pieces_after(pieces, *others):
        return [after(pieces[0], *others)] + pieces[1:]

    place = jnp.stack(
        [lax.dynamic_index_in_dim(lengths, window, keepdims=False), seat * held]
    ).astype(jnp.int32)
    cosines, sines = rope_tables(seat * held)

    members = [[s] for s in range(windows)] if head_cols % LANES == 0 else [list(range(windows))]
    feed_weights = [gate_weight, up_weight, down_weight]
    slices_sent, slices = spread_windows(feed_weights)
    _, normed_one = norm(after(tokens, *slices_sent), [], gain_first, shift_first)
    full_one = gather_rows(normed_one)
    qkv_own = jnp.concatenate([query_weight, key_weight, value_weight], axis=1)
    qkv_other = all_windows(after(qkv_own, *slices))[1:]
    qkv_shards = [qkv_own] + qkv_other
    def joined(parts, axis):
        return parts[0] if len(parts) == 1 else jnp.concatenate(parts, axis=axis)

    def part_of(value, part):
        return value[:, part * head_cols : (part + 1) * head_cols]

    qkv_weights = [
        qkv_shards[group[0]]
        if len(group) == 1
        else joined([part_of(qkv_shards[s], part) for part in range(3) for s in group], 1)
        for group in members
    ]
    target = gather_rows([cotangent])
    qkv, attended = [], []
    rows_one = full_one
    for weight in qkv_weights:
        parts = project(rows_one, weight, cosines, sines)
        if not qkv:
            slices = [after(piece, parts[0]) for piece in slices]
            feed_shards = [feed_weights]
            feed_shards += [gather_spread(feed_weights, piece) for piece in slices]
        waits = slices if not qkv else target
        qkv.append((after(parts[0], *waits), *parts[1:]))
        attended.append(attend(place, *qkv[-1]))
        if len(attended) == 1:
            sent = after(output_weight, attended[0][0])
            output_shards = [output_weight] + all_windows(sent)[1:]
        rows_one = pieces_after(full_one, attended[-1][0])

    out_weights = [joined([output_shards[s] for s in group], 0) for group in members]
    mixer_terms = [
        (mixed, None, weight, None, 0) for (mixed, _), weight in zip(attended, out_weights)
    ]
    hidden_one, normed_two = norm(
        tokens,
        scatter(lambda start, rows: sum_products(mixer_terms, start, rows)),
        gain_second,
        shift_second,
    )
    full_two = gather_rows(normed_two)

    flip = [(d, d ^ 1) for d in range(dp_size)]
    odd = lax.axis_index("dp") % 2

    def half(value, which):
        count = value.shape[0] // 2
        return lax.dynamic_slice_in_dim(value, which * count, count, axis=0)

    def total(pieces, which):
        return sum(half(piece, which).astype(F32) for piece in pieces).astype(BF16)

    def swap_half(pieces, *others):
        pieces = [after(piece, *others) for piece in pieces]
        mine, sent = total(pieces, odd), total(pieces, 1 - odd)
        return (mine, lax.ppermute(sent, "dp", flip)), [mine, sent]

    def add_half(halves, *others):
        mine, received = (after(value, *others) for value in halves)
        return (mine.astype(F32) + received.astype(F32)).astype(BF16)

    def sum_half(value, turn):
        groups = [list(range(0, dp_size, 2)), list(range(1, dp_size, 2))]
        if turn & 1:
            groups = groups[::-1]
        if turn & 2:
            groups = [group[::-1] for group in groups]
        return lax.psum(value, "dp", axis_index_groups=groups)

    def swap_sum(mine, *others):
        mine = after(mine, *others)
        return mine, lax.ppermute(mine, "dp", flip)

    def whole_sum(halves, *others):
        mine, received = (after(value, *others) for value in halves)
        first, second = jnp.where(odd == 0, mine, received), jnp.where(odd == 0, received, mine)
        return jnp.concatenate([first, second], axis=0).astype(F32)

    def send_to_owner(parts):
        return [to_window(parts[shift], shift) for shift in range(1, windows)]

    order = list(range(1, windows)) + [0]
    fed = {}
    rows_two = full_two
    for s in order:
        fed[s] = feed(rows_two, target, feed_shards[s])
        rows_two = pieces_after(full_two, fed[s][0])
    down_pieces, up_pieces, gate_pieces = (
        send_to_owner({s: fed[s][k] for s in order}) + [fed[0][k]] for k in (5, 4, 3)
    )
    two_terms, feed_terms = [], []
    for s in order:
        gate, up, down = feed_shards[s]
        two_terms += [(fed[s][1], None, gate, None, 1), (fed[s][2], None, up, None, 1)]
        feed_terms.append((fed[s][0], None, down, None, 0))

    two_sent = [
        sum_products(two_terms, shift * held, held, BF16) for shift in range(1, span)
    ]
    down_half, marks = swap_half(down_pieces, *two_sent)
    two_terms = [(after(two_terms[0][0], *marks), *two_terms[0][1:])] + two_terms[1:]
    two_kept = sum_products(two_terms, 0, held)
    grad_branch_own, grad_hidden, norm_two = norm_back(
        hidden_one,
        cotangent,
        gain_second,
        [two_kept] + [to_seat(part, shift + 1) for shift, part in enumerate(two_sent)],
        False,
    )
    grad_branch = gather_rows(grad_branch_own)
    down_half = add_half(down_half, *grad_branch_own)
    down_sum = sum_half(down_half, 0)
    grad_branch = pieces_after(grad_branch, down_half)

    members = members[::-1]
    out_weights, qkv_weights = out_weights[::-1], qkv_weights[::-1]
    qkv, attended = qkv[::-1], attended[::-1]
    grad_mixed, found = branch_back(grad_branch, out_weights, [mixed for mixed, _ in attended])
    out_grads = {
        s: out_grad[spot * head_cols : (spot + 1) * head_cols]
        for group, out_grad in zip(members, found)
        for spot, s in enumerate(group)
    }
    out_pieces = send_to_owner(out_grads) + [out_grads[0]]

    def up_swap(last):
        sums["up"], waits = swap_half(up_pieces, *last)
        return waits

    def up_sum(last):
        value = add_half(sums["up"], *last)
        sums["up"] = sum_half(value, 1)
        return [value]

    def gate_swap(last):
        sums["gate"], waits = swap_half(gate_pieces, *last)
        sums["out"], more = swap_half(out_pieces, *last)
        sums["down"] = after(down_sum, *waits, *more)
        return waits + more + [sums["down"]]

    def gate_sum(last):
        values = add_half(sums["gate"], *last), add_half(sums["out"], *last)
        sums["gate"], sums["out"] = sum_half(values, 2)
        sums["up"] = swap_sum(sums["up"], *last)
        return [*values, sums["up"][0]]

    exchange = exchanges("tensor", tensor_size) + exchanges("dp", dp_size)
    sums = {}
    moves = [up_swap, up_sum, gate_swap, gate_sum]
    last = list(grad_mixed)
    grad_qkv, qkv_grads = [], {}
    for index, group in enumerate(members):
        mixed, logs = attended[index]
        count = len(group) * head_cols
        grads = None
        for pair in range(count // LANES):
            waits = moves.pop(0)(last) if moves else last
            grads = attend_back(
                place,
                *qkv[index],
                mixed,
                after(grad_mixed[index], *waits),
                logs,
                cosines,
                sines,
                pair,
                grads,
            )
            last = [grads]
        grad_qkv.append(grads)
        qkv_grad = outer(full_one, grads)
        last = [qkv_grad]
        for spot, s in enumerate(group):
            if len(group) == 1:
                qkv_grads[s] = qkv_grad
            else:
                qkv_grads[s] = joined(
                    [
                        lax.slice_in_dim(
                            qkv_grad,
                            part * count + spot * head_cols,
                            part * count + (spot + 1) * head_cols,
                            axis=1,
                        )
                        for part in range(3)
                    ],
                    1,
                )
    for move in moves:
        last = move(last)

    qkv_half, marks = swap_half(send_to_owner(qkv_grads) + [qkv_grads[0]])
    grad_up = whole_sum(sums["up"], *marks)
    down_halves = swap_sum(sums["down"], *marks)
    feed_terms[0] = (after(feed_terms[0][0], grad_up, down_halves[0]), *feed_terms[0][1:])
    one_terms = [
        (grad_qkv[index], part, weight, part, 1)
        for index, weight in enumerate(qkv_weights)
        for part in range(3)
    ]

    def later(terms, *others):
        return [(after(terms[0][0], *others), *terms[0][1:])] + terms[1:]

    shifts = range(1, span)
    feed_sent = [sum_products(feed_terms, shift * held, held, BF16) for shift in shifts]
    qkv_half = add_half(qkv_half, *feed_sent)
    gate_halves = swap_sum(sums["gate"], *feed_sent)
    out_halves = swap_sum(sums["out"], *feed_sent)
    qkv_sum = sum_half(after(qkv_half, gate_halves[0], out_halves[0]), 3)
    one_terms = later(one_terms, qkv_half, gate_halves[0])
    one_sent = [sum_products(one_terms, shift * held, held, BF16) for shift in shifts]
    feed_parts = [sum_products(later(feed_terms, *one_sent), 0, held)]
    one_parts = [sum_products(later(one_terms, feed_parts[0]), 0, held)]
    feed_parts += [to_seat(part, shift) for shift, part in zip(shifts, feed_sent)]
    one_parts += [to_seat(part, shift) for shift, part in zip(shifts, one_sent)]
    output = (hidden_one + sum(feed_parts)).astype(BF16)
    (input_grad,), _, norm_one = norm_back(tokens, grad_hidden, gain_first, one_parts, True, 1)
    window = [input_grad, output]
    qkv_halves = swap_sum(qkv_sum, *window)
    norms = jnp.concatenate([after(norm_one, qkv_halves[0]), norm_two], axis=0)
    for step in exchange:
        norms = step(norms)
    grad_down = whole_sum(down_halves, qkv_halves[0])
    grad_gate = whole_sum(gate_halves, qkv_halves[0])
    out_grad = whole_sum(out_halves, qkv_halves[0])
    qkv_grad = whole_sum(qkv_halves)
    return (
        output,
        input_grad,
        *(part_of(qkv_grad, part) for part in range(3)),
        out_grad,
        grad_gate,
        grad_up,
        grad_down,
        norms[0],
        norms[1],
        norms[2],
        norms[3],
    )


def solution(mesh):
    rows = P(("dp", "tensor"), None)
    columns = P(None, "tensor")
    depth = P("tensor", None)
    return jax.shard_map(
        functools.partial(shards, mesh.shape["dp"], mesh.shape["tensor"]),
        mesh=mesh,
        in_specs=(
            rows,
            P("dp"),
            P(),
            P(),
            columns,
            columns,
            columns,
            depth,
            P(),
            P(),
            columns,
            columns,
            depth,
            rows,
        ),
        out_specs=(
            rows,
            rows,
            columns,
            columns,
            columns,
            depth,
            columns,
            columns,
            depth,
            P(),
            P(),
            P(),
            P(),
        ),
        check_vma=False,
    )
```

```python
import functools
import math

import jax
import jax.numpy as jnp
from jax import lax
from jax.experimental import pallas as pl
from jax.experimental.pallas import tpu as pltpu
from jax.sharding import PartitionSpec as P

HD = 64
LEN = 2048
EPSILON = 1e-05
MASKED = -1e30
LANES = 128
LOG2E = math.log2(math.e)
BF16 = jnp.bfloat16
F32 = jnp.float32
MIB = 1 << 20
COST_SHARE = 0.1
PIECES = 2


def contract(left, right, left_dim, right_dim):
    return lax.dot_general(
        left, right, (((left_dim,), (right_dim,)), ((), ())), preferred_element_type=F32
    )


def cost(flops, moved, transcendentals=0):
    return pl.CostEstimate(
        flops=int(flops * COST_SHARE),
        bytes_accessed=int(moved * COST_SHARE),
        transcendentals=int(transcendentals * COST_SHARE),
    )


def swap_halves(value):
    columns = value.shape[1]
    lane = lax.broadcasted_iota(jnp.int32, value.shape, 1)
    return jnp.where(
        lane % HD < HD // 2,
        pltpu.roll(value, columns - HD // 2, 1),
        pltpu.roll(value, HD // 2, 1),
    )


def fetch(pieces, rows, sems):
    copies, start = [], 0
    for index, piece in enumerate(pieces):
        count = piece.shape[0]
        copies.append(
            pltpu.make_async_copy(piece, rows.at[pl.ds(start, count), :], sems.at[index])
        )
        start += count
    for copy in copies:
        copy.start()
    return copies


def room(pieces):
    count = sum(piece.shape[0] for piece in pieces)
    return [
        pltpu.VMEM((count, pieces[0].shape[1]), BF16),
        pltpu.SemaphoreType.DMA((len(pieces),)),
    ]


def unpacked(ref):
    value = ref[...]
    return value.reshape(-1, value.shape[-1]) if value.ndim == 3 else value


def packed(weight):
    return isinstance(weight, tuple)


def project_kernel(*refs, count):
    pieces = refs[:count]
    weight_ref, cos_ref, sin_ref, q_ref, k_ref, v_ref, rows, sems = refs[count:]
    columns = q_ref.shape[1]
    block = q_ref.shape[0]

    @pl.when(pl.program_id(0) == 0)
    def _():
        for copy in fetch(pieces, rows, sems):
            copy.wait()

    start = pl.multiple_of(pl.program_id(0) * block, block)
    product = contract(rows[pl.ds(start, block), :], weight_ref[...], 1, 0)
    cosines = jnp.concatenate([cos_ref[...]] * (columns // LANES), axis=1)
    sines = jnp.concatenate([sin_ref[...]] * (columns // LANES), axis=1)
    for part, out_ref in ((0, q_ref), (1, k_ref)):
        value = product[:, part * columns : (part + 1) * columns]
        out_ref[...] = (value * cosines + swap_halves(value) * sines).astype(BF16)
    v_ref[...] = product[:, 2 * columns :].astype(BF16)


def project(pieces, weight, cosines, sines, block=512):
    width = weight.shape[0]
    columns = weight.shape[1] // 3
    count = sum(piece.shape[0] for piece in pieces)
    table = pl.BlockSpec((block, LANES), lambda i: (i, 0))
    out = pl.BlockSpec((block, columns), lambda i: (i, 0))
    return pl.pallas_call(
        functools.partial(project_kernel, count=len(pieces)),
        grid=(count // block,),
        in_specs=[pl.BlockSpec(memory_space=pl.ANY)] * len(pieces)
        + [pl.BlockSpec(weight.shape, lambda i: (0, 0)), table, table],
        out_specs=[out, out, out],
        out_shape=[jax.ShapeDtypeStruct((count, columns), BF16)] * 3,
        scratch_shapes=room(pieces),
        cost_estimate=cost(
            2 * count * width * 3 * columns,
            2 * (count * width + width * 3 * columns + count * 3 * columns),
        ),
        compiler_params=pltpu.CompilerParams(vmem_limit_bytes=40 * MIB),
        name="project_rope",
    )(*pieces, weight, cosines, sines)


def masked_keys(place_ref, key_ref, masked_ref):
    count = key_ref.shape[0]
    lane = lax.broadcasted_iota(jnp.int32, (count, LANES), 1)
    row = lax.broadcasted_iota(jnp.int32, (count, LANES), 0) + place_ref[1]
    position = jnp.where(row >= count, row - count, row)
    bias = jnp.where(position >= place_ref[0], MASKED, 0.0).astype(BF16)
    nothing = jnp.zeros_like(bias)
    key = key_ref[...]
    masked_ref[0] = jnp.where(lane < HD, key, jnp.where(lane == HD, bias, nothing))
    masked_ref[1] = jnp.where(lane >= HD, key, jnp.where(lane == 0, bias, nothing))


def masked_queries(query):
    lane = lax.broadcasted_iota(jnp.int32, query.shape, 1)
    scaled = query * jnp.asarray(1.0 / math.sqrt(HD), BF16)
    one = jnp.ones_like(query)
    nothing = jnp.zeros_like(query)
    return (
        scaled,
        jnp.where(lane < HD, scaled, jnp.where(lane == HD, one, nothing)),
        jnp.where(lane >= HD, scaled, jnp.where(lane == 0, one, nothing)),
    )


def attend_kernel(place_ref, q_ref, k_ref, v_ref, out_ref, log_ref, keys, values_t, *, chunk):
    count = k_ref.shape[0]

    @pl.when(pl.program_id(1) == 0)
    def _():
        masked_keys(place_ref, k_ref, keys)
        values_t[...] = v_ref[...].T

    queries = masked_queries(q_ref[...])[1:]
    mixed, logs = [], []
    for head in range(2):
        scores = [
            contract(keys[head, start : start + chunk, :], queries[head], 1, 1)
            for start in range(0, count, chunk)
        ]
        top = functools.reduce(
            jnp.maximum, [jnp.max(block, axis=0, keepdims=True) for block in scores]
        )
        total = 0.0
        summed = 0.0
        for index, block in enumerate(scores):
            weights = jnp.exp2((block - top) * LOG2E)
            total = total + jnp.sum(weights, axis=0, keepdims=True)
            value = values_t[
                head * HD : (head + 1) * HD, index * chunk : (index + 1) * chunk
            ]
            summed = summed + contract(value, weights.astype(BF16), 1, 0)
        mixed.append(summed / total)
        logs.append(top * LOG2E + jnp.log2(total))
    out_ref[...] = jnp.concatenate(mixed, axis=0).T.astype(BF16)
    log_ref[0] = jnp.concatenate(logs + [jnp.zeros((6, q_ref.shape[0]), F32)], axis=0)


def attend(place, queries, keys, values, block=1024, chunk=512):
    count, columns = queries.shape
    pairs = columns // LANES
    whole = pl.BlockSpec((count, LANES), lambda p, i, _: (0, p))
    rows = pl.BlockSpec((block, LANES), lambda p, i, _: (i, p))
    return pl.pallas_call(
        functools.partial(attend_kernel, chunk=chunk),
        grid_spec=pltpu.PrefetchScalarGridSpec(
            num_scalar_prefetch=1,
            grid=(pairs, count // block),
            in_specs=[rows, whole, whole],
            out_specs=[rows, pl.BlockSpec((1, 8, block), lambda p, i, _: (p, 0, i))],
            scratch_shapes=[
                pltpu.VMEM((2, count, LANES), BF16),
                pltpu.VMEM((LANES, count), BF16),
            ],
        ),
        out_shape=[
            jax.ShapeDtypeStruct((count, columns), BF16),
            jax.ShapeDtypeStruct((pairs, 8, count), F32),
        ],
        cost_estimate=cost(16 * count * count * columns, 8 * count * columns, count * count * columns // HD),
        compiler_params=pltpu.CompilerParams(vmem_limit_bytes=56 * MIB),
        name="attention_forward",
    )(place, queries, keys, values)


def attend_back_kernel(
    place_ref,
    q_ref,
    k_ref,
    v_ref,
    out_ref,
    up_ref,
    log_ref,
    cos_row_ref,
    sin_row_ref,
    cos_ref,
    sin_ref,
    *rest,
    chunk,
):
    grad_ref, keys, grad_keys_t, grad_values_t = rest[-4:]
    count = k_ref.shape[0]
    step = pl.program_id(1)

    @pl.when(step == 0)
    def _():
        masked_keys(place_ref, k_ref, keys)
        grad_keys_t[...] = jnp.zeros_like(grad_keys_t)
        grad_values_t[...] = jnp.zeros_like(grad_values_t)

    scaled, *queries = masked_queries(q_ref[...])
    upstream = up_ref[...]
    lane = lax.broadcasted_iota(jnp.int32, upstream.shape, 1)
    nothing = jnp.zeros_like(upstream)
    products = upstream.astype(F32) * out_ref[...].astype(F32)
    scaled_t = scaled.T
    upstream_t = upstream.T
    logs = log_ref[0].T
    grad_queries = []
    for head in range(2):
        mine = (lane < HD) == (head == 0)
        own_upstream = jnp.where(mine, upstream, nothing)
        row_dot = jnp.sum(jnp.where(mine, products, 0.0), axis=1, keepdims=True)
        log_total = logs[:, head : head + 1]
        heads = slice(head * HD, (head + 1) * HD)
        grad_query = 0.0
        for start in range(0, count, chunk):
            span = slice(start, start + chunk)
            scores = contract(queries[head], keys[head, span, :], 1, 1)
            probs = jnp.exp2(scores * LOG2E - log_total)
            grad_probs = contract(own_upstream, v_ref[span, :], 1, 1)
            grad_scores = (probs * (grad_probs - row_dot)).astype(BF16)
            grad_values_t[heads, span] += contract(
                upstream_t[heads, :], probs.astype(BF16), 1, 0
            )
            grad_keys_t[heads, span] += contract(scaled_t[heads, :], grad_scores, 1, 0)
            grad_query = grad_query + contract(grad_scores, k_ref[span, :], 1, 0)
        grad_queries.append(grad_query)
    grad_query = jnp.where(lane < HD, *grad_queries) * (1.0 / math.sqrt(HD))
    block = grad_query.shape[0]
    grad_ref[0, pl.ds(pl.multiple_of(step * block, block), block), :] = (
        grad_query * cos_row_ref[...] - swap_halves(grad_query) * sin_row_ref[...]
    ).astype(BF16)

    @pl.when(step == pl.num_programs(1) - 1)
    def _():
        grad_key = grad_keys_t[...].T
        grad_ref[1] = (
            grad_key * cos_ref[...] - swap_halves(grad_key) * sin_ref[...]
        ).astype(BF16)
        grad_ref[2] = grad_values_t[...].T.astype(BF16)


def attend_back(
    place, queries, keys, values, mixed, upstream, logs, cosines, sines, pair, grads, block=512, chunk=512
):
    count, columns = queries.shape
    whole = pl.BlockSpec((count, LANES), lambda p, i, _: (0, pair))
    rows = pl.BlockSpec((block, LANES), lambda p, i, _: (i, pair))
    table = pl.BlockSpec((count, LANES), lambda p, i, _: (0, 0))
    table_rows = pl.BlockSpec((block, LANES), lambda p, i, _: (i, 0))
    held = [] if grads is None else [grads]
    return pl.pallas_call(
        functools.partial(attend_back_kernel, chunk=chunk),
        grid_spec=pltpu.PrefetchScalarGridSpec(
            num_scalar_prefetch=1,
            grid=(1, count // block),
            in_specs=[
                rows,
                whole,
                whole,
                rows,
                rows,
                pl.BlockSpec((1, 8, block), lambda p, i, _: (pair, 0, i)),
                table_rows,
                table_rows,
                table,
                table,
            ]
            + [pl.BlockSpec(memory_space=pl.ANY)] * len(held),
            out_specs=pl.BlockSpec((3, count, LANES), lambda p, i, _: (0, 0, pair)),
            scratch_shapes=[
                pltpu.VMEM((2, count, LANES), BF16),
                pltpu.VMEM((LANES, count), F32),
                pltpu.VMEM((LANES, count), F32),
            ],
        ),
        out_shape=jax.ShapeDtypeStruct((3, count, columns), BF16),
        input_output_aliases={11: 0} if held else {},
        cost_estimate=cost(28 * count * count * LANES, 16 * count * LANES, count * count * 2),
        compiler_params=pltpu.CompilerParams(vmem_limit_bytes=60 * MIB),
        name="attention_backward",
    )(place, queries, keys, values, mixed, upstream, logs, cosines, sines, cosines, sines, *held)


def feed_kernel(*refs, counts, chunk):
    row_pieces, target_pieces = refs[: counts[0]], refs[counts[0] : sum(counts)]
    refs = refs[sum(counts) :]
    gate_ref, up_ref, down_ref, inner_ref, grad_gate_ref, grad_up_ref = refs[:6]
    weight_gate_ref, weight_up_ref, weight_down_ref = refs[6:9]
    rows, row_sems, target, target_sems, rows_t, target_t = refs[9:]

    @pl.when(pl.program_id(0) == 0)
    def _():
        copies = fetch(row_pieces, rows, row_sems) + fetch(target_pieces, target, target_sems)
        for copy in copies:
            copy.wait()
        rows_t[...] = rows[...].T
        target_t[...] = target[...].T

    gate_weight, up_weight, down_weight = unpacked(gate_ref), unpacked(up_ref), unpacked(down_ref)
    for start in range(0, rows.shape[0], chunk):
        span = slice(start, start + chunk)
        gate = contract(rows[span, :], gate_weight, 1, 0)
        up = contract(rows[span, :], up_weight, 1, 0)
        grad_inner = contract(target[span, :], down_weight, 1, 1)
        share = jax.nn.sigmoid(gate)
        activated = gate * share
        inner_ref[span, :] = (activated * up).astype(BF16)
        grad_up_ref[span, :] = (grad_inner * activated).astype(BF16)
        grad_gate_ref[span, :] = (
            grad_inner * up * share * (1.0 + gate * (1.0 - share))
        ).astype(BF16)
    weight_gate_ref[...] = contract(rows_t[...], grad_gate_ref[...], 1, 0).astype(BF16)
    weight_up_ref[...] = contract(rows_t[...], grad_up_ref[...], 1, 0).astype(BF16)
    weight_down_ref[...] = contract(target_t[...], inner_ref[...], 1, 0).T.astype(BF16)


def feed(rows, target, weights, block=256, chunk=512):
    count = sum(piece.shape[0] for piece in rows)
    width = rows[0].shape[1]
    across_spec = lambda units: pl.BlockSpec((width, min(block, units)), lambda i: (0, i))
    down_spec = lambda units: pl.BlockSpec((min(block, units), width), lambda i: (i, 0))
    if packed(weights[0]):
        units = width
        replicas, deep = weights[0][0].shape[0], width // weights[0][0].shape[0]
        specs = [
            pl.BlockSpec((replicas, deep, block), lambda i, plane=weights[k][1]: (0, plane, i))
            for k in range(2)
        ] + [
            pl.BlockSpec(
                (block // deep, deep, width), lambda i, plane=weights[2][1]: (i, plane, 0)
            )
        ]
        weights = [weight for weight, _ in weights]
    else:
        units = weights[0].shape[1]
        specs = [across_spec(units)] * 2 + [down_spec(units)]
    block = min(block, units)
    out = pl.BlockSpec((count, block), lambda i: (0, i))
    return pl.pallas_call(
        functools.partial(feed_kernel, counts=(len(rows), len(target)), chunk=chunk),
        grid=(units // block,),
        in_specs=[pl.BlockSpec(memory_space=pl.ANY)] * (len(rows) + len(target)) + specs,
        out_specs=[out, out, out] + [across_spec(units)] * 2 + [down_spec(units)],
        out_shape=[jax.ShapeDtypeStruct((count, units), BF16)] * 3
        + [jax.ShapeDtypeStruct((width, units), BF16)] * 2
        + [jax.ShapeDtypeStruct((units, width), BF16)],
        scratch_shapes=room(rows) + room(target) + [pltpu.VMEM((width, count), BF16)] * 2,
        cost_estimate=cost(
            12 * count * width * units,
            4 * count * width + 12 * width * units + 6 * count * units,
            2 * count * units,
        ),
        compiler_params=pltpu.CompilerParams(vmem_limit_bytes=60 * MIB),
        name="feed_forward",
    )(*rows, *target, *weights)


def sum_kernel(*refs, places, dims, start, chunk):
    terms = len(dims)
    operands, out_ref = refs[: 2 * terms], refs[2 * terms]
    buffers = refs[2 * terms + 1 : 4 * terms + 1]
    total, result, sems, out_sems = refs[4 * terms + 1 :]
    rows = total.shape[0]
    copies = []
    for index, (ref, place) in enumerate(zip(operands, places)):
        copy = pltpu.make_async_copy(ref.at[place], buffers[index], sems.at[index])
        copy.start()
        copies.append(copy)
    sent = []
    for index, dim in enumerate(dims):
        copies[2 * index].wait()
        copies[2 * index + 1].wait()
        right = unpacked(buffers[2 * index + 1])
        for first in range(0, rows, chunk):
            span = slice(first, first + chunk)
            product = contract(buffers[2 * index][span, :], right, 1, dim)
            if index:
                product = total[span, :] + product
            if index + 1 < terms:
                total[span, :] = product
                continue
            result[span, :] = product.astype(result.dtype)
            copy = pltpu.make_async_copy(
                result.at[pl.ds(first, chunk), :],
                out_ref.at[pl.ds(first, chunk), :],
                out_sems.at[first // chunk],
            )
            copy.start()
            sent.append(copy)
    for copy in sent:
        copy.wait()


def sum_products(terms, start, rows, dtype=F32, chunk=256):
    chunk = min(chunk, rows)
    operands, places, shapes, dims, flops, moved = [], [], [], [], 0, 0
    for left, plane, right, part, dim in terms:
        depth = left.shape[-1]
        span = pl.ds(start, rows)
        places.append((span, slice(None)) if plane is None else (plane, span, slice(None)))
        shapes.append((rows, depth))
        if packed(right):
            right, plane = right
            width = right.shape[2]
            deep = width // right.shape[0]
            places.append((slice(None), pl.ds(plane * deep, deep), slice(None)))
            shapes.append((right.shape[0], deep, width))
        else:
            column = pl.ds(0, right.shape[1]) if part is None else pl.ds(part * depth, depth)
            places.append((slice(None), column))
            shapes.append((right.shape[0], column.size))
            width = shapes[-1][1 - dim]
        operands += [left, right]
        dims.append(dim)
        flops += 2 * rows * depth * width
        moved += 2 * rows * depth + 2 * depth * width
    anywhere = pl.BlockSpec(memory_space=pl.ANY)
    return pl.pallas_call(
        functools.partial(
            sum_kernel, places=places, dims=tuple(dims), start=start, chunk=chunk
        ),
        in_specs=[anywhere] * len(operands),
        out_specs=anywhere,
        out_shape=jax.ShapeDtypeStruct((rows, width), dtype),
        scratch_shapes=[pltpu.VMEM(shape, BF16) for shape in shapes]
        + [
            pltpu.VMEM((rows, width), F32),
            pltpu.VMEM((rows, width), dtype),
            pltpu.SemaphoreType.DMA((len(operands),)),
            pltpu.SemaphoreType.DMA((rows // chunk,)),
        ],
        cost_estimate=cost(flops, moved + 4 * rows * width),
        compiler_params=pltpu.CompilerParams(vmem_limit_bytes=58 * MIB),
        name="sum_products",
    )(*operands)


def outer_kernel(*refs, count):
    right_ref, out_ref, left, sems, left_t = refs[count:]

    @pl.when(pl.program_id(0) == 0)
    def _():
        for copy in fetch(refs[:count], left, sems):
            copy.wait()
        left_t[...] = left[...].T

    out_ref[...] = contract(left_t[...], right_ref[...], 1, 0).astype(BF16)


def outer(pieces, right):
    width = pieces[0].shape[1]
    planes, count, columns = right.shape
    return pl.pallas_call(
        functools.partial(outer_kernel, count=len(pieces)),
        grid=(planes,),
        in_specs=[pl.BlockSpec(memory_space=pl.ANY)] * len(pieces)
        + [pl.BlockSpec((None, count, columns), lambda i: (i, 0, 0))],
        out_specs=pl.BlockSpec((width, columns), lambda i: (0, i)),
        out_shape=jax.ShapeDtypeStruct((width, planes * columns), BF16),
        scratch_shapes=room(pieces) + [pltpu.VMEM((width, count), BF16)],
        cost_estimate=cost(
            2 * count * width * planes * columns,
            2 * count * (width + planes * columns) + 2 * width * planes * columns,
        ),
        compiler_params=pltpu.CompilerParams(vmem_limit_bytes=40 * MIB),
        name="outer_product",
    )(*pieces, right)


def branch_kernel(*refs, count, groups, chunk):
    weights = refs[count : count + groups]
    mixed = refs[count + groups : count + 2 * groups]
    outs = refs[count + 2 * groups : count + 4 * groups]
    rows, sems = refs[count + 4 * groups :]
    for copy in fetch(refs[:count], rows, sems):
        copy.wait()
    for index in range(groups):
        outs[groups + index][...] = contract(mixed[index][...].T, rows[...], 1, 0).astype(BF16)
        for start in range(0, rows.shape[0], chunk):
            span = slice(start, start + chunk)
            outs[index][span, :] = contract(rows[span, :], weights[index][...], 1, 1).astype(BF16)


def branch_back(pieces, weights, mixed, chunk=512):
    count = sum(piece.shape[0] for piece in pieces)
    width = pieces[0].shape[1]
    groups = len(weights)
    vmem = pl.BlockSpec(memory_space=pltpu.VMEM)
    columns = [weight.shape[0] for weight in weights]
    results = pl.pallas_call(
        functools.partial(branch_kernel, count=len(pieces), groups=groups, chunk=chunk),
        in_specs=[pl.BlockSpec(memory_space=pl.ANY)] * len(pieces) + [vmem] * (2 * groups),
        out_specs=[vmem] * (2 * groups),
        out_shape=[jax.ShapeDtypeStruct((count, size), BF16) for size in columns]
        + [jax.ShapeDtypeStruct((size, width), BF16) for size in columns],
        scratch_shapes=room(pieces),
        cost_estimate=cost(4 * count * width * sum(columns), 6 * count * width),
        compiler_params=pltpu.CompilerParams(vmem_limit_bytes=48 * MIB),
        name="branch_backward",
    )(*pieces, *weights, *mixed)
    return results[:groups], results[groups:]


def standardize(value):
    centred = value - jnp.mean(value, axis=-1, keepdims=True)
    scale = lax.rsqrt(jnp.mean(centred * centred, axis=-1, keepdims=True) + EPSILON)
    return centred * scale, scale


def norm_kernel(*refs, added):
    value = refs[0][...].astype(F32)
    for ref in refs[1 : 1 + added]:
        value = value + ref[...].astype(F32)
    gain_ref, shift_ref = refs[1 + added : 3 + added]
    standard, _ = standardize(value)
    if added:
        refs[-2][...] = value
    refs[-1][...] = (standard * gain_ref[...] + shift_ref[...]).astype(BF16)


def norm(base, terms, gain, shift, pieces=PIECES, block=256):
    count, width = base.shape
    rows = count // pieces
    block = min(block, rows)
    vector = pl.BlockSpec((1, width), lambda i: (0, 0))
    total, out = None, []
    for piece in range(pieces):
        first = piece * rows // block
        whole = pl.BlockSpec((block, width), lambda i, first=first: (first + i, 0))
        shapes = [jax.ShapeDtypeStruct((rows, width), BF16)]
        specs = [pl.BlockSpec((block, width), lambda i: (i, 0))]
        held = []
        if terms:
            shapes = [jax.ShapeDtypeStruct((count, width), F32)] + shapes
            specs = [whole] + specs
            held = [] if total is None else [total]
        results = pl.pallas_call(
            lambda *refs, held=len(held): norm_kernel(
                *refs[: 3 + len(terms)], *refs[3 + len(terms) + held :], added=len(terms)
            ),
            grid=(rows // block,),
            in_specs=[whole] * (1 + len(terms))
            + [vector, vector]
            + [pl.BlockSpec(memory_space=pl.ANY)] * len(held),
            out_specs=specs,
            out_shape=shapes,
            input_output_aliases={3 + len(terms): 0} if held else {},
            cost_estimate=cost(16 * rows * width, 8 * rows * width * len(shapes)),
            name="layer_norm",
        )(base, *terms, gain.reshape(1, width), shift.reshape(1, width), *held)
        out.append(results[-1])
        if terms:
            total = results[0]
    return total, out


def norm_back_kernel(*refs, added, low):
    base_ref, straight_ref, gain_ref = refs[:3]
    upstream = refs[3][...].astype(F32)
    for ref in refs[4 : 3 + added]:
        upstream = upstream + ref[...].astype(F32)
    outs = refs[3 + added :]
    standard, scale = standardize(base_ref[...].astype(F32))
    scaled = upstream * gain_ref[...]
    back = straight_ref[...].astype(F32) + scale * (
        scaled
        - jnp.mean(scaled, axis=-1, keepdims=True)
        - standard * jnp.mean(scaled * standard, axis=-1, keepdims=True)
    )
    outs[0][...] = back.astype(BF16)
    if not low:
        outs[1][...] = back
    sums = jnp.concatenate(
        [
            jnp.sum(upstream * standard, axis=0, keepdims=True),
            jnp.sum(upstream, axis=0, keepdims=True),
        ],
        axis=0,
    )

    @pl.when(pl.program_id(0) == 0)
    def _():
        outs[-1][...] = sums

    @pl.when(pl.program_id(0) > 0)
    def _():
        outs[-1][...] += sums


def norm_back(base, straight, gain, terms, low, pieces=PIECES, block=256):
    count, width = base.shape
    rows = count // pieces
    block = min(block, rows)
    total, out, found = None, [], []
    for piece in range(pieces):
        first = piece * rows // block
        whole = pl.BlockSpec((block, width), lambda i, first=first: (first + i, 0))
        shapes = [jax.ShapeDtypeStruct((rows, width), BF16)]
        specs = [pl.BlockSpec((block, width), lambda i: (i, 0))]
        held = []
        if not low:
            shapes.append(jax.ShapeDtypeStruct((count, width), F32))
            specs.append(whole)
            held = [] if total is None else [total]
        results = pl.pallas_call(
            lambda *refs, held=len(held): norm_back_kernel(
                *refs[: 3 + len(terms)],
                *refs[3 + len(terms) + held :],
                added=len(terms),
                low=low,
            ),
            grid=(rows // block,),
            in_specs=[whole, whole, pl.BlockSpec((1, width), lambda i: (0, 0))]
            + [whole] * len(terms)
            + [pl.BlockSpec(memory_space=pl.ANY)] * len(held),
            out_specs=specs + [pl.BlockSpec((2, width), lambda i: (0, 0))],
            out_shape=shapes + [jax.ShapeDtypeStruct((2, width), F32)],
            input_output_aliases={3 + len(terms): 1} if held else {},
            cost_estimate=cost(30 * rows * width, 16 * rows * width),
            name="layer_norm_backward",
        )(base, straight, gain.reshape(1, width), *terms, *held)
        out.append(results[0])
        found.append(results[-1])
        if not low:
            total = results[1]
    return out, total, sum(found)


def rope_tables(offset):
    half = HD // 2
    groups = LANES // half
    count = LEN // groups
    lane = jnp.arange(LANES, dtype=jnp.int32)
    position = jnp.arange(count, dtype=jnp.int32)[:, None] + lane[None, :] // half * count
    position = (position + offset) % LEN
    inverse = 10000.0 ** (-2.0 * (lane % half).astype(F32) / HD)
    angles = position.astype(F32) * inverse[None, :]
    cosines, sines = lax.optimization_barrier((jnp.cos(angles), jnp.sin(angles)))

    def rows(table, signs):
        parts = [table[:, g * half : (g + 1) * half] for g in range(groups)]
        return jnp.concatenate(
            [jnp.concatenate([sign * part for sign in signs], axis=1) for part in parts], axis=0
        )

    return rows(cosines, (1, 1, 1, 1)), rows(sines, (-1, 1, -1, 1))


def exchanges(axis, size):
    if size & (size - 1):
        return [lambda value: lax.psum(value, axis)]
    return [
        lambda value, pairs=[(i, i ^ (1 << bit)) for i in range(size)]: value
        + lax.ppermute(value, axis, pairs)
        for bit in range(size.bit_length() - 1)
    ]


def shards(
    dp_size,
    tensor_size,
    tokens,
    lengths,
    gain_first,
    shift_first,
    query_weight,
    key_weight,
    value_weight,
    output_weight,
    gain_second,
    shift_second,
    gate_weight,
    up_weight,
    down_weight,
    cotangent,
):
    windows = lengths.shape[0]
    span = tensor_size // windows
    held = tokens.shape[0]
    width = tokens.shape[1]
    head_cols = query_weight.shape[1]
    here = lax.axis_index("tensor")
    window, seat = here // span, here % span

    def from_seat(value, shift):
        pairs = [
            (w * span + (s + shift) % span, w * span + s)
            for w in range(windows)
            for s in range(span)
        ]
        return lax.ppermute(value, "tensor", pairs)

    def to_seat(value, shift):
        return from_seat(value, span - shift)

    def from_window(value, shift):
        pairs = [((t + shift * span) % tensor_size, t) for t in range(tensor_size)]
        return lax.ppermute(value, "tensor", pairs)

    def to_window(value, shift):
        return from_window(value, windows - shift)

    def gather_rows(value):
        return value + [from_seat(piece, s) for s in range(1, span) for piece in value]

    def scatter(partial):
        sent = [to_seat(partial(s * held, held), s) for s in range(1, span)]
        return [partial(0, held)] + sent

    def all_windows(value):
        return [value] + [from_window(value, shift) for shift in range(1, windows)]

    def spread_windows(values):
        group = lax.axis_index("dp")
        sizes = [value.shape[0] // dp_size for value in values]
        mine = jnp.concatenate(
            [
                lax.dynamic_slice_in_dim(value, group * size, size, axis=0).reshape(-1, width)
                for value, size in zip(values, sizes)
            ],
            axis=0,
        )
        return [mine], [from_window(mine, shift) for shift in range(1, windows)]

    def gather_spread(values, piece):
        gathered = lax.all_gather(piece, "dp", axis=0)
        if all(value.shape == (width, width) for value in values):
            return [(gathered, plane) for plane in range(len(values))]
        out, start = [], 0
        for value in values:
            count = value.size // width // dp_size
            out.append(gathered[:, start : start + count].reshape(value.shape))
            start += count
        return out

    def after(value, *others):
        return lax.optimization_barrier((value, *others))[0]

    def pieces_after(pieces, *others):
        return [after(pieces[0], *others)] + pieces[1:]

    place = jnp.stack(
        [lax.dynamic_index_in_dim(lengths, window, keepdims=False), seat * held]
    ).astype(jnp.int32)
    cosines, sines = rope_tables(seat * held)

    members = [[s] for s in range(windows)] if head_cols % LANES == 0 else [list(range(windows))]
    feed_weights = [gate_weight, up_weight, down_weight]
    slices_sent, slices = spread_windows(feed_weights)
    _, normed_one = norm(after(tokens, *slices_sent), [], gain_first, shift_first)
    full_one = gather_rows(normed_one)
    qkv_own = jnp.concatenate([query_weight, key_weight, value_weight], axis=1)
    qkv_other = all_windows(after(qkv_own, *slices))[1:]
    qkv_shards = [qkv_own] + qkv_other
    def joined(parts, axis):
        return parts[0] if len(parts) == 1 else jnp.concatenate(parts, axis=axis)

    def part_of(value, part):
        return value[:, part * head_cols : (part + 1) * head_cols]

    qkv_weights = [
        qkv_shards[group[0]]
        if len(group) == 1
        else joined([part_of(qkv_shards[s], part) for part in range(3) for s in group], 1)
        for group in members
    ]
    target = gather_rows([cotangent])
    qkv, attended = [], []
    rows_one = full_one
    for weight in qkv_weights:
        parts = project(rows_one, weight, cosines, sines)
        if not qkv:
            slices = [after(piece, parts[0]) for piece in slices]
            feed_shards = [feed_weights]
            feed_shards += [gather_spread(feed_weights, piece) for piece in slices]
        waits = slices if not qkv else target
        qkv.append((after(parts[0], *waits), *parts[1:]))
        attended.append(attend(place, *qkv[-1]))
        if len(attended) == 1:
            sent = after(output_weight, attended[0][0])
            output_shards = [output_weight] + all_windows(sent)[1:]
        rows_one = pieces_after(full_one, attended[-1][0])

    out_weights = [joined([output_shards[s] for s in group], 0) for group in members]
    mixer_terms = [
        (mixed, None, weight, None, 0) for (mixed, _), weight in zip(attended, out_weights)
    ]
    hidden_one, normed_two = norm(
        tokens,
        scatter(lambda start, rows: sum_products(mixer_terms, start, rows)),
        gain_second,
        shift_second,
    )
    full_two = gather_rows(normed_two)

    flip = [(d, d ^ 1) for d in range(dp_size)]
    odd = lax.axis_index("dp") % 2

    def half(value, which):
        count = value.shape[0] // 2
        return lax.dynamic_slice_in_dim(value, which * count, count, axis=0)

    def total(pieces, which):
        return sum(half(piece, which).astype(F32) for piece in pieces).astype(BF16)

    def swap_half(pieces, *others):
        pieces = [after(piece, *others) for piece in pieces]
        mine, sent = total(pieces, odd), total(pieces, 1 - odd)
        return (mine, lax.ppermute(sent, "dp", flip)), [mine, sent]

    def add_half(halves, *others):
        mine, received = (after(value, *others) for value in halves)
        return (mine.astype(F32) + received.astype(F32)).astype(BF16)

    def sum_half(value, turn):
        groups = [list(range(0, dp_size, 2)), list(range(1, dp_size, 2))]
        if turn & 1:
            groups = groups[::-1]
        if turn & 2:
            groups = [group[::-1] for group in groups]
        return lax.psum(value, "dp", axis_index_groups=groups)

    def swap_sum(mine, *others):
        mine = after(mine, *others)
        return mine, lax.ppermute(mine, "dp", flip)

    def whole_sum(halves, *others):
        mine, received = (after(value, *others) for value in halves)
        first, second = jnp.where(odd == 0, mine, received), jnp.where(odd == 0, received, mine)
        return jnp.concatenate([first, second], axis=0).astype(F32)

    def send_to_owner(parts):
        return [to_window(parts[shift], shift) for shift in range(1, windows)]

    order = list(range(1, windows)) + [0]
    fed = {}
    rows_two = full_two
    for s in order:
        fed[s] = feed(rows_two, target, feed_shards[s])
        rows_two = pieces_after(full_two, fed[s][0])
    down_pieces, up_pieces, gate_pieces = (
        send_to_owner({s: fed[s][k] for s in order}) + [fed[0][k]] for k in (5, 4, 3)
    )
    two_terms, feed_terms = [], []
    for s in order:
        gate, up, down = feed_shards[s]
        two_terms += [(fed[s][1], None, gate, None, 1), (fed[s][2], None, up, None, 1)]
        feed_terms.append((fed[s][0], None, down, None, 0))

    two_sent = [
        sum_products(two_terms, shift * held, held, BF16) for shift in range(1, span)
    ]
    down_half, marks = swap_half(down_pieces, *two_sent)
    two_terms = [(after(two_terms[0][0], *marks), *two_terms[0][1:])] + two_terms[1:]
    two_kept = sum_products(two_terms, 0, held)
    grad_branch_own, grad_hidden, norm_two = norm_back(
        hidden_one,
        cotangent,
        gain_second,
        [two_kept] + [to_seat(part, shift + 1) for shift, part in enumerate(two_sent)],
        False,
    )
    grad_branch = gather_rows(grad_branch_own)
    down_half = add_half(down_half, *grad_branch_own)
    down_sum = sum_half(down_half, 0)
    grad_branch = pieces_after(grad_branch, down_half)

    members = members[::-1]
    out_weights, qkv_weights = out_weights[::-1], qkv_weights[::-1]
    qkv, attended = qkv[::-1], attended[::-1]
    grad_mixed, found = branch_back(grad_branch, out_weights, [mixed for mixed, _ in attended])
    out_grads = {
        s: out_grad[spot * head_cols : (spot + 1) * head_cols]
        for group, out_grad in zip(members, found)
        for spot, s in enumerate(group)
    }
    out_pieces = send_to_owner(out_grads) + [out_grads[0]]

    def up_swap(last):
        sums["up"], waits = swap_half(up_pieces, *last)
        return waits

    def up_sum(last):
        value = add_half(sums["up"], *last)
        sums["up"] = sum_half(value, 1)
        return [value]

    def gate_swap(last):
        sums["gate"], waits = swap_half(gate_pieces, *last)
        sums["out"], more = swap_half(out_pieces, *last)
        sums["down"] = after(down_sum, *waits, *more)
        return waits + more + [sums["down"]]

    def gate_sum(last):
        values = add_half(sums["gate"], *last), add_half(sums["out"], *last)
        sums["gate"], sums["out"] = sum_half(values, 2)
        sums["up"] = swap_sum(sums["up"], *last)
        sums["down"] = swap_sum(sums["down"], *last)
        return [*values, sums["up"][0]]

    along = exchanges("dp", dp_size)
    exchange = exchanges("tensor", tensor_size) + along[1:] + along[:1]
    sums = {}
    moves = [up_swap, up_sum, gate_swap, gate_sum]
    last = list(grad_mixed)
    grad_qkv, qkv_grads = [], {}
    for index, group in enumerate(members):
        mixed, logs = attended[index]
        count = len(group) * head_cols
        grads = None
        for pair in range(count // LANES):
            waits = moves.pop(0)(last) if moves else last
            grads = attend_back(
                place,
                *qkv[index],
                mixed,
                after(grad_mixed[index], *waits),
                logs,
                cosines,
                sines,
                pair,
                grads,
            )
            last = [grads]
        grad_qkv.append(grads)
        qkv_grad = outer(full_one, grads)
        last = [qkv_grad]
        for spot, s in enumerate(group):
            if len(group) == 1:
                qkv_grads[s] = qkv_grad
            else:
                qkv_grads[s] = joined(
                    [
                        lax.slice_in_dim(
                            qkv_grad,
                            part * count + spot * head_cols,
                            part * count + (spot + 1) * head_cols,
                            axis=1,
                        )
                        for part in range(3)
                    ],
                    1,
                )
    for move in moves:
        last = move(last)

    qkv_half, marks = swap_half(send_to_owner(qkv_grads) + [qkv_grads[0]])
    grad_up = whole_sum(sums["up"], *marks)
    feed_terms[0] = (after(feed_terms[0][0], grad_up), *feed_terms[0][1:])
    one_terms = [
        (grad_qkv[index], part, weight, part, 1)
        for index, weight in enumerate(qkv_weights)
        for part in range(3)
    ]

    def later(terms, *others):
        return [(after(terms[0][0], *others), *terms[0][1:])] + terms[1:]

    shifts = range(1, span)
    feed_sent = [sum_products(feed_terms, shift * held, held, BF16) for shift in shifts]
    qkv_half = add_half(qkv_half, *feed_sent)
    gate_halves = swap_sum(sums["gate"], *feed_sent)
    out_halves = swap_sum(sums["out"], *feed_sent)
    qkv_sum = sum_half(after(qkv_half, gate_halves[0], out_halves[0]), 3)
    grad_down = whole_sum(sums["down"], *feed_sent)
    one_terms = later(one_terms, qkv_half, gate_halves[0], grad_down)
    one_sent = [sum_products(one_terms, shift * held, held, BF16) for shift in shifts]
    feed_parts = [sum_products(later(feed_terms, *one_sent), 0, held)]
    one_parts = [sum_products(later(one_terms, feed_parts[0]), 0, held)]
    feed_parts += [to_seat(part, shift) for shift, part in zip(shifts, feed_sent)]
    one_parts += [to_seat(part, shift) for shift, part in zip(shifts, one_sent)]
    output = (hidden_one + sum(feed_parts)).astype(BF16)
    (input_grad,), _, norm_one = norm_back(tokens, grad_hidden, gain_first, one_parts, True, 1)
    window = [input_grad, output]
    qkv_halves = swap_sum(qkv_sum, *window)
    norms = jnp.concatenate([after(norm_one, qkv_halves[0]), norm_two], axis=0)
    for step in exchange:
        norms = step(norms)
    grad_gate = whole_sum(gate_halves, qkv_halves[0])
    out_grad = whole_sum(out_halves, qkv_halves[0])
    qkv_grad = whole_sum(qkv_halves)
    return (
        output,
        input_grad,
        *(part_of(qkv_grad, part) for part in range(3)),
        out_grad,
        grad_gate,
        grad_up,
        grad_down,
        norms[0],
        norms[1],
        norms[2],
        norms[3],
    )


def solution(mesh):
    rows = P(("dp", "tensor"), None)
    columns = P(None, "tensor")
    depth = P("tensor", None)
    return jax.shard_map(
        functools.partial(shards, mesh.shape["dp"], mesh.shape["tensor"]),
        mesh=mesh,
        in_specs=(
            rows,
            P("dp"),
            P(),
            P(),
            columns,
            columns,
            columns,
            depth,
            P(),
            P(),
            columns,
            columns,
            depth,
            rows,
        ),
        out_specs=(
            rows,
            rows,
            columns,
            columns,
            columns,
            depth,
            columns,
            columns,
            depth,
            P(),
            P(),
            P(),
            P(),
        ),
        check_vma=False,
    )
```

```python
import functools
import math

import jax
import jax.numpy as jnp
from jax import lax
from jax.experimental import pallas as pl
from jax.experimental.pallas import tpu as pltpu
from jax.sharding import PartitionSpec as P

HD = 64
LEN = 2048
EPSILON = 1e-05
MASKED = -1e30
LANES = 128
LOG2E = math.log2(math.e)
BF16 = jnp.bfloat16
F32 = jnp.float32
MIB = 1 << 20
COST_SHARE = 0.1
PIECES = 2


def contract(left, right, left_dim, right_dim):
    return lax.dot_general(
        left, right, (((left_dim,), (right_dim,)), ((), ())), preferred_element_type=F32
    )


def cost(flops, moved, transcendentals=0):
    return pl.CostEstimate(
        flops=int(flops * COST_SHARE),
        bytes_accessed=int(moved * COST_SHARE),
        transcendentals=int(transcendentals * COST_SHARE),
    )


def swap_halves(value):
    columns = value.shape[1]
    lane = lax.broadcasted_iota(jnp.int32, value.shape, 1)
    return jnp.where(
        lane % HD < HD // 2,
        pltpu.roll(value, columns - HD // 2, 1),
        pltpu.roll(value, HD // 2, 1),
    )


def fetch(pieces, rows, sems):
    copies, start = [], 0
    for index, piece in enumerate(pieces):
        count = piece.shape[0]
        copies.append(
            pltpu.make_async_copy(piece, rows.at[pl.ds(start, count), :], sems.at[index])
        )
        start += count
    for copy in copies:
        copy.start()
    return copies


def room(pieces):
    count = sum(piece.shape[0] for piece in pieces)
    return [
        pltpu.VMEM((count, pieces[0].shape[1]), BF16),
        pltpu.SemaphoreType.DMA((len(pieces),)),
    ]


def unpacked(ref):
    value = ref[...]
    return value.reshape(-1, value.shape[-1]) if value.ndim == 3 else value


def packed(weight):
    return isinstance(weight, tuple)


def project_kernel(*refs, count):
    pieces = refs[:count]
    weight_ref, cos_ref, sin_ref, q_ref, k_ref, v_ref, rows, sems = refs[count:]
    columns = q_ref.shape[1]
    block = q_ref.shape[0]

    @pl.when(pl.program_id(0) == 0)
    def _():
        for copy in fetch(pieces, rows, sems):
            copy.wait()

    start = pl.multiple_of(pl.program_id(0) * block, block)
    product = contract(rows[pl.ds(start, block), :], weight_ref[...], 1, 0)
    cosines = jnp.concatenate([cos_ref[...]] * (columns // LANES), axis=1)
    sines = jnp.concatenate([sin_ref[...]] * (columns // LANES), axis=1)
    for part, out_ref in ((0, q_ref), (1, k_ref)):
        value = product[:, part * columns : (part + 1) * columns]
        out_ref[...] = (value * cosines + swap_halves(value) * sines).astype(BF16)
    v_ref[...] = product[:, 2 * columns :].astype(BF16)


def project(pieces, weight, cosines, sines, block=512):
    width = weight.shape[0]
    columns = weight.shape[1] // 3
    count = sum(piece.shape[0] for piece in pieces)
    table = pl.BlockSpec((block, LANES), lambda i: (i, 0))
    out = pl.BlockSpec((block, columns), lambda i: (i, 0))
    return pl.pallas_call(
        functools.partial(project_kernel, count=len(pieces)),
        grid=(count // block,),
        in_specs=[pl.BlockSpec(memory_space=pl.ANY)] * len(pieces)
        + [pl.BlockSpec(weight.shape, lambda i: (0, 0)), table, table],
        out_specs=[out, out, out],
        out_shape=[jax.ShapeDtypeStruct((count, columns), BF16)] * 3,
        scratch_shapes=room(pieces),
        cost_estimate=cost(
            2 * count * width * 3 * columns,
            2 * (count * width + width * 3 * columns + count * 3 * columns),
        ),
        compiler_params=pltpu.CompilerParams(vmem_limit_bytes=40 * MIB),
        name="project_rope",
    )(*pieces, weight, cosines, sines)


def masked_keys(place_ref, key_ref, masked_ref):
    count = key_ref.shape[0]
    lane = lax.broadcasted_iota(jnp.int32, (count, LANES), 1)
    row = lax.broadcasted_iota(jnp.int32, (count, LANES), 0) + place_ref[1]
    position = jnp.where(row >= count, row - count, row)
    bias = jnp.where(position >= place_ref[0], MASKED, 0.0).astype(BF16)
    nothing = jnp.zeros_like(bias)
    key = key_ref[...]
    masked_ref[0] = jnp.where(lane < HD, key, jnp.where(lane == HD, bias, nothing))
    masked_ref[1] = jnp.where(lane >= HD, key, jnp.where(lane == 0, bias, nothing))


def masked_queries(query):
    lane = lax.broadcasted_iota(jnp.int32, query.shape, 1)
    scaled = query * jnp.asarray(1.0 / math.sqrt(HD), BF16)
    one = jnp.ones_like(query)
    nothing = jnp.zeros_like(query)
    return (
        scaled,
        jnp.where(lane < HD, scaled, jnp.where(lane == HD, one, nothing)),
        jnp.where(lane >= HD, scaled, jnp.where(lane == 0, one, nothing)),
    )


def attend_kernel(place_ref, q_ref, k_ref, v_ref, out_ref, log_ref, keys, values_t, *, chunk):
    count = k_ref.shape[0]

    @pl.when(pl.program_id(1) == 0)
    def _():
        masked_keys(place_ref, k_ref, keys)
        values_t[...] = v_ref[...].T

    queries = masked_queries(q_ref[...])[1:]
    mixed, logs = [], []
    for head in range(2):
        scores = [
            contract(keys[head, start : start + chunk, :], queries[head], 1, 1)
            for start in range(0, count, chunk)
        ]
        top = functools.reduce(
            jnp.maximum, [jnp.max(block, axis=0, keepdims=True) for block in scores]
        )
        total = 0.0
        summed = 0.0
        for index, block in enumerate(scores):
            weights = jnp.exp2((block - top) * LOG2E)
            total = total + jnp.sum(weights, axis=0, keepdims=True)
            value = values_t[
                head * HD : (head + 1) * HD, index * chunk : (index + 1) * chunk
            ]
            summed = summed + contract(value, weights.astype(BF16), 1, 0)
        mixed.append(summed / total)
        logs.append(top * LOG2E + jnp.log2(total))
    out_ref[...] = jnp.concatenate(mixed, axis=0).T.astype(BF16)
    log_ref[0] = jnp.concatenate(logs + [jnp.zeros((6, q_ref.shape[0]), F32)], axis=0)


def attend(place, queries, keys, values, block=1024, chunk=2048):
    count, columns = queries.shape
    pairs = columns // LANES
    whole = pl.BlockSpec((count, LANES), lambda p, i, _: (0, p))
    rows = pl.BlockSpec((block, LANES), lambda p, i, _: (i, p))
    return pl.pallas_call(
        functools.partial(attend_kernel, chunk=chunk),
        grid_spec=pltpu.PrefetchScalarGridSpec(
            num_scalar_prefetch=1,
            grid=(pairs, count // block),
            in_specs=[rows, whole, whole],
            out_specs=[rows, pl.BlockSpec((1, 8, block), lambda p, i, _: (p, 0, i))],
            scratch_shapes=[
                pltpu.VMEM((2, count, LANES), BF16),
                pltpu.VMEM((LANES, count), BF16),
            ],
        ),
        out_shape=[
            jax.ShapeDtypeStruct((count, columns), BF16),
            jax.ShapeDtypeStruct((pairs, 8, count), F32),
        ],
        cost_estimate=cost(16 * count * count * columns, 8 * count * columns, count * count * columns // HD),
        compiler_params=pltpu.CompilerParams(vmem_limit_bytes=56 * MIB),
        name="attention_forward",
    )(place, queries, keys, values)


def attend_back_kernel(
    place_ref,
    q_ref,
    k_ref,
    v_ref,
    out_ref,
    up_ref,
    log_ref,
    cos_row_ref,
    sin_row_ref,
    cos_ref,
    sin_ref,
    *rest,
    chunk,
):
    grad_ref, keys, grad_keys_t, grad_values_t = rest[-4:]
    count = k_ref.shape[0]
    step = pl.program_id(1)

    @pl.when(step == 0)
    def _():
        masked_keys(place_ref, k_ref, keys)
        grad_keys_t[...] = jnp.zeros_like(grad_keys_t)
        grad_values_t[...] = jnp.zeros_like(grad_values_t)

    scaled, *queries = masked_queries(q_ref[...])
    upstream = up_ref[...]
    lane = lax.broadcasted_iota(jnp.int32, upstream.shape, 1)
    nothing = jnp.zeros_like(upstream)
    products = upstream.astype(F32) * out_ref[...].astype(F32)
    scaled_t = scaled.T
    upstream_t = upstream.T
    logs = log_ref[0].T
    grad_queries = []
    for head in range(2):
        mine = (lane < HD) == (head == 0)
        own_upstream = jnp.where(mine, upstream, nothing)
        row_dot = jnp.sum(jnp.where(mine, products, 0.0), axis=1, keepdims=True)
        log_total = logs[:, head : head + 1]
        heads = slice(head * HD, (head + 1) * HD)
        grad_query = 0.0
        for start in range(0, count, chunk):
            span = slice(start, start + chunk)
            scores = contract(queries[head], keys[head, span, :], 1, 1)
            probs = jnp.exp2(scores * LOG2E - log_total)
            grad_probs = contract(own_upstream, v_ref[span, :], 1, 1)
            grad_scores = (probs * (grad_probs - row_dot)).astype(BF16)
            grad_values_t[heads, span] += contract(
                upstream_t[heads, :], probs.astype(BF16), 1, 0
            )
            grad_keys_t[heads, span] += contract(scaled_t[heads, :], grad_scores, 1, 0)
            grad_query = grad_query + contract(grad_scores, k_ref[span, :], 1, 0)
        grad_queries.append(grad_query)
    grad_query = jnp.where(lane < HD, *grad_queries) * (1.0 / math.sqrt(HD))
    block = grad_query.shape[0]
    grad_ref[0, pl.ds(pl.multiple_of(step * block, block), block), :] = (
        grad_query * cos_row_ref[...] - swap_halves(grad_query) * sin_row_ref[...]
    ).astype(BF16)

    @pl.when(step == pl.num_programs(1) - 1)
    def _():
        grad_key = grad_keys_t[...].T
        grad_ref[1] = (
            grad_key * cos_ref[...] - swap_halves(grad_key) * sin_ref[...]
        ).astype(BF16)
        grad_ref[2] = grad_values_t[...].T.astype(BF16)


def attend_back(
    place, queries, keys, values, mixed, upstream, logs, cosines, sines, pair, grads, block=512, chunk=512
):
    count, columns = queries.shape
    whole = pl.BlockSpec((count, LANES), lambda p, i, _: (0, pair))
    rows = pl.BlockSpec((block, LANES), lambda p, i, _: (i, pair))
    table = pl.BlockSpec((count, LANES), lambda p, i, _: (0, 0))
    table_rows = pl.BlockSpec((block, LANES), lambda p, i, _: (i, 0))
    held = [] if grads is None else [grads]
    return pl.pallas_call(
        functools.partial(attend_back_kernel, chunk=chunk),
        grid_spec=pltpu.PrefetchScalarGridSpec(
            num_scalar_prefetch=1,
            grid=(1, count // block),
            in_specs=[
                rows,
                whole,
                whole,
                rows,
                rows,
                pl.BlockSpec((1, 8, block), lambda p, i, _: (pair, 0, i)),
                table_rows,
                table_rows,
                table,
                table,
            ]
            + [pl.BlockSpec(memory_space=pl.ANY)] * len(held),
            out_specs=pl.BlockSpec((3, count, LANES), lambda p, i, _: (0, 0, pair)),
            scratch_shapes=[
                pltpu.VMEM((2, count, LANES), BF16),
                pltpu.VMEM((LANES, count), F32),
                pltpu.VMEM((LANES, count), F32),
            ],
        ),
        out_shape=jax.ShapeDtypeStruct((3, count, columns), BF16),
        input_output_aliases={11: 0} if held else {},
        cost_estimate=cost(28 * count * count * LANES, 16 * count * LANES, count * count * 2),
        compiler_params=pltpu.CompilerParams(vmem_limit_bytes=60 * MIB),
        name="attention_backward",
    )(place, queries, keys, values, mixed, upstream, logs, cosines, sines, cosines, sines, *held)


def feed_kernel(*refs, counts, chunk):
    row_pieces, target_pieces = refs[: counts[0]], refs[counts[0] : sum(counts)]
    refs = refs[sum(counts) :]
    gate_ref, up_ref, down_ref, inner_ref, grad_gate_ref, grad_up_ref = refs[:6]
    weight_gate_ref, weight_up_ref, weight_down_ref = refs[6:9]
    rows, row_sems, target, target_sems, rows_t, target_t = refs[9:]

    @pl.when(pl.program_id(0) == 0)
    def _():
        copies = fetch(row_pieces, rows, row_sems) + fetch(target_pieces, target, target_sems)
        for copy in copies:
            copy.wait()
        rows_t[...] = rows[...].T
        target_t[...] = target[...].T

    gate_weight, up_weight, down_weight = unpacked(gate_ref), unpacked(up_ref), unpacked(down_ref)
    for start in range(0, rows.shape[0], chunk):
        span = slice(start, start + chunk)
        gate = contract(rows[span, :], gate_weight, 1, 0)
        up = contract(rows[span, :], up_weight, 1, 0)
        grad_inner = contract(target[span, :], down_weight, 1, 1)
        share = jax.nn.sigmoid(gate)
        activated = gate * share
        inner_ref[span, :] = (activated * up).astype(BF16)
        grad_up_ref[span, :] = (grad_inner * activated).astype(BF16)
        grad_gate_ref[span, :] = (
            grad_inner * up * share * (1.0 + gate * (1.0 - share))
        ).astype(BF16)
    weight_gate_ref[...] = contract(rows_t[...], grad_gate_ref[...], 1, 0).astype(BF16)
    weight_up_ref[...] = contract(rows_t[...], grad_up_ref[...], 1, 0).astype(BF16)
    weight_down_ref[...] = contract(target_t[...], inner_ref[...], 1, 0).T.astype(BF16)


def feed(rows, target, weights, block=256, chunk=512):
    count = sum(piece.shape[0] for piece in rows)
    width = rows[0].shape[1]
    across_spec = lambda units: pl.BlockSpec((width, min(block, units)), lambda i: (0, i))
    down_spec = lambda units: pl.BlockSpec((min(block, units), width), lambda i: (i, 0))
    if packed(weights[0]):
        units = width
        replicas, deep = weights[0][0].shape[0], width // weights[0][0].shape[0]
        specs = [
            pl.BlockSpec((replicas, deep, block), lambda i, plane=weights[k][1]: (0, plane, i))
            for k in range(2)
        ] + [
            pl.BlockSpec(
                (block // deep, deep, width), lambda i, plane=weights[2][1]: (i, plane, 0)
            )
        ]
        weights = [weight for weight, _ in weights]
    else:
        units = weights[0].shape[1]
        specs = [across_spec(units)] * 2 + [down_spec(units)]
    block = min(block, units)
    out = pl.BlockSpec((count, block), lambda i: (0, i))
    return pl.pallas_call(
        functools.partial(feed_kernel, counts=(len(rows), len(target)), chunk=chunk),
        grid=(units // block,),
        in_specs=[pl.BlockSpec(memory_space=pl.ANY)] * (len(rows) + len(target)) + specs,
        out_specs=[out, out, out] + [across_spec(units)] * 2 + [down_spec(units)],
        out_shape=[jax.ShapeDtypeStruct((count, units), BF16)] * 3
        + [jax.ShapeDtypeStruct((width, units), BF16)] * 2
        + [jax.ShapeDtypeStruct((units, width), BF16)],
        scratch_shapes=room(rows) + room(target) + [pltpu.VMEM((width, count), BF16)] * 2,
        cost_estimate=cost(
            12 * count * width * units,
            4 * count * width + 12 * width * units + 6 * count * units,
            2 * count * units,
        ),
        compiler_params=pltpu.CompilerParams(vmem_limit_bytes=60 * MIB),
        name="feed_forward",
    )(*rows, *target, *weights)


def sum_kernel(*refs, places, dims, start, chunk):
    terms = len(dims)
    operands, out_ref = refs[: 2 * terms], refs[2 * terms]
    buffers = refs[2 * terms + 1 : 4 * terms + 1]
    total, result, sems, out_sems = refs[4 * terms + 1 :]
    rows = total.shape[0]
    copies = []
    for index, (ref, place) in enumerate(zip(operands, places)):
        copy = pltpu.make_async_copy(ref.at[place], buffers[index], sems.at[index])
        copy.start()
        copies.append(copy)
    sent = []
    for index, dim in enumerate(dims):
        copies[2 * index].wait()
        copies[2 * index + 1].wait()
        right = unpacked(buffers[2 * index + 1])
        for first in range(0, rows, chunk):
            span = slice(first, first + chunk)
            product = contract(buffers[2 * index][span, :], right, 1, dim)
            if index:
                product = total[span, :] + product
            if index + 1 < terms:
                total[span, :] = product
                continue
            result[span, :] = product.astype(result.dtype)
            copy = pltpu.make_async_copy(
                result.at[pl.ds(first, chunk), :],
                out_ref.at[pl.ds(first, chunk), :],
                out_sems.at[first // chunk],
            )
            copy.start()
            sent.append(copy)
    for copy in sent:
        copy.wait()


def sum_products(terms, start, rows, dtype=F32, chunk=256):
    chunk = min(chunk, rows)
    operands, places, shapes, dims, flops, moved = [], [], [], [], 0, 0
    for left, plane, right, part, dim in terms:
        depth = left.shape[-1]
        span = pl.ds(start, rows)
        places.append((span, slice(None)) if plane is None else (plane, span, slice(None)))
        shapes.append((rows, depth))
        if packed(right):
            right, plane = right
            width = right.shape[2]
            deep = width // right.shape[0]
            places.append((slice(None), pl.ds(plane * deep, deep), slice(None)))
            shapes.append((right.shape[0], deep, width))
        else:
            column = pl.ds(0, right.shape[1]) if part is None else pl.ds(part * depth, depth)
            places.append((slice(None), column))
            shapes.append((right.shape[0], column.size))
            width = shapes[-1][1 - dim]
        operands += [left, right]
        dims.append(dim)
        flops += 2 * rows * depth * width
        moved += 2 * rows * depth + 2 * depth * width
    anywhere = pl.BlockSpec(memory_space=pl.ANY)
    return pl.pallas_call(
        functools.partial(
            sum_kernel, places=places, dims=tuple(dims), start=start, chunk=chunk
        ),
        in_specs=[anywhere] * len(operands),
        out_specs=anywhere,
        out_shape=jax.ShapeDtypeStruct((rows, width), dtype),
        scratch_shapes=[pltpu.VMEM(shape, BF16) for shape in shapes]
        + [
            pltpu.VMEM((rows, width), F32),
            pltpu.VMEM((rows, width), dtype),
            pltpu.SemaphoreType.DMA((len(operands),)),
            pltpu.SemaphoreType.DMA((rows // chunk,)),
        ],
        cost_estimate=cost(flops, moved + 4 * rows * width),
        compiler_params=pltpu.CompilerParams(vmem_limit_bytes=58 * MIB),
        name="sum_products",
    )(*operands)


def outer_kernel(*refs, count):
    right_ref, out_ref, left, sems, left_t = refs[count:]

    @pl.when(pl.program_id(0) == 0)
    def _():
        for copy in fetch(refs[:count], left, sems):
            copy.wait()
        left_t[...] = left[...].T

    out_ref[...] = contract(left_t[...], right_ref[...], 1, 0).astype(BF16)


def outer(pieces, right):
    width = pieces[0].shape[1]
    planes, count, columns = right.shape
    return pl.pallas_call(
        functools.partial(outer_kernel, count=len(pieces)),
        grid=(planes,),
        in_specs=[pl.BlockSpec(memory_space=pl.ANY)] * len(pieces)
        + [pl.BlockSpec((None, count, columns), lambda i: (i, 0, 0))],
        out_specs=pl.BlockSpec((width, columns), lambda i: (0, i)),
        out_shape=jax.ShapeDtypeStruct((width, planes * columns), BF16),
        scratch_shapes=room(pieces) + [pltpu.VMEM((width, count), BF16)],
        cost_estimate=cost(
            2 * count * width * planes * columns,
            2 * count * (width + planes * columns) + 2 * width * planes * columns,
        ),
        compiler_params=pltpu.CompilerParams(vmem_limit_bytes=40 * MIB),
        name="outer_product",
    )(*pieces, right)


def branch_kernel(*refs, count, groups, chunk):
    weights = refs[count : count + groups]
    mixed = refs[count + groups : count + 2 * groups]
    outs = refs[count + 2 * groups : count + 4 * groups]
    rows, sems = refs[count + 4 * groups :]
    for copy in fetch(refs[:count], rows, sems):
        copy.wait()
    for index in range(groups):
        outs[groups + index][...] = contract(mixed[index][...].T, rows[...], 1, 0).astype(BF16)
        for start in range(0, rows.shape[0], chunk):
            span = slice(start, start + chunk)
            outs[index][span, :] = contract(rows[span, :], weights[index][...], 1, 1).astype(BF16)


def branch_back(pieces, weights, mixed, chunk=512):
    count = sum(piece.shape[0] for piece in pieces)
    width = pieces[0].shape[1]
    groups = len(weights)
    vmem = pl.BlockSpec(memory_space=pltpu.VMEM)
    columns = [weight.shape[0] for weight in weights]
    results = pl.pallas_call(
        functools.partial(branch_kernel, count=len(pieces), groups=groups, chunk=chunk),
        in_specs=[pl.BlockSpec(memory_space=pl.ANY)] * len(pieces) + [vmem] * (2 * groups),
        out_specs=[vmem] * (2 * groups),
        out_shape=[jax.ShapeDtypeStruct((count, size), BF16) for size in columns]
        + [jax.ShapeDtypeStruct((size, width), BF16) for size in columns],
        scratch_shapes=room(pieces),
        cost_estimate=cost(4 * count * width * sum(columns), 6 * count * width),
        compiler_params=pltpu.CompilerParams(vmem_limit_bytes=48 * MIB),
        name="branch_backward",
    )(*pieces, *weights, *mixed)
    return results[:groups], results[groups:]


def standardize(value):
    centred = value - jnp.mean(value, axis=-1, keepdims=True)
    scale = lax.rsqrt(jnp.mean(centred * centred, axis=-1, keepdims=True) + EPSILON)
    return centred * scale, scale


def norm_kernel(*refs, added):
    value = refs[0][...].astype(F32)
    for ref in refs[1 : 1 + added]:
        value = value + ref[...].astype(F32)
    gain_ref, shift_ref = refs[1 + added : 3 + added]
    standard, _ = standardize(value)
    if added:
        refs[-2][...] = value
    refs[-1][...] = (standard * gain_ref[...] + shift_ref[...]).astype(BF16)


def norm(base, terms, gain, shift, pieces=PIECES, block=256):
    count, width = base.shape
    rows = count // pieces
    block = min(block, rows)
    vector = pl.BlockSpec((1, width), lambda i: (0, 0))
    total, out = None, []
    for piece in range(pieces):
        first = piece * rows // block
        whole = pl.BlockSpec((block, width), lambda i, first=first: (first + i, 0))
        shapes = [jax.ShapeDtypeStruct((rows, width), BF16)]
        specs = [pl.BlockSpec((block, width), lambda i: (i, 0))]
        held = []
        if terms:
            shapes = [jax.ShapeDtypeStruct((count, width), F32)] + shapes
            specs = [whole] + specs
            held = [] if total is None else [total]
        results = pl.pallas_call(
            lambda *refs, held=len(held): norm_kernel(
                *refs[: 3 + len(terms)], *refs[3 + len(terms) + held :], added=len(terms)
            ),
            grid=(rows // block,),
            in_specs=[whole] * (1 + len(terms))
            + [vector, vector]
            + [pl.BlockSpec(memory_space=pl.ANY)] * len(held),
            out_specs=specs,
            out_shape=shapes,
            input_output_aliases={3 + len(terms): 0} if held else {},
            cost_estimate=cost(16 * rows * width, 8 * rows * width * len(shapes)),
            name="layer_norm",
        )(base, *terms, gain.reshape(1, width), shift.reshape(1, width), *held)
        out.append(results[-1])
        if terms:
            total = results[0]
    return total, out


def norm_back_kernel(*refs, added, low):
    base_ref, straight_ref, gain_ref = refs[:3]
    upstream = refs[3][...].astype(F32)
    for ref in refs[4 : 3 + added]:
        upstream = upstream + ref[...].astype(F32)
    outs = refs[3 + added :]
    standard, scale = standardize(base_ref[...].astype(F32))
    scaled = upstream * gain_ref[...]
    back = straight_ref[...].astype(F32) + scale * (
        scaled
        - jnp.mean(scaled, axis=-1, keepdims=True)
        - standard * jnp.mean(scaled * standard, axis=-1, keepdims=True)
    )
    outs[0][...] = back.astype(BF16)
    if not low:
        outs[1][...] = back
    sums = jnp.concatenate(
        [
            jnp.sum(upstream * standard, axis=0, keepdims=True),
            jnp.sum(upstream, axis=0, keepdims=True),
        ],
        axis=0,
    )

    @pl.when(pl.program_id(0) == 0)
    def _():
        outs[-1][...] = sums

    @pl.when(pl.program_id(0) > 0)
    def _():
        outs[-1][...] += sums


def norm_back(base, straight, gain, terms, low, pieces=PIECES, block=256):
    count, width = base.shape
    rows = count // pieces
    block = min(block, rows)
    total, out, found = None, [], []
    for piece in range(pieces):
        first = piece * rows // block
        whole = pl.BlockSpec((block, width), lambda i, first=first: (first + i, 0))
        shapes = [jax.ShapeDtypeStruct((rows, width), BF16)]
        specs = [pl.BlockSpec((block, width), lambda i: (i, 0))]
        held = []
        if not low:
            shapes.append(jax.ShapeDtypeStruct((count, width), F32))
            specs.append(whole)
            held = [] if total is None else [total]
        results = pl.pallas_call(
            lambda *refs, held=len(held): norm_back_kernel(
                *refs[: 3 + len(terms)],
                *refs[3 + len(terms) + held :],
                added=len(terms),
                low=low,
            ),
            grid=(rows // block,),
            in_specs=[whole, whole, pl.BlockSpec((1, width), lambda i: (0, 0))]
            + [whole] * len(terms)
            + [pl.BlockSpec(memory_space=pl.ANY)] * len(held),
            out_specs=specs + [pl.BlockSpec((2, width), lambda i: (0, 0))],
            out_shape=shapes + [jax.ShapeDtypeStruct((2, width), F32)],
            input_output_aliases={3 + len(terms): 1} if held else {},
            cost_estimate=cost(30 * rows * width, 16 * rows * width),
            name="layer_norm_backward",
        )(base, straight, gain.reshape(1, width), *terms, *held)
        out.append(results[0])
        found.append(results[-1])
        if not low:
            total = results[1]
    return out, total, sum(found)


def rope_tables(offset):
    half = HD // 2
    groups = LANES // half
    count = LEN // groups
    lane = jnp.arange(LANES, dtype=jnp.int32)
    position = jnp.arange(count, dtype=jnp.int32)[:, None] + lane[None, :] // half * count
    position = (position + offset) % LEN
    inverse = 10000.0 ** (-2.0 * (lane % half).astype(F32) / HD)
    angles = position.astype(F32) * inverse[None, :]
    cosines, sines = lax.optimization_barrier((jnp.cos(angles), jnp.sin(angles)))

    def rows(table, signs):
        parts = [table[:, g * half : (g + 1) * half] for g in range(groups)]
        return jnp.concatenate(
            [jnp.concatenate([sign * part for sign in signs], axis=1) for part in parts], axis=0
        )

    return rows(cosines, (1, 1, 1, 1)), rows(sines, (-1, 1, -1, 1))


def exchanges(axis, size):
    if size & (size - 1):
        return [lambda value: lax.psum(value, axis)]
    return [
        lambda value, pairs=[(i, i ^ (1 << bit)) for i in range(size)]: value
        + lax.ppermute(value, axis, pairs)
        for bit in range(size.bit_length() - 1)
    ]


def shards(
    dp_size,
    tensor_size,
    tokens,
    lengths,
    gain_first,
    shift_first,
    query_weight,
    key_weight,
    value_weight,
    output_weight,
    gain_second,
    shift_second,
    gate_weight,
    up_weight,
    down_weight,
    cotangent,
):
    windows = lengths.shape[0]
    span = tensor_size // windows
    held = tokens.shape[0]
    width = tokens.shape[1]
    head_cols = query_weight.shape[1]
    here = lax.axis_index("tensor")
    window, seat = here // span, here % span

    def from_seat(value, shift):
        pairs = [
            (w * span + (s + shift) % span, w * span + s)
            for w in range(windows)
            for s in range(span)
        ]
        return lax.ppermute(value, "tensor", pairs)

    def to_seat(value, shift):
        return from_seat(value, span - shift)

    def from_window(value, shift):
        pairs = [((t + shift * span) % tensor_size, t) for t in range(tensor_size)]
        return lax.ppermute(value, "tensor", pairs)

    def to_window(value, shift):
        return from_window(value, windows - shift)

    def gather_rows(value):
        return value + [from_seat(piece, s) for s in range(1, span) for piece in value]

    def scatter(partial):
        sent = [to_seat(partial(s * held, held), s) for s in range(1, span)]
        return [partial(0, held)] + sent

    def all_windows(value):
        return [value] + [from_window(value, shift) for shift in range(1, windows)]

    def spread_windows(values):
        group = lax.axis_index("dp")
        sizes = [value.shape[0] // dp_size for value in values]
        mine = jnp.concatenate(
            [
                lax.dynamic_slice_in_dim(value, group * size, size, axis=0).reshape(-1, width)
                for value, size in zip(values, sizes)
            ],
            axis=0,
        )
        return [mine], [from_window(mine, shift) for shift in range(1, windows)]

    def gather_spread(values, piece):
        gathered = lax.all_gather(piece, "dp", axis=0)
        if all(value.shape == (width, width) for value in values):
            return [(gathered, plane) for plane in range(len(values))]
        out, start = [], 0
        for value in values:
            count = value.size // width // dp_size
            out.append(gathered[:, start : start + count].reshape(value.shape))
            start += count
        return out

    def after(value, *others):
        return lax.optimization_barrier((value, *others))[0]

    def pieces_after(pieces, *others):
        return [after(pieces[0], *others)] + pieces[1:]

    place = jnp.stack(
        [lax.dynamic_index_in_dim(lengths, window, keepdims=False), seat * held]
    ).astype(jnp.int32)
    cosines, sines = rope_tables(seat * held)

    members = [[s] for s in range(windows)] if head_cols % LANES == 0 else [list(range(windows))]
    feed_weights = [gate_weight, up_weight, down_weight]
    slices_sent, slices = spread_windows(feed_weights)
    _, normed_one = norm(after(tokens, *slices_sent), [], gain_first, shift_first)
    full_one = gather_rows(normed_one)
    qkv_own = jnp.concatenate([query_weight, key_weight, value_weight], axis=1)
    qkv_other = all_windows(after(qkv_own, *slices))[1:]
    qkv_shards = [qkv_own] + qkv_other
    def joined(parts, axis):
        return parts[0] if len(parts) == 1 else jnp.concatenate(parts, axis=axis)

    def part_of(value, part):
        return value[:, part * head_cols : (part + 1) * head_cols]

    qkv_weights = [
        qkv_shards[group[0]]
        if len(group) == 1
        else joined([part_of(qkv_shards[s], part) for part in range(3) for s in group], 1)
        for group in members
    ]
    target = gather_rows([cotangent])
    qkv, attended = [], []
    rows_one = full_one
    for weight in qkv_weights:
        parts = project(rows_one, weight, cosines, sines)
        if not qkv:
            slices = [after(piece, parts[0]) for piece in slices]
            feed_shards = [feed_weights]
            feed_shards += [gather_spread(feed_weights, piece) for piece in slices]
        waits = slices if not qkv else target
        qkv.append((after(parts[0], *waits), *parts[1:]))
        attended.append(attend(place, *qkv[-1]))
        if len(attended) == 1:
            sent = after(output_weight, attended[0][0])
            output_shards = [output_weight] + all_windows(sent)[1:]
        rows_one = pieces_after(full_one, attended[-1][0])

    out_weights = [joined([output_shards[s] for s in group], 0) for group in members]
    mixer_terms = [
        (mixed, None, weight, None, 0) for (mixed, _), weight in zip(attended, out_weights)
    ]
    hidden_one, normed_two = norm(
        tokens,
        scatter(lambda start, rows: sum_products(mixer_terms, start, rows)),
        gain_second,
        shift_second,
    )
    full_two = gather_rows(normed_two)

    flip = [(d, d ^ 1) for d in range(dp_size)]
    odd = lax.axis_index("dp") % 2

    def half(value, which):
        count = value.shape[0] // 2
        return lax.dynamic_slice_in_dim(value, which * count, count, axis=0)

    def total(pieces, which):
        return sum(half(piece, which).astype(F32) for piece in pieces).astype(BF16)

    def swap_half(pieces, *others):
        pieces = [after(piece, *others) for piece in pieces]
        mine, sent = total(pieces, odd), total(pieces, 1 - odd)
        return (mine, lax.ppermute(sent, "dp", flip)), [mine, sent]

    def add_half(halves, *others):
        mine, received = (after(value, *others) for value in halves)
        return (mine.astype(F32) + received.astype(F32)).astype(BF16)

    def sum_half(value, turn):
        groups = [list(range(0, dp_size, 2)), list(range(1, dp_size, 2))]
        if turn & 1:
            groups = groups[::-1]
        if turn & 2:
            groups = [group[::-1] for group in groups]
        return lax.psum(value, "dp", axis_index_groups=groups)

    def swap_sum(mine, *others):
        mine = after(mine, *others)
        return mine, lax.ppermute(mine, "dp", flip)

    def whole_sum(halves, *others):
        mine, received = (after(value, *others) for value in halves)
        first, second = jnp.where(odd == 0, mine, received), jnp.where(odd == 0, received, mine)
        return jnp.concatenate([first, second], axis=0).astype(F32)

    def send_to_owner(parts):
        return [to_window(parts[shift], shift) for shift in range(1, windows)]

    order = list(range(1, windows)) + [0]
    fed = {}
    rows_two = full_two
    for s in order:
        fed[s] = feed(rows_two, target, feed_shards[s])
        rows_two = pieces_after(full_two, fed[s][0])
    down_pieces, up_pieces, gate_pieces = (
        send_to_owner({s: fed[s][k] for s in order}) + [fed[0][k]] for k in (5, 4, 3)
    )
    two_terms, feed_terms = [], []
    for s in order:
        gate, up, down = feed_shards[s]
        two_terms += [(fed[s][1], None, gate, None, 1), (fed[s][2], None, up, None, 1)]
        feed_terms.append((fed[s][0], None, down, None, 0))

    two_sent = [
        sum_products(two_terms, shift * held, held, BF16) for shift in range(1, span)
    ]
    down_half, marks = swap_half(down_pieces, *two_sent)
    two_terms = [(after(two_terms[0][0], *marks), *two_terms[0][1:])] + two_terms[1:]
    two_kept = sum_products(two_terms, 0, held)
    grad_branch_own, grad_hidden, norm_two = norm_back(
        hidden_one,
        cotangent,
        gain_second,
        [two_kept] + [to_seat(part, shift + 1) for shift, part in enumerate(two_sent)],
        False,
    )
    grad_branch = gather_rows(grad_branch_own)
    down_half = add_half(down_half, *grad_branch_own)
    down_sum = sum_half(down_half, 0)
    grad_branch = pieces_after(grad_branch, down_half)

    members = members[::-1]
    out_weights, qkv_weights = out_weights[::-1], qkv_weights[::-1]
    qkv, attended = qkv[::-1], attended[::-1]
    grad_mixed, found = branch_back(grad_branch, out_weights, [mixed for mixed, _ in attended])
    out_grads = {
        s: out_grad[spot * head_cols : (spot + 1) * head_cols]
        for group, out_grad in zip(members, found)
        for spot, s in enumerate(group)
    }
    out_pieces = send_to_owner(out_grads) + [out_grads[0]]

    def up_swap(last):
        sums["up"], waits = swap_half(up_pieces, *last)
        return waits

    def up_sum(last):
        value = add_half(sums["up"], *last)
        sums["up"] = sum_half(value, 1)
        return [value]

    def gate_swap(last):
        sums["gate"], waits = swap_half(gate_pieces, *last)
        sums["out"], more = swap_half(out_pieces, *last)
        sums["down"] = after(down_sum, *waits, *more)
        return waits + more + [sums["down"]]

    def gate_sum(last):
        values = add_half(sums["gate"], *last), add_half(sums["out"], *last)
        sums["gate"], sums["out"] = sum_half(values, 2)
        sums["up"] = swap_sum(sums["up"], *last)
        sums["down"] = swap_sum(sums["down"], *last)
        return [*values, sums["up"][0]]

    along = exchanges("dp", dp_size)
    exchange = exchanges("tensor", tensor_size) + along[1:] + along[:1]
    sums = {}
    moves = [up_swap, up_sum, gate_swap, gate_sum]
    last = list(grad_mixed)
    grad_qkv, qkv_grads = [], {}
    for index, group in enumerate(members):
        mixed, logs = attended[index]
        count = len(group) * head_cols
        grads = None
        for pair in range(count // LANES):
            waits = moves.pop(0)(last) if moves else last
            grads = attend_back(
                place,
                *qkv[index],
                mixed,
                after(grad_mixed[index], *waits),
                logs,
                cosines,
                sines,
                pair,
                grads,
            )
            last = [grads]
        grad_qkv.append(grads)
        qkv_grad = outer(full_one, grads)
        last = [qkv_grad]
        for spot, s in enumerate(group):
            if len(group) == 1:
                qkv_grads[s] = qkv_grad
            else:
                qkv_grads[s] = joined(
                    [
                        lax.slice_in_dim(
                            qkv_grad,
                            part * count + spot * head_cols,
                            part * count + (spot + 1) * head_cols,
                            axis=1,
                        )
                        for part in range(3)
                    ],
                    1,
                )
    for move in moves:
        last = move(last)

    qkv_half, marks = swap_half(send_to_owner(qkv_grads) + [qkv_grads[0]])
    grad_up = whole_sum(sums["up"], *marks)
    feed_terms[0] = (after(feed_terms[0][0], grad_up), *feed_terms[0][1:])
    one_terms = [
        (grad_qkv[index], part, weight, part, 1)
        for index, weight in enumerate(qkv_weights)
        for part in range(3)
    ]

    def later(terms, *others):
        return [(after(terms[0][0], *others), *terms[0][1:])] + terms[1:]

    shifts = range(1, span)
    feed_sent = [sum_products(feed_terms, shift * held, held, BF16) for shift in shifts]
    qkv_half = add_half(qkv_half, *feed_sent)
    gate_halves = swap_sum(sums["gate"], *feed_sent)
    out_halves = swap_sum(sums["out"], *feed_sent)
    qkv_sum = sum_half(after(qkv_half, gate_halves[0], out_halves[0]), 3)
    grad_down = whole_sum(sums["down"], *feed_sent)
    one_terms = later(one_terms, qkv_half, gate_halves[0], grad_down)
    one_sent = [sum_products(one_terms, shift * held, held, BF16) for shift in shifts]
    feed_parts = [sum_products(later(feed_terms, *one_sent), 0, held)]
    one_parts = [sum_products(later(one_terms, feed_parts[0]), 0, held)]
    feed_parts += [to_seat(part, shift) for shift, part in zip(shifts, feed_sent)]
    one_parts += [to_seat(part, shift) for shift, part in zip(shifts, one_sent)]
    output = (hidden_one + sum(feed_parts)).astype(BF16)
    (input_grad,), _, norm_one = norm_back(tokens, grad_hidden, gain_first, one_parts, True, 1)
    window = [input_grad, output]
    qkv_halves = swap_sum(qkv_sum, *window)
    norms = jnp.concatenate([after(norm_one, qkv_halves[0]), norm_two], axis=0)
    for step in exchange:
        norms = step(norms)
    grad_gate = whole_sum(gate_halves, qkv_halves[0])
    out_grad = whole_sum(out_halves, qkv_halves[0])
    qkv_grad = whole_sum(qkv_halves)
    return (
        output,
        input_grad,
        *(part_of(qkv_grad, part) for part in range(3)),
        out_grad,
        grad_gate,
        grad_up,
        grad_down,
        norms[0],
        norms[1],
        norms[2],
        norms[3],
    )


def solution(mesh):
    rows = P(("dp", "tensor"), None)
    columns = P(None, "tensor")
    depth = P("tensor", None)
    return jax.shard_map(
        functools.partial(shards, mesh.shape["dp"], mesh.shape["tensor"]),
        mesh=mesh,
        in_specs=(
            rows,
            P("dp"),
            P(),
            P(),
            columns,
            columns,
            columns,
            depth,
            P(),
            P(),
            columns,
            columns,
            depth,
            rows,
        ),
        out_specs=(
            rows,
            rows,
            columns,
            columns,
            columns,
            depth,
            columns,
            columns,
            depth,
            P(),
            P(),
            P(),
            P(),
        ),
        check_vma=False,
    )
```

```python
import functools
import math

import jax
import jax.numpy as jnp
from jax import lax
from jax.experimental import pallas as pl
from jax.experimental.pallas import tpu as pltpu
from jax.sharding import PartitionSpec as P

HD = 64
LEN = 2048
EPSILON = 1e-05
MASKED = -1e30
LANES = 128
LOG2E = math.log2(math.e)
BF16 = jnp.bfloat16
F32 = jnp.float32
MIB = 1 << 20
COST_SHARE = 0.1
PIECES = 2


def contract(left, right, left_dim, right_dim):
    return lax.dot_general(
        left, right, (((left_dim,), (right_dim,)), ((), ())), preferred_element_type=F32
    )


def cost(flops, moved, transcendentals=0):
    return pl.CostEstimate(
        flops=int(flops * COST_SHARE),
        bytes_accessed=int(moved * COST_SHARE),
        transcendentals=int(transcendentals * COST_SHARE),
    )


def swap_halves(value):
    columns = value.shape[1]
    lane = lax.broadcasted_iota(jnp.int32, value.shape, 1)
    return jnp.where(
        lane % HD < HD // 2,
        pltpu.roll(value, columns - HD // 2, 1),
        pltpu.roll(value, HD // 2, 1),
    )


def fetch(pieces, rows, sems):
    copies, start = [], 0
    for index, piece in enumerate(pieces):
        count = piece.shape[0]
        copies.append(
            pltpu.make_async_copy(piece, rows.at[pl.ds(start, count), :], sems.at[index])
        )
        start += count
    for copy in copies:
        copy.start()
    return copies


def room(pieces):
    count = sum(piece.shape[0] for piece in pieces)
    return [
        pltpu.VMEM((count, pieces[0].shape[1]), BF16),
        pltpu.SemaphoreType.DMA((len(pieces),)),
    ]


def unpacked(ref):
    value = ref[...]
    return value.reshape(-1, value.shape[-1]) if value.ndim == 3 else value


def packed(weight):
    return isinstance(weight, tuple)


def project_kernel(*refs, count):
    pieces = refs[:count]
    weight_ref, cos_ref, sin_ref, q_ref, k_ref, v_ref, rows, sems = refs[count:]
    columns = q_ref.shape[1]
    block = q_ref.shape[0]

    @pl.when(pl.program_id(0) == 0)
    def _():
        for copy in fetch(pieces, rows, sems):
            copy.wait()

    start = pl.multiple_of(pl.program_id(0) * block, block)
    product = contract(rows[pl.ds(start, block), :], weight_ref[...], 1, 0)
    cosines = jnp.concatenate([cos_ref[...]] * (columns // LANES), axis=1)
    sines = jnp.concatenate([sin_ref[...]] * (columns // LANES), axis=1)
    for part, out_ref in ((0, q_ref), (1, k_ref)):
        value = product[:, part * columns : (part + 1) * columns]
        out_ref[...] = (value * cosines + swap_halves(value) * sines).astype(BF16)
    v_ref[...] = product[:, 2 * columns :].astype(BF16)


def project(pieces, weight, cosines, sines, block=512):
    width = weight.shape[0]
    columns = weight.shape[1] // 3
    count = sum(piece.shape[0] for piece in pieces)
    table = pl.BlockSpec((block, LANES), lambda i: (i, 0))
    out = pl.BlockSpec((block, columns), lambda i: (i, 0))
    return pl.pallas_call(
        functools.partial(project_kernel, count=len(pieces)),
        grid=(count // block,),
        in_specs=[pl.BlockSpec(memory_space=pl.ANY)] * len(pieces)
        + [pl.BlockSpec(weight.shape, lambda i: (0, 0)), table, table],
        out_specs=[out, out, out],
        out_shape=[jax.ShapeDtypeStruct((count, columns), BF16)] * 3,
        scratch_shapes=room(pieces),
        cost_estimate=cost(
            2 * count * width * 3 * columns,
            2 * (count * width + width * 3 * columns + count * 3 * columns),
        ),
        compiler_params=pltpu.CompilerParams(vmem_limit_bytes=40 * MIB),
        name="project_rope",
    )(*pieces, weight, cosines, sines)


def masked_keys(place_ref, key_ref, masked_ref):
    count = key_ref.shape[0]
    lane = lax.broadcasted_iota(jnp.int32, (count, LANES), 1)
    row = lax.broadcasted_iota(jnp.int32, (count, LANES), 0) + place_ref[1]
    position = jnp.where(row >= count, row - count, row)
    bias = jnp.where(position >= place_ref[0], MASKED, 0.0).astype(BF16)
    nothing = jnp.zeros_like(bias)
    key = key_ref[...]
    masked_ref[0] = jnp.where(lane < HD, key, jnp.where(lane == HD, bias, nothing))
    masked_ref[1] = jnp.where(lane >= HD, key, jnp.where(lane == 0, bias, nothing))


def masked_queries(query):
    lane = lax.broadcasted_iota(jnp.int32, query.shape, 1)
    scaled = query * jnp.asarray(1.0 / math.sqrt(HD), BF16)
    one = jnp.ones_like(query)
    nothing = jnp.zeros_like(query)
    return (
        scaled,
        jnp.where(lane < HD, scaled, jnp.where(lane == HD, one, nothing)),
        jnp.where(lane >= HD, scaled, jnp.where(lane == 0, one, nothing)),
    )


def attend_kernel(place_ref, q_ref, k_ref, v_ref, out_ref, log_ref, keys, values_t, *, chunk):
    count = k_ref.shape[0]

    @pl.when(pl.program_id(1) == 0)
    def _():
        masked_keys(place_ref, k_ref, keys)
        values_t[...] = v_ref[...].T

    queries = masked_queries(q_ref[...])[1:]
    mixed, logs = [], []
    for head in range(2):
        scores = [
            contract(keys[head, start : start + chunk, :], queries[head], 1, 1)
            for start in range(0, count, chunk)
        ]
        top = functools.reduce(
            jnp.maximum, [jnp.max(block, axis=0, keepdims=True) for block in scores]
        )
        total = 0.0
        summed = 0.0
        for index, block in enumerate(scores):
            weights = jnp.exp2((block - top) * LOG2E)
            total = total + jnp.sum(weights, axis=0, keepdims=True)
            value = values_t[
                head * HD : (head + 1) * HD, index * chunk : (index + 1) * chunk
            ]
            summed = summed + contract(value, weights.astype(BF16), 1, 0)
        mixed.append(summed / total)
        logs.append(top * LOG2E + jnp.log2(total))
    out_ref[...] = jnp.concatenate(mixed, axis=0).T.astype(BF16)
    log_ref[0] = jnp.concatenate(logs + [jnp.zeros((6, q_ref.shape[0]), F32)], axis=0)


def attend(place, queries, keys, values, block=1024, chunk=2048):
    count, columns = queries.shape
    pairs = columns // LANES
    whole = pl.BlockSpec((count, LANES), lambda p, i, _: (0, p))
    rows = pl.BlockSpec((block, LANES), lambda p, i, _: (i, p))
    return pl.pallas_call(
        functools.partial(attend_kernel, chunk=chunk),
        grid_spec=pltpu.PrefetchScalarGridSpec(
            num_scalar_prefetch=1,
            grid=(pairs, count // block),
            in_specs=[rows, whole, whole],
            out_specs=[rows, pl.BlockSpec((1, 8, block), lambda p, i, _: (p, 0, i))],
            scratch_shapes=[
                pltpu.VMEM((2, count, LANES), BF16),
                pltpu.VMEM((LANES, count), BF16),
            ],
        ),
        out_shape=[
            jax.ShapeDtypeStruct((count, columns), BF16),
            jax.ShapeDtypeStruct((pairs, 8, count), F32),
        ],
        cost_estimate=cost(16 * count * count * columns, 8 * count * columns, count * count * columns // HD),
        compiler_params=pltpu.CompilerParams(vmem_limit_bytes=56 * MIB),
        name="attention_forward",
    )(place, queries, keys, values)


def attend_back_kernel(
    place_ref,
    q_ref,
    k_ref,
    v_ref,
    out_ref,
    up_ref,
    log_ref,
    cos_row_ref,
    sin_row_ref,
    cos_ref,
    sin_ref,
    *rest,
    chunk,
):
    grad_ref, keys, grad_keys_t, grad_values_t = rest[-4:]
    count = k_ref.shape[0]
    step = pl.program_id(1)

    @pl.when(step == 0)
    def _():
        masked_keys(place_ref, k_ref, keys)
        grad_keys_t[...] = jnp.zeros_like(grad_keys_t)
        grad_values_t[...] = jnp.zeros_like(grad_values_t)

    scaled, *queries = masked_queries(q_ref[...])
    upstream = up_ref[...]
    lane = lax.broadcasted_iota(jnp.int32, upstream.shape, 1)
    nothing = jnp.zeros_like(upstream)
    products = upstream.astype(F32) * out_ref[...].astype(F32)
    scaled_t = scaled.T
    upstream_t = upstream.T
    logs = log_ref[0].T
    grad_queries = []
    for head in range(2):
        mine = (lane < HD) == (head == 0)
        own_upstream = jnp.where(mine, upstream, nothing)
        row_dot = jnp.sum(jnp.where(mine, products, 0.0), axis=1, keepdims=True)
        log_total = logs[:, head : head + 1]
        heads = slice(head * HD, (head + 1) * HD)
        grad_query = 0.0
        for start in range(0, count, chunk):
            span = slice(start, start + chunk)
            scores = contract(queries[head], keys[head, span, :], 1, 1)
            probs = jnp.exp2(scores * LOG2E - log_total)
            grad_probs = contract(own_upstream, v_ref[span, :], 1, 1)
            grad_scores = (probs * (grad_probs - row_dot)).astype(BF16)
            grad_values_t[heads, span] += contract(
                upstream_t[heads, :], probs.astype(BF16), 1, 0
            )
            grad_keys_t[heads, span] += contract(scaled_t[heads, :], grad_scores, 1, 0)
            grad_query = grad_query + contract(grad_scores, k_ref[span, :], 1, 0)
        grad_queries.append(grad_query)
    grad_query = jnp.where(lane < HD, *grad_queries) * (1.0 / math.sqrt(HD))
    block = grad_query.shape[0]
    grad_ref[0, pl.ds(pl.multiple_of(step * block, block), block), :] = (
        grad_query * cos_row_ref[...] - swap_halves(grad_query) * sin_row_ref[...]
    ).astype(BF16)

    @pl.when(step == pl.num_programs(1) - 1)
    def _():
        grad_key = grad_keys_t[...].T
        grad_ref[1] = (
            grad_key * cos_ref[...] - swap_halves(grad_key) * sin_ref[...]
        ).astype(BF16)
        grad_ref[2] = grad_values_t[...].T.astype(BF16)


def attend_back(
    place, queries, keys, values, mixed, upstream, logs, cosines, sines, pair, grads, block=1024, chunk=512
):
    count, columns = queries.shape
    whole = pl.BlockSpec((count, LANES), lambda p, i, _: (0, pair))
    rows = pl.BlockSpec((block, LANES), lambda p, i, _: (i, pair))
    table = pl.BlockSpec((count, LANES), lambda p, i, _: (0, 0))
    table_rows = pl.BlockSpec((block, LANES), lambda p, i, _: (i, 0))
    held = [] if grads is None else [grads]
    return pl.pallas_call(
        functools.partial(attend_back_kernel, chunk=chunk),
        grid_spec=pltpu.PrefetchScalarGridSpec(
            num_scalar_prefetch=1,
            grid=(1, count // block),
            in_specs=[
                rows,
                whole,
                whole,
                rows,
                rows,
                pl.BlockSpec((1, 8, block), lambda p, i, _: (pair, 0, i)),
                table_rows,
                table_rows,
                table,
                table,
            ]
            + [pl.BlockSpec(memory_space=pl.ANY)] * len(held),
            out_specs=pl.BlockSpec((3, count, LANES), lambda p, i, _: (0, 0, pair)),
            scratch_shapes=[
                pltpu.VMEM((2, count, LANES), BF16),
                pltpu.VMEM((LANES, count), F32),
                pltpu.VMEM((LANES, count), F32),
            ],
        ),
        out_shape=jax.ShapeDtypeStruct((3, count, columns), BF16),
        input_output_aliases={11: 0} if held else {},
        cost_estimate=cost(28 * count * count * LANES, 16 * count * LANES, count * count * 2),
        compiler_params=pltpu.CompilerParams(vmem_limit_bytes=60 * MIB),
        name="attention_backward",
    )(place, queries, keys, values, mixed, upstream, logs, cosines, sines, cosines, sines, *held)


def feed_kernel(*refs, counts, chunk):
    row_pieces, target_pieces = refs[: counts[0]], refs[counts[0] : sum(counts)]
    refs = refs[sum(counts) :]
    gate_ref, up_ref, down_ref, inner_ref, grad_gate_ref, grad_up_ref = refs[:6]
    weight_gate_ref, weight_up_ref, weight_down_ref = refs[6:9]
    rows, row_sems, target, target_sems, rows_t, target_t = refs[9:]

    @pl.when(pl.program_id(0) == 0)
    def _():
        copies = fetch(row_pieces, rows, row_sems) + fetch(target_pieces, target, target_sems)
        for copy in copies:
            copy.wait()
        rows_t[...] = rows[...].T
        target_t[...] = target[...].T

    gate_weight, up_weight, down_weight = unpacked(gate_ref), unpacked(up_ref), unpacked(down_ref)
    for start in range(0, rows.shape[0], chunk):
        span = slice(start, start + chunk)
        gate = contract(rows[span, :], gate_weight, 1, 0)
        up = contract(rows[span, :], up_weight, 1, 0)
        grad_inner = contract(target[span, :], down_weight, 1, 1)
        share = jax.nn.sigmoid(gate)
        activated = gate * share
        inner_ref[span, :] = (activated * up).astype(BF16)
        grad_up_ref[span, :] = (grad_inner * activated).astype(BF16)
        grad_gate_ref[span, :] = (
            grad_inner * up * share * (1.0 + gate * (1.0 - share))
        ).astype(BF16)
    weight_gate_ref[...] = contract(rows_t[...], grad_gate_ref[...], 1, 0).astype(BF16)
    weight_up_ref[...] = contract(rows_t[...], grad_up_ref[...], 1, 0).astype(BF16)
    weight_down_ref[...] = contract(target_t[...], inner_ref[...], 1, 0).T.astype(BF16)


def feed(rows, target, weights, block=256, chunk=512):
    count = sum(piece.shape[0] for piece in rows)
    width = rows[0].shape[1]
    across_spec = lambda units: pl.BlockSpec((width, min(block, units)), lambda i: (0, i))
    down_spec = lambda units: pl.BlockSpec((min(block, units), width), lambda i: (i, 0))
    if packed(weights[0]):
        units = width
        replicas, deep = weights[0][0].shape[0], width // weights[0][0].shape[0]
        specs = [
            pl.BlockSpec((replicas, deep, block), lambda i, plane=weights[k][1]: (0, plane, i))
            for k in range(2)
        ] + [
            pl.BlockSpec(
                (block // deep, deep, width), lambda i, plane=weights[2][1]: (i, plane, 0)
            )
        ]
        weights = [weight for weight, _ in weights]
    else:
        units = weights[0].shape[1]
        specs = [across_spec(units)] * 2 + [down_spec(units)]
    block = min(block, units)
    out = pl.BlockSpec((count, block), lambda i: (0, i))
    return pl.pallas_call(
        functools.partial(feed_kernel, counts=(len(rows), len(target)), chunk=chunk),
        grid=(units // block,),
        in_specs=[pl.BlockSpec(memory_space=pl.ANY)] * (len(rows) + len(target)) + specs,
        out_specs=[out, out, out] + [across_spec(units)] * 2 + [down_spec(units)],
        out_shape=[jax.ShapeDtypeStruct((count, units), BF16)] * 3
        + [jax.ShapeDtypeStruct((width, units), BF16)] * 2
        + [jax.ShapeDtypeStruct((units, width), BF16)],
        scratch_shapes=room(rows) + room(target) + [pltpu.VMEM((width, count), BF16)] * 2,
        cost_estimate=cost(
            12 * count * width * units,
            4 * count * width + 12 * width * units + 6 * count * units,
            2 * count * units,
        ),
        compiler_params=pltpu.CompilerParams(vmem_limit_bytes=60 * MIB),
        name="feed_forward",
    )(*rows, *target, *weights)


def sum_kernel(*refs, places, dims, start, chunk):
    terms = len(dims)
    operands, out_ref = refs[: 2 * terms], refs[2 * terms]
    buffers = refs[2 * terms + 1 : 4 * terms + 1]
    total, result, sems, out_sems = refs[4 * terms + 1 :]
    rows = total.shape[0]
    copies = []
    for index, (ref, place) in enumerate(zip(operands, places)):
        copy = pltpu.make_async_copy(ref.at[place], buffers[index], sems.at[index])
        copy.start()
        copies.append(copy)
    sent = []
    for index, dim in enumerate(dims):
        copies[2 * index].wait()
        copies[2 * index + 1].wait()
        right = unpacked(buffers[2 * index + 1])
        for first in range(0, rows, chunk):
            span = slice(first, first + chunk)
            product = contract(buffers[2 * index][span, :], right, 1, dim)
            if index:
                product = total[span, :] + product
            if index + 1 < terms:
                total[span, :] = product
                continue
            result[span, :] = product.astype(result.dtype)
            copy = pltpu.make_async_copy(
                result.at[pl.ds(first, chunk), :],
                out_ref.at[pl.ds(first, chunk), :],
                out_sems.at[first // chunk],
            )
            copy.start()
            sent.append(copy)
    for copy in sent:
        copy.wait()


def sum_products(terms, start, rows, dtype=F32, chunk=256):
    chunk = min(chunk, rows)
    operands, places, shapes, dims, flops, moved = [], [], [], [], 0, 0
    for left, plane, right, part, dim in terms:
        depth = left.shape[-1]
        span = pl.ds(start, rows)
        places.append((span, slice(None)) if plane is None else (plane, span, slice(None)))
        shapes.append((rows, depth))
        if packed(right):
            right, plane = right
            width = right.shape[2]
            deep = width // right.shape[0]
            places.append((slice(None), pl.ds(plane * deep, deep), slice(None)))
            shapes.append((right.shape[0], deep, width))
        else:
            column = pl.ds(0, right.shape[1]) if part is None else pl.ds(part * depth, depth)
            places.append((slice(None), column))
            shapes.append((right.shape[0], column.size))
            width = shapes[-1][1 - dim]
        operands += [left, right]
        dims.append(dim)
        flops += 2 * rows * depth * width
        moved += 2 * rows * depth + 2 * depth * width
    anywhere = pl.BlockSpec(memory_space=pl.ANY)
    return pl.pallas_call(
        functools.partial(
            sum_kernel, places=places, dims=tuple(dims), start=start, chunk=chunk
        ),
        in_specs=[anywhere] * len(operands),
        out_specs=anywhere,
        out_shape=jax.ShapeDtypeStruct((rows, width), dtype),
        scratch_shapes=[pltpu.VMEM(shape, BF16) for shape in shapes]
        + [
            pltpu.VMEM((rows, width), F32),
            pltpu.VMEM((rows, width), dtype),
            pltpu.SemaphoreType.DMA((len(operands),)),
            pltpu.SemaphoreType.DMA((rows // chunk,)),
        ],
        cost_estimate=cost(flops, moved + 4 * rows * width),
        compiler_params=pltpu.CompilerParams(vmem_limit_bytes=58 * MIB),
        name="sum_products",
    )(*operands)


def outer_kernel(*refs, count):
    right_ref, out_ref, left, sems, left_t = refs[count:]

    @pl.when(pl.program_id(0) == 0)
    def _():
        for copy in fetch(refs[:count], left, sems):
            copy.wait()
        left_t[...] = left[...].T

    out_ref[...] = contract(left_t[...], right_ref[...], 1, 0).astype(BF16)


def outer(pieces, right):
    width = pieces[0].shape[1]
    planes, count, columns = right.shape
    return pl.pallas_call(
        functools.partial(outer_kernel, count=len(pieces)),
        grid=(planes,),
        in_specs=[pl.BlockSpec(memory_space=pl.ANY)] * len(pieces)
        + [pl.BlockSpec((None, count, columns), lambda i: (i, 0, 0))],
        out_specs=pl.BlockSpec((width, columns), lambda i: (0, i)),
        out_shape=jax.ShapeDtypeStruct((width, planes * columns), BF16),
        scratch_shapes=room(pieces) + [pltpu.VMEM((width, count), BF16)],
        cost_estimate=cost(
            2 * count * width * planes * columns,
            2 * count * (width + planes * columns) + 2 * width * planes * columns,
        ),
        compiler_params=pltpu.CompilerParams(vmem_limit_bytes=40 * MIB),
        name="outer_product",
    )(*pieces, right)


def branch_kernel(*refs, count, groups, chunk):
    weights = refs[count : count + groups]
    mixed = refs[count + groups : count + 2 * groups]
    outs = refs[count + 2 * groups : count + 4 * groups]
    rows, sems = refs[count + 4 * groups :]
    for copy in fetch(refs[:count], rows, sems):
        copy.wait()
    for index in range(groups):
        outs[groups + index][...] = contract(mixed[index][...].T, rows[...], 1, 0).astype(BF16)
        for start in range(0, rows.shape[0], chunk):
            span = slice(start, start + chunk)
            outs[index][span, :] = contract(rows[span, :], weights[index][...], 1, 1).astype(BF16)


def branch_back(pieces, weights, mixed, chunk=512):
    count = sum(piece.shape[0] for piece in pieces)
    width = pieces[0].shape[1]
    groups = len(weights)
    vmem = pl.BlockSpec(memory_space=pltpu.VMEM)
    columns = [weight.shape[0] for weight in weights]
    results = pl.pallas_call(
        functools.partial(branch_kernel, count=len(pieces), groups=groups, chunk=chunk),
        in_specs=[pl.BlockSpec(memory_space=pl.ANY)] * len(pieces) + [vmem] * (2 * groups),
        out_specs=[vmem] * (2 * groups),
        out_shape=[jax.ShapeDtypeStruct((count, size), BF16) for size in columns]
        + [jax.ShapeDtypeStruct((size, width), BF16) for size in columns],
        scratch_shapes=room(pieces),
        cost_estimate=cost(4 * count * width * sum(columns), 6 * count * width),
        compiler_params=pltpu.CompilerParams(vmem_limit_bytes=48 * MIB),
        name="branch_backward",
    )(*pieces, *weights, *mixed)
    return results[:groups], results[groups:]


def standardize(value):
    centred = value - jnp.mean(value, axis=-1, keepdims=True)
    scale = lax.rsqrt(jnp.mean(centred * centred, axis=-1, keepdims=True) + EPSILON)
    return centred * scale, scale


def norm_kernel(*refs, added):
    value = refs[0][...].astype(F32)
    for ref in refs[1 : 1 + added]:
        value = value + ref[...].astype(F32)
    gain_ref, shift_ref = refs[1 + added : 3 + added]
    standard, _ = standardize(value)
    if added:
        refs[-2][...] = value
    refs[-1][...] = (standard * gain_ref[...] + shift_ref[...]).astype(BF16)


def norm(base, terms, gain, shift, pieces=PIECES, block=256):
    count, width = base.shape
    rows = count // pieces
    block = min(block, rows)
    vector = pl.BlockSpec((1, width), lambda i: (0, 0))
    total, out = None, []
    for piece in range(pieces):
        first = piece * rows // block
        whole = pl.BlockSpec((block, width), lambda i, first=first: (first + i, 0))
        shapes = [jax.ShapeDtypeStruct((rows, width), BF16)]
        specs = [pl.BlockSpec((block, width), lambda i: (i, 0))]
        held = []
        if terms:
            shapes = [jax.ShapeDtypeStruct((count, width), F32)] + shapes
            specs = [whole] + specs
            held = [] if total is None else [total]
        results = pl.pallas_call(
            lambda *refs, held=len(held): norm_kernel(
                *refs[: 3 + len(terms)], *refs[3 + len(terms) + held :], added=len(terms)
            ),
            grid=(rows // block,),
            in_specs=[whole] * (1 + len(terms))
            + [vector, vector]
            + [pl.BlockSpec(memory_space=pl.ANY)] * len(held),
            out_specs=specs,
            out_shape=shapes,
            input_output_aliases={3 + len(terms): 0} if held else {},
            cost_estimate=cost(16 * rows * width, 8 * rows * width * len(shapes)),
            name="layer_norm",
        )(base, *terms, gain.reshape(1, width), shift.reshape(1, width), *held)
        out.append(results[-1])
        if terms:
            total = results[0]
    return total, out


def norm_back_kernel(*refs, added, low):
    base_ref, straight_ref, gain_ref = refs[:3]
    upstream = refs[3][...].astype(F32)
    for ref in refs[4 : 3 + added]:
        upstream = upstream + ref[...].astype(F32)
    outs = refs[3 + added :]
    standard, scale = standardize(base_ref[...].astype(F32))
    scaled = upstream * gain_ref[...]
    back = straight_ref[...].astype(F32) + scale * (
        scaled
        - jnp.mean(scaled, axis=-1, keepdims=True)
        - standard * jnp.mean(scaled * standard, axis=-1, keepdims=True)
    )
    outs[0][...] = back.astype(BF16)
    if not low:
        outs[1][...] = back
    sums = jnp.concatenate(
        [
            jnp.sum(upstream * standard, axis=0, keepdims=True),
            jnp.sum(upstream, axis=0, keepdims=True),
        ],
        axis=0,
    )

    @pl.when(pl.program_id(0) == 0)
    def _():
        outs[-1][...] = sums

    @pl.when(pl.program_id(0) > 0)
    def _():
        outs[-1][...] += sums


def norm_back(base, straight, gain, terms, low, pieces=PIECES, block=256):
    count, width = base.shape
    rows = count // pieces
    block = min(block, rows)
    total, out, found = None, [], []
    for piece in range(pieces):
        first = piece * rows // block
        whole = pl.BlockSpec((block, width), lambda i, first=first: (first + i, 0))
        shapes = [jax.ShapeDtypeStruct((rows, width), BF16)]
        specs = [pl.BlockSpec((block, width), lambda i: (i, 0))]
        held = []
        if not low:
            shapes.append(jax.ShapeDtypeStruct((count, width), F32))
            specs.append(whole)
            held = [] if total is None else [total]
        results = pl.pallas_call(
            lambda *refs, held=len(held): norm_back_kernel(
                *refs[: 3 + len(terms)],
                *refs[3 + len(terms) + held :],
                added=len(terms),
                low=low,
            ),
            grid=(rows // block,),
            in_specs=[whole, whole, pl.BlockSpec((1, width), lambda i: (0, 0))]
            + [whole] * len(terms)
            + [pl.BlockSpec(memory_space=pl.ANY)] * len(held),
            out_specs=specs + [pl.BlockSpec((2, width), lambda i: (0, 0))],
            out_shape=shapes + [jax.ShapeDtypeStruct((2, width), F32)],
            input_output_aliases={3 + len(terms): 1} if held else {},
            cost_estimate=cost(30 * rows * width, 16 * rows * width),
            name="layer_norm_backward",
        )(base, straight, gain.reshape(1, width), *terms, *held)
        out.append(results[0])
        found.append(results[-1])
        if not low:
            total = results[1]
    return out, total, sum(found)


def rope_tables(offset):
    half = HD // 2
    groups = LANES // half
    count = LEN // groups
    lane = jnp.arange(LANES, dtype=jnp.int32)
    position = jnp.arange(count, dtype=jnp.int32)[:, None] + lane[None, :] // half * count
    position = (position + offset) % LEN
    inverse = 10000.0 ** (-2.0 * (lane % half).astype(F32) / HD)
    angles = position.astype(F32) * inverse[None, :]
    cosines, sines = lax.optimization_barrier((jnp.cos(angles), jnp.sin(angles)))

    def rows(table, signs):
        parts = [table[:, g * half : (g + 1) * half] for g in range(groups)]
        return jnp.concatenate(
            [jnp.concatenate([sign * part for sign in signs], axis=1) for part in parts], axis=0
        )

    return rows(cosines, (1, 1, 1, 1)), rows(sines, (-1, 1, -1, 1))


def exchanges(axis, size):
    if size & (size - 1):
        return [lambda value: lax.psum(value, axis)]
    return [
        lambda value, pairs=[(i, i ^ (1 << bit)) for i in range(size)]: value
        + lax.ppermute(value, axis, pairs)
        for bit in range(size.bit_length() - 1)
    ]


def shards(
    dp_size,
    tensor_size,
    tokens,
    lengths,
    gain_first,
    shift_first,
    query_weight,
    key_weight,
    value_weight,
    output_weight,
    gain_second,
    shift_second,
    gate_weight,
    up_weight,
    down_weight,
    cotangent,
):
    windows = lengths.shape[0]
    span = tensor_size // windows
    held = tokens.shape[0]
    width = tokens.shape[1]
    head_cols = query_weight.shape[1]
    here = lax.axis_index("tensor")
    window, seat = here // span, here % span

    def from_seat(value, shift):
        pairs = [
            (w * span + (s + shift) % span, w * span + s)
            for w in range(windows)
            for s in range(span)
        ]
        return lax.ppermute(value, "tensor", pairs)

    def to_seat(value, shift):
        return from_seat(value, span - shift)

    def from_window(value, shift):
        pairs = [((t + shift * span) % tensor_size, t) for t in range(tensor_size)]
        return lax.ppermute(value, "tensor", pairs)

    def to_window(value, shift):
        return from_window(value, windows - shift)

    def gather_rows(value):
        return value + [from_seat(piece, s) for s in range(1, span) for piece in value]

    def scatter(partial):
        sent = [to_seat(partial(s * held, held), s) for s in range(1, span)]
        return [partial(0, held)] + sent

    def all_windows(value):
        return [value] + [from_window(value, shift) for shift in range(1, windows)]

    def spread_windows(values):
        group = lax.axis_index("dp")
        sizes = [value.shape[0] // dp_size for value in values]
        mine = jnp.concatenate(
            [
                lax.dynamic_slice_in_dim(value, group * size, size, axis=0).reshape(-1, width)
                for value, size in zip(values, sizes)
            ],
            axis=0,
        )
        return [mine], [from_window(mine, shift) for shift in range(1, windows)]

    def gather_spread(values, piece):
        gathered = lax.all_gather(piece, "dp", axis=0)
        if all(value.shape == (width, width) for value in values):
            return [(gathered, plane) for plane in range(len(values))]
        out, start = [], 0
        for value in values:
            count = value.size // width // dp_size
            out.append(gathered[:, start : start + count].reshape(value.shape))
            start += count
        return out

    def after(value, *others):
        return lax.optimization_barrier((value, *others))[0]

    def pieces_after(pieces, *others):
        return [after(pieces[0], *others)] + pieces[1:]

    place = jnp.stack(
        [lax.dynamic_index_in_dim(lengths, window, keepdims=False), seat * held]
    ).astype(jnp.int32)
    cosines, sines = rope_tables(seat * held)

    members = [[s] for s in range(windows)] if head_cols % LANES == 0 else [list(range(windows))]
    feed_weights = [gate_weight, up_weight, down_weight]
    slices_sent, slices = spread_windows(feed_weights)
    _, normed_one = norm(after(tokens, *slices_sent), [], gain_first, shift_first)
    full_one = gather_rows(normed_one)
    qkv_own = jnp.concatenate([query_weight, key_weight, value_weight], axis=1)
    qkv_other = all_windows(after(qkv_own, *slices))[1:]
    qkv_shards = [qkv_own] + qkv_other
    def joined(parts, axis):
        return parts[0] if len(parts) == 1 else jnp.concatenate(parts, axis=axis)

    def part_of(value, part):
        return value[:, part * head_cols : (part + 1) * head_cols]

    qkv_weights = [
        qkv_shards[group[0]]
        if len(group) == 1
        else joined([part_of(qkv_shards[s], part) for part in range(3) for s in group], 1)
        for group in members
    ]
    target = gather_rows([cotangent])
    qkv, attended = [], []
    rows_one = full_one
    for weight in qkv_weights:
        parts = project(rows_one, weight, cosines, sines)
        if not qkv:
            slices = [after(piece, parts[0]) for piece in slices]
            feed_shards = [feed_weights]
            feed_shards += [gather_spread(feed_weights, piece) for piece in slices]
        waits = slices if not qkv else target
        qkv.append((after(parts[0], *waits), *parts[1:]))
        attended.append(attend(place, *qkv[-1]))
        if len(attended) == 1:
            sent = after(output_weight, attended[0][0])
            output_shards = [output_weight] + all_windows(sent)[1:]
        rows_one = pieces_after(full_one, attended[-1][0])

    out_weights = [joined([output_shards[s] for s in group], 0) for group in members]
    mixer_terms = [
        (mixed, None, weight, None, 0) for (mixed, _), weight in zip(attended, out_weights)
    ]
    hidden_one, normed_two = norm(
        tokens,
        scatter(lambda start, rows: sum_products(mixer_terms, start, rows)),
        gain_second,
        shift_second,
    )
    full_two = gather_rows(normed_two)

    flip = [(d, d ^ 1) for d in range(dp_size)]
    odd = lax.axis_index("dp") % 2

    def half(value, which):
        count = value.shape[0] // 2
        return lax.dynamic_slice_in_dim(value, which * count, count, axis=0)

    def total(pieces, which):
        return sum(half(piece, which).astype(F32) for piece in pieces).astype(BF16)

    def swap_half(pieces, *others):
        pieces = [after(piece, *others) for piece in pieces]
        mine, sent = total(pieces, odd), total(pieces, 1 - odd)
        return (mine, lax.ppermute(sent, "dp", flip)), [mine, sent]

    def add_half(halves, *others):
        mine, received = (after(value, *others) for value in halves)
        return (mine.astype(F32) + received.astype(F32)).astype(BF16)

    def sum_half(value, turn):
        groups = [list(range(0, dp_size, 2)), list(range(1, dp_size, 2))]
        if turn & 1:
            groups = groups[::-1]
        if turn & 2:
            groups = [group[::-1] for group in groups]
        return lax.psum(value, "dp", axis_index_groups=groups)

    def swap_sum(mine, *others):
        mine = after(mine, *others)
        return mine, lax.ppermute(mine, "dp", flip)

    def whole_sum(halves, *others):
        mine, received = (after(value, *others) for value in halves)
        first, second = jnp.where(odd == 0, mine, received), jnp.where(odd == 0, received, mine)
        return jnp.concatenate([first, second], axis=0).astype(F32)

    def send_to_owner(parts):
        return [to_window(parts[shift], shift) for shift in range(1, windows)]

    order = list(range(1, windows)) + [0]
    fed = {}
    rows_two = full_two
    for s in order:
        fed[s] = feed(rows_two, target, feed_shards[s])
        rows_two = pieces_after(full_two, fed[s][0])
    down_pieces, up_pieces, gate_pieces = (
        send_to_owner({s: fed[s][k] for s in order}) + [fed[0][k]] for k in (5, 4, 3)
    )
    two_terms, feed_terms = [], []
    for s in order:
        gate, up, down = feed_shards[s]
        two_terms += [(fed[s][1], None, gate, None, 1), (fed[s][2], None, up, None, 1)]
        feed_terms.append((fed[s][0], None, down, None, 0))

    two_sent = [
        sum_products(two_terms, shift * held, held, BF16) for shift in range(1, span)
    ]
    down_half, marks = swap_half(down_pieces, *two_sent)
    two_terms = [(after(two_terms[0][0], *marks), *two_terms[0][1:])] + two_terms[1:]
    two_kept = sum_products(two_terms, 0, held)
    grad_branch_own, grad_hidden, norm_two = norm_back(
        hidden_one,
        cotangent,
        gain_second,
        [two_kept] + [to_seat(part, shift + 1) for shift, part in enumerate(two_sent)],
        False,
    )
    grad_branch = gather_rows(grad_branch_own)
    down_half = add_half(down_half, *grad_branch_own)
    down_sum = sum_half(down_half, 0)
    grad_branch = pieces_after(grad_branch, down_half)

    members = members[::-1]
    out_weights, qkv_weights = out_weights[::-1], qkv_weights[::-1]
    qkv, attended = qkv[::-1], attended[::-1]
    grad_mixed, found = branch_back(grad_branch, out_weights, [mixed for mixed, _ in attended])
    out_grads = {
        s: out_grad[spot * head_cols : (spot + 1) * head_cols]
        for group, out_grad in zip(members, found)
        for spot, s in enumerate(group)
    }
    out_pieces = send_to_owner(out_grads) + [out_grads[0]]

    def up_swap(last):
        sums["up"], waits = swap_half(up_pieces, *last)
        return waits

    def up_sum(last):
        value = add_half(sums["up"], *last)
        sums["up"] = sum_half(value, 1)
        return [value]

    def gate_swap(last):
        sums["gate"], waits = swap_half(gate_pieces, *last)
        sums["out"], more = swap_half(out_pieces, *last)
        sums["down"] = after(down_sum, *waits, *more)
        return waits + more + [sums["down"]]

    def gate_sum(last):
        values = add_half(sums["gate"], *last), add_half(sums["out"], *last)
        sums["gate"], sums["out"] = sum_half(values, 2)
        sums["up"] = swap_sum(sums["up"], *last)
        sums["down"] = swap_sum(sums["down"], *last)
        return [*values, sums["up"][0]]

    along = exchanges("dp", dp_size)
    exchange = exchanges("tensor", tensor_size) + along[1:] + along[:1]
    sums = {}
    moves = [up_swap, up_sum, gate_swap, gate_sum]
    last = list(grad_mixed)
    grad_qkv, qkv_grads = [], {}
    for index, group in enumerate(members):
        mixed, logs = attended[index]
        count = len(group) * head_cols
        grads = None
        for pair in range(count // LANES):
            waits = moves.pop(0)(last) if moves else last
            grads = attend_back(
                place,
                *qkv[index],
                mixed,
                after(grad_mixed[index], *waits),
                logs,
                cosines,
                sines,
                pair,
                grads,
            )
            last = [grads]
        grad_qkv.append(grads)
        qkv_grad = outer(full_one, grads)
        last = [qkv_grad]
        for spot, s in enumerate(group):
            if len(group) == 1:
                qkv_grads[s] = qkv_grad
            else:
                qkv_grads[s] = joined(
                    [
                        lax.slice_in_dim(
                            qkv_grad,
                            part * count + spot * head_cols,
                            part * count + (spot + 1) * head_cols,
                            axis=1,
                        )
                        for part in range(3)
                    ],
                    1,
                )
    for move in moves:
        last = move(last)

    qkv_half, marks = swap_half(send_to_owner(qkv_grads) + [qkv_grads[0]])
    grad_up = whole_sum(sums["up"], *marks)
    feed_terms[0] = (after(feed_terms[0][0], grad_up), *feed_terms[0][1:])
    one_terms = [
        (grad_qkv[index], part, weight, part, 1)
        for index, weight in enumerate(qkv_weights)
        for part in range(3)
    ]

    def later(terms, *others):
        return [(after(terms[0][0], *others), *terms[0][1:])] + terms[1:]

    shifts = range(1, span)
    feed_sent = [sum_products(feed_terms, shift * held, held, BF16) for shift in shifts]
    qkv_half = add_half(qkv_half, *feed_sent)
    gate_halves = swap_sum(sums["gate"], *feed_sent)
    out_halves = swap_sum(sums["out"], *feed_sent)
    qkv_sum = sum_half(after(qkv_half, gate_halves[0], out_halves[0]), 3)
    grad_down = whole_sum(sums["down"], *feed_sent)
    one_terms = later(one_terms, qkv_half, gate_halves[0], grad_down)
    one_sent = [sum_products(one_terms, shift * held, held, BF16) for shift in shifts]
    feed_parts = [sum_products(later(feed_terms, *one_sent), 0, held)]
    one_parts = [sum_products(later(one_terms, feed_parts[0]), 0, held)]
    feed_parts += [to_seat(part, shift) for shift, part in zip(shifts, feed_sent)]
    one_parts += [to_seat(part, shift) for shift, part in zip(shifts, one_sent)]
    output = (hidden_one + sum(feed_parts)).astype(BF16)
    (input_grad,), _, norm_one = norm_back(tokens, grad_hidden, gain_first, one_parts, True, 1)
    window = [input_grad, output]
    qkv_halves = swap_sum(qkv_sum, *window)
    norms = jnp.concatenate([after(norm_one, qkv_halves[0]), norm_two], axis=0)
    for step in exchange:
        norms = step(norms)
    grad_gate = whole_sum(gate_halves, qkv_halves[0])
    out_grad = whole_sum(out_halves, qkv_halves[0])
    qkv_grad = whole_sum(qkv_halves)
    return (
        output,
        input_grad,
        *(part_of(qkv_grad, part) for part in range(3)),
        out_grad,
        grad_gate,
        grad_up,
        grad_down,
        norms[0],
        norms[1],
        norms[2],
        norms[3],
    )


def solution(mesh):
    rows = P(("dp", "tensor"), None)
    columns = P(None, "tensor")
    depth = P("tensor", None)
    return jax.shard_map(
        functools.partial(shards, mesh.shape["dp"], mesh.shape["tensor"]),
        mesh=mesh,
        in_specs=(
            rows,
            P("dp"),
            P(),
            P(),
            columns,
            columns,
            columns,
            depth,
            P(),
            P(),
            columns,
            columns,
            depth,
            rows,
        ),
        out_specs=(
            rows,
            rows,
            columns,
            columns,
            columns,
            depth,
            columns,
            columns,
            depth,
            P(),
            P(),
            P(),
            P(),
        ),
        check_vma=False,
    )
```
